512 devices in a mesh: span: 32 (over z, core), chord: 16 (over y, x).
Axes of the slice: x: 4, y: 4, z: 16, core: 2. Of those that a mesh axis runs over, the one named last changes fastest.
Arguments:
- right_side: float32 [16, 1024, 2048], P(None, 'span', 'chord'), may hold values from -6 to 6
- stiff_scale: float32 [1024, 2048], P('span', 'chord'), may hold values from 0.5 to 2
- extra_diag: float32 [1024, 2048], P('span', 'chord'), may hold values from 0.5 to 4
- iface_line: int32 [128], P('chord'), may hold values from 0 to 127, as said below
- partner: int32 [128], P('chord'), may hold values from 0 to 127, as said below
Outputs:
- solution: float32 [16, 1024, 2048], P(None, 'span', 'chord')
- residual: float32 [16, 1024, 2048], P(None, 'span', 'chord')
The draws below stay inside these ranges and needn't reach their ends.
Inputs may be any that keep to these rules, and one draw needn't show every extreme that they name: `iface_line`: each device's 8 entries are distinct; the first two are 0 and 127, the patch's edge lines. partner pairs the slots: partner[partner[q]] = q and partner[q] != q.
All inputs are finite; a program needn't handle non-finite values.
Results may differ from the reference program's by a relative error of at most 0.00016.
Values sent between devices are 32-bit elements; how exact they have to be, the bound alone decides.
No kernel may reach another device: no remote copies, remote signals or barrier semaphores. Data moves between devices by JAX's collectives and lax.ppermute only.
A program may use at most 64 MiB of HBM per device.

```python
import math
import jax
import jax.numpy as jnp
from jax import lax

CC = 128
COLS = 16
IFACE = 8
ITERS = 2
NS = 1024
NC = 2048
SLOTS = 128


def draw_iface_line(key, part):
    device_keys = jax.random.split(jax.random.fold_in(key, 17), SLOTS // IFACE)

    def choose_lines(subkey):
        inner = jax.random.permutation(subkey, CC - 2)[:IFACE - 2].astype(jnp.int32) + 1
        edges = jnp.array([0, CC - 1], dtype=jnp.int32)
        return jnp.concatenate([edges, inner])
    return jax.vmap(choose_lines)(device_keys).reshape(SLOTS).astype(jnp.int32)


def draw_partner(key, part):
    shuffled = jax.random.permutation(jax.random.fold_in(key, 29), SLOTS).astype(jnp.int32)
    swapped = shuffled.reshape(-1, 2)[:, ::-1].reshape(-1)
    return jnp.zeros((SLOTS,), jnp.int32).at[shuffled].set(swapped)


def steps_of(own_key, extent, cuts, least, high):
    gain, own = 1.0, jax.random.fold_in(own_key, 6)
    for axis_at, blocks in cuts:
        draws = jnp.exp(jax.random.uniform(jax.random.fold_in(own, axis_at), (blocks,), jnp.float32, least / len(cuts), high / len(cuts)))
        gain = gain * jnp.repeat(draws, extent[axis_at] // blocks).reshape([-1 if axis == axis_at else 1 for axis in range(len(extent))])
    return gain


def bell_draw(key, extent, deviation, most, shards=(), kind=jnp.bfloat16):
    result = deviation * jax.random.normal(key, extent, jnp.float32)
    if shards:
        result = result * steps_of(key, extent, shards, -0.22, 0.18)
    return jnp.clip(result, -most, most).astype(kind)


def setup_inputs(seed: int = 0) -> dict:
    arg_keys = jax.random.split(jax.random.key(seed), 6)
    return {
        "right_side": bell_draw(arg_keys[0], (COLS, NS, NC), 1.0, 6.0, ((1, 32), (2, 16)), jnp.float32),
        "stiff_scale": jnp.clip(jnp.exp(math.log(2.0) - 1.3862944 * jax.random.uniform(arg_keys[1], (NS, NC), jnp.float32) ** steps_of(arg_keys[1], (NS, NC), ((0, 32), (1, 16)), -0.2, 0.2)), 0.5, 2.0),
        "extra_diag": jnp.clip(jnp.exp(math.log(4.0) - 2.0794415 * jax.random.uniform(arg_keys[2], (NS, NC), jnp.float32) ** steps_of(arg_keys[2], (NS, NC), ((0, 32), (1, 16)), -0.2, 0.2)), 0.5, 4.0),
        "iface_line": draw_iface_line(jax.random.fold_in(arg_keys[5], 71), 0),
        "partner": draw_partner(jax.random.fold_in(arg_keys[5], 71), 0),
    }


mass_taps = (1.0 / 5040.0, 120.0 / 5040.0, 1191.0 / 5040.0, 2416.0 / 5040.0, 1191.0 / 5040.0, 120.0 / 5040.0, 1.0 / 5040.0)
bend_taps = (1.0 / 6.0, 0.0, -1.5, 8.0 / 3.0, -1.5, 0.0, 1.0 / 6.0)
penalty_weight = 4.0

def tap_sum(extended, tap_list, along_dim, length):
    summed = tap_list[0] * lax.slice_in_dim(extended, 0, length, axis=along_dim)
    for offset in range(1, 7):
        if tap_list[offset] != 0.0:
            summed = summed + tap_list[offset] * lax.slice_in_dim(extended, offset, offset + length, axis=along_dim)
    return summed

def gram_of(left_field, right_field):
    return jnp.dot(left_field.reshape(left_field.shape[0], -1), right_field.reshape(right_field.shape[0], -1).T, precision=lax.Precision.HIGHEST)

def combine(vector, coeffs):
    return jnp.einsum('aij,ab->bij', vector, coeffs, precision=lax.Precision.HIGHEST)

def spd_solve(matrix, right_hand):
    factor = jnp.linalg.cholesky(matrix)
    forward = lax.linalg.triangular_solve(factor, right_hand, left_side=True, lower=True)
    return lax.linalg.triangular_solve(factor, forward, left_side=True, lower=True, transpose_a=True)

def stiffness(vector, stiff_scale, extra_diag, iface_line, partner):

    def one_column(column):
        weighted = stiff_scale * column
        wrapped = jnp.concatenate([weighted[:, -3:], weighted, weighted[:, :3]], axis=1)
        chord_mass = tap_sum(wrapped, mass_taps, 1, NC)
        chord_bend = tap_sum(wrapped, bend_taps, 1, NC)
        zero_rim = jnp.zeros((3, NC), column.dtype)
        mass_ext = jnp.concatenate([zero_rim, chord_mass, zero_rim], axis=0)
        bend_ext = jnp.concatenate([zero_rim, chord_bend, zero_rim], axis=0)
        spanwise = tap_sum(mass_ext, bend_taps, 0, NS) + tap_sum(bend_ext, mass_taps, 0, NS)
        return stiff_scale * spanwise + extra_diag * column
    stiff_part = lax.map(one_column, vector)
    slot_ids = jnp.arange(SLOTS, dtype=jnp.int32)
    global_line = slot_ids // IFACE * CC + iface_line.astype(jnp.int32)
    own_values = vector[:, :, global_line]
    partner_values = own_values[:, :, partner.astype(jnp.int32)]
    return stiff_part.at[:, :, global_line].add(penalty_weight * (own_values - partner_values))

def reference(right_side, stiff_scale, extra_diag, iface_line, partner):
    solution = jnp.zeros_like(right_side)
    residual = right_side
    direction = right_side
    norm_now = gram_of(residual, residual)
    for iteration in range(ITERS):
        image_now = stiffness(direction, stiff_scale, extra_diag, iface_line, partner)
        curvature = gram_of(direction, image_now)
        alpha = spd_solve(curvature, norm_now)
        solution = solution + combine(direction, alpha)
        residual = residual - combine(image_now, alpha)
        if iteration + 1 < ITERS:
            norm_next = gram_of(residual, residual)
            beta = spd_solve(norm_now, norm_next)
            direction = residual + combine(direction, beta)
            norm_now = norm_next
    return (solution, residual)
```

```python
import jax
import jax.numpy as jnp
from jax import lax
from jax.sharding import Mesh
from jax.sharding import PartitionSpec as P

SPAN = ("z", "core")


mass_taps = (
    1.0 / 5040.0,
    120.0 / 5040.0,
    1191.0 / 5040.0,
    2416.0 / 5040.0,
    1191.0 / 5040.0,
    120.0 / 5040.0,
    1.0 / 5040.0,
)
bend_taps = (1.0 / 6.0, 0.0, -1.5, 8.0 / 3.0, -1.5, 0.0, 1.0 / 6.0)
penalty_weight = 4.0


def with_halo(cells, sides, width, closed):
    for axis, dim in sides:
        count = lax.axis_size(axis)
        ends = count if closed else count - 1
        head = lax.slice_in_dim(cells, 0, width, axis=dim)
        tail = lax.slice_in_dim(cells, cells.shape[dim] - width, cells.shape[dim], axis=dim)
        cells = jnp.concatenate(
            [
                lax.ppermute(tail, axis, [(i, (i + 1) % count) for i in range(ends)]),
                cells,
                lax.ppermute(head, axis, [((i + 1) % count, i) for i in range(ends)]),
            ],
            axis=dim,
        )
    return cells


def tap_sum(extended, tap_list, along_dim, length):
    summed = tap_list[0] * lax.slice_in_dim(extended, 0, length, axis=along_dim)
    for offset in range(1, 7):
        if tap_list[offset] != 0.0:
            summed = summed + tap_list[offset] * lax.slice_in_dim(
                extended, offset, offset + length, axis=along_dim
            )
    return summed


def gram_of(left_field, right_field):
    return jnp.dot(
        left_field.reshape(left_field.shape[0], -1),
        right_field.reshape(right_field.shape[0], -1).T,
        precision=lax.Precision.HIGHEST,
    )


def combine(vector, coeffs):
    return jnp.einsum("aij,ab->bij", vector, coeffs, precision=lax.Precision.HIGHEST)


def spd_solve(matrix, right_hand):
    factor = jnp.linalg.cholesky(matrix)
    forward = lax.linalg.triangular_solve(factor, right_hand, left_side=True, lower=True)
    return lax.linalg.triangular_solve(
        factor, forward, left_side=True, lower=True, transpose_a=True
    )


def apply_stiffness(vector, stiff_scale, extra_diag, line_pick, partner):
    row_count = vector.shape[1]
    line_count = vector.shape[2]
    flattened = vector.reshape(-1, line_count)
    own_values = jnp.einsum("lc,kc->lk", line_pick, flattened, precision=lax.Precision.HIGHEST)
    all_lines = lax.all_gather(own_values, "chord", axis=0, tiled=True)
    weighted = stiff_scale[None] * vector
    wrapped = with_halo(weighted, (("chord", 2),), 3, True)
    stacked = jnp.stack(
        [tap_sum(wrapped, mass_taps, 2, line_count), tap_sum(wrapped, bend_taps, 2, line_count)]
    )
    stacked_ext = with_halo(stacked, ((SPAN, 2),), 3, False)
    mass_ext = stacked_ext[0]
    bend_ext = stacked_ext[1]
    spanwise = tap_sum(mass_ext, bend_taps, 1, row_count) + tap_sum(
        bend_ext, mass_taps, 1, row_count
    )
    stiff_part = stiff_scale[None] * spanwise + extra_diag[None] * vector
    partner_values = jnp.take(all_lines, partner, axis=0)
    coupling = penalty_weight * (own_values - partner_values)
    spread = jnp.einsum("lk,lc->kc", coupling, line_pick, precision=lax.Precision.HIGHEST)
    return stiff_part + spread.reshape(vector.shape)


def gathered_sum(partial, axes, count):
    sent = jnp.broadcast_to(partial[None], (count,) + partial.shape)
    return jnp.sum(lax.all_to_all(sent, axes, 0, 0), axis=0)


def body(right_side, stiff_scale, extra_diag, iface_line, partner):
    line_count = right_side.shape[2]
    line_pick = (iface_line[:, None] == jnp.arange(line_count, dtype=jnp.int32)[None, :]).astype(
        jnp.float32
    )
    first = apply_stiffness(right_side, stiff_scale, extra_diag, line_pick, partner)
    second = apply_stiffness(first, stiff_scale, extra_diag, line_pick, partner)
    columns = right_side.shape[0]
    gram = jnp.concatenate(
        [
            gram_of(right_side, jnp.concatenate([right_side, first])),
            gram_of(first, jnp.concatenate([first, second])),
        ],
        axis=1,
    ).reshape(8, 128)
    gram = gathered_sum(gram, ("core", "chord"), lax.axis_size(("core", "chord")))
    gram = gathered_sum(gram, "z", lax.axis_size("z")).reshape(columns, 4 * columns)
    g00, g01, g11, g12 = jnp.split(gram, 4, axis=1)
    matrix = jnp.concatenate(
        [jnp.concatenate([g01, g11], axis=1), jnp.concatenate([g11, g12], axis=1)], axis=0
    )
    coeffs = spd_solve(matrix, jnp.concatenate([g00, g01], axis=0))
    zero, one = coeffs[:columns], coeffs[columns:]
    solution = combine(right_side, zero) + combine(first, one)
    residual = right_side - combine(first, zero) - combine(second, one)
    return (solution, residual)


def solution(mesh):
    fine = Mesh(mesh.devices.reshape(-1, 2, mesh.devices.shape[1]), ("z", "core", "chord"))
    return jax.shard_map(
        body,
        mesh=fine,
        in_specs=(
            P(None, SPAN, "chord"),
            P(SPAN, "chord"),
            P(SPAN, "chord"),
            P("chord"),
            P("chord"),
        ),
        out_specs=(P(None, SPAN, "chord"), P(None, SPAN, "chord")),
        check_vma=False,
    )
```

```python
import jax
import jax.numpy as jnp
from jax import lax
from jax.experimental import pallas as pl
from jax.experimental.pallas import tpu as pltpu
from jax.sharding import Mesh
from jax.sharding import PartitionSpec as P

SPAN = ("z", "core")
COLS = 16
ROWS = 32
LINES = 128
SLOTS = 8
CHORD = 16
DEEP = 6
NEAR = 3
WIDE = ROWS + 2 * NEAR
FLAT = WIDE * COLS
SENT = 640
SPARE = 32

mass_taps = (2416.0 / 5040.0, 1191.0 / 5040.0, 120.0 / 5040.0, 1.0 / 5040.0)
bend_taps = (8.0 / 3.0, -1.5, 0.0, 1.0 / 6.0)
penalty_weight = 4.0

f32 = jnp.float32
INTERPRET = False


def dot(left, right, contract):
    return lax.dot_general(
        left,
        right,
        (contract, ((), ())),
        precision=lax.Precision.HIGHEST,
        preferred_element_type=f32,
    )


def dot_nn(left, right):
    return dot(left, right, ((1,), (0,)))


def dot_nt(left, right):
    return dot(left, right, ((1,), (1,)))


def dot_tn(left, right):
    return dot(left, right, ((0,), (0,)))


def iota(shape, dim):
    return lax.broadcasted_iota(jnp.int32, shape, dim)


def taps_at(distance, taps):
    value = jnp.zeros(distance.shape, f32)
    for step in range(4):
        if taps[step] != 0.0:
            value = jnp.where(distance == step, taps[step], value)
    return value


def outer_line(row):
    return jnp.where(row < 3, row - 3, jnp.where(row < 6, row + LINES - 3, 4 * LINES))


def edge_line(row):
    return jnp.where(row < 3, row + LINES - 3, jnp.where(row < 6, row - 3, 4 * LINES))


def pair_of(field, step):
    lane = iota((COLS, LINES), 1)
    ahead = jnp.where(lane < LINES - step, pltpu.roll(field, LINES - step, 1), 0.0)
    behind = jnp.where(lane >= step, pltpu.roll(field, step, 1), 0.0)
    return ahead + behind


def row_stencil(rows, at, taps):
    total = taps[0] * rows[at]
    for step in range(1, 4):
        if taps[step] != 0.0:
            total = total + taps[step] * (rows[at - step] + rows[at + step])
    return total


def spread(row):
    return jnp.broadcast_to(row, (COLS, LINES))


def pack_kernel(r_ref, s_ref, d_ref, field_ref, up_ref, down_ref):
    for row in range(ROWS):
        cells = r_ref[pl.ds(row, COLS, stride=ROWS), :]
        field_ref[pl.ds(row * COLS, COLS), :] = cells
        if row < DEEP:
            down_ref[pl.ds(row * COLS, COLS), :] = cells
        if row >= ROWS - DEEP:
            up_ref[pl.ds((row - ROWS + DEEP) * COLS, COLS), :] = cells
    pad = jnp.zeros((2, LINES), f32)
    start = DEEP * COLS
    low, high = slice(0, DEEP), slice(ROWS - DEEP, ROWS)
    down_ref[start : start + 16, :] = jnp.concatenate(
        [s_ref[low, :], pad, d_ref[low, :], pad], axis=0
    )
    up_ref[start : start + 16, :] = jnp.concatenate(
        [s_ref[high, :], pad, d_ref[high, :], pad], axis=0
    )


def rows_of(below, own, above, first, reach):
    rows = [below[first + DEEP - reach + k : first + DEEP - reach + k + 1, :] for k in range(reach)]
    rows += [own[k : k + 1, :] for k in range(ROWS)]
    rows += [above[first + k : first + k + 1, :] for k in range(reach)]
    return rows


def send_kernel(
    field_ref, s_ref, d_ref, below_ref, above_ref, line_ref, partner_ref, base_ref, message_ref
):
    start = DEEP * COLS
    scale = rows_of(below_ref, s_ref, above_ref, start, DEEP)
    extra = rows_of(below_ref, d_ref, above_ref, start + 8, NEAR)
    cells = [below_ref[pl.ds(k * COLS, COLS), :] for k in range(DEEP)]
    cells += [field_ref[pl.ds(k * COLS, COLS), :] for k in range(ROWS)]
    cells += [above_ref[pl.ds(k * COLS, COLS), :] for k in range(DEEP)]
    weighted = [spread(scale[k]) * cells[k] for k in range(ROWS + 2 * DEEP)]
    masses, bends, bases = [], [], []
    for row in range(WIDE):
        mass = row_stencil(weighted, row + NEAR, mass_taps)
        bend = row_stencil(weighted, row + NEAR, bend_taps)
        total = mass_taps[0] * bend + bend_taps[0] * mass
        for step in range(1, 4):
            mixed = mass_taps[step] * bend
            if bend_taps[step] != 0.0:
                mixed = mixed + bend_taps[step] * mass
            total = total + pair_of(mixed, step)
        base = spread(scale[row + NEAR]) * total + spread(extra[row]) * cells[row + NEAR]
        masses.append(mass)
        bends.append(bend)
        bases.append(base)
        base_ref[pl.ds(row * COLS, COLS), :] = base
    own_scale = s_ref[...]
    blank = jnp.zeros((SENT - FLAT, LINES), f32)
    lane = iota((SLOTS, LINES), 1)
    row8 = iota((SLOTS, LINES), 0)
    at_slot = (lane == line_ref[...]).astype(f32)
    at_edge = (lane == edge_line(row8)).astype(f32)
    values = jnp.concatenate(cells[NEAR : NEAR + WIDE] + [blank], axis=0)
    sent_cells = dot_nt(at_slot, values)
    wide_lane = iota((SLOTS, SENT), 1)
    sent_cells = jnp.where(wide_lane == FLAT, partner_ref[...].astype(f32), sent_cells)
    sent_cells = jnp.where(wide_lane == FLAT + 1, line_ref[...].astype(f32), sent_cells)
    sent_base = dot_nt(
        jnp.concatenate([at_slot, at_edge], axis=0),
        jnp.concatenate(bases + [own_scale], axis=0),
    )
    distance = jnp.abs(outer_line(row8) - lane)
    rim = [scale[NEAR + k] for k in (0, 1, 2, WIDE - 3, WIDE - 2, WIDE - 1)]
    rim_stack = jnp.concatenate(rim + [jnp.zeros((SENT - FLAT - 6, LINES), f32)], axis=0)
    reach = jnp.concatenate(
        [taps_at(distance, mass_taps), taps_at(distance, bend_taps)], axis=1
    )
    sent_reach = dot_nt(
        jnp.concatenate([reach, at_edge], axis=1),
        jnp.concatenate(
            [
                jnp.concatenate(bends + [blank], axis=0),
                jnp.concatenate(masses + [blank], axis=0),
                jnp.concatenate([jnp.zeros((FLAT, LINES), f32), rim_stack], axis=0),
            ],
            axis=1,
        ),
    )
    message = jnp.concatenate([sent_cells, sent_base[:SLOTS], sent_reach, sent_base[SLOTS:]], axis=0)
    for device in range(CHORD):
        message_ref[device] = message


def apply_kernel(
    here_ref, got_ref, field_ref, base_ref, s_ref, d_ref, below_ref, above_ref, line_ref,
    w_ref, z_ref, gram_ref
):
    here = here_ref[0]
    mine = got_ref[here]
    left = got_ref[lax.rem(here + CHORD - 1, CHORD)]
    right = got_ref[lax.rem(here + 1, CHORD)]
    all_cells = got_ref[:, 0:8, :].reshape(CHORD * SLOTS, SENT)
    all_base = got_ref[:, 8:16, :].reshape(CHORD * SLOTS, SENT)
    all_reach = got_ref[:, 16:24, :].reshape(CHORD * SLOTS, SENT)

    slots = jnp.concatenate([mine[0:8], left[0:8], right[0:8]], axis=0)
    partner = slots[:, FLAT : FLAT + 1].astype(jnp.int32)
    line = slots[:, FLAT + 1 : FLAT + 2].astype(jnp.int32)
    pick = (iota((3 * SLOTS, LINES), 1) == partner).astype(f32)
    other = dot_nn(pick, all_cells)
    apart = penalty_weight * (slots - other)
    other_line = other[:SLOTS, FLAT + 1 : FLAT + 2].astype(jnp.int32)
    other_device = partner[:SLOTS] // SLOTS
    other_base = dot_nn(pick[:SLOTS], all_base)

    device = jnp.concatenate([jnp.full((SLOTS, 1), here, jnp.int32), other_device], axis=0)
    at = jnp.concatenate([line[:SLOTS], other_line], axis=0)
    before = lax.rem(device + CHORD - 1, CHORD) * SLOTS + NEAR + at
    after = lax.rem(device + 1, CHORD) * SLOTS + at - (LINES - NEAR)
    source = jnp.where(at < NEAR, before, jnp.where(at >= LINES - NEAR, after, -1))
    added = dot_nn((iota((2 * SLOTS, LINES), 1) == source).astype(f32), all_reach)

    spot = iota((LINES, SENT), 0) - (LINES - ROWS)
    row_at = iota((LINES, SENT), 1) // COLS - NEAR
    inner = ((spot == row_at) & (spot >= 0)).astype(f32)
    rim_row = jnp.where(spot < NEAR, spot - NEAR, spot + ROWS - NEAR)
    rim = ((rim_row == row_at) & (spot >= 0) & (spot < 2 * NEAR)).astype(f32)
    row8 = iota((SLOTS, SENT), 0)
    halo_base = jnp.where(row8 < 3, left[24:32], right[24:32])
    halo_rim = jnp.where(row8 < 3, left[16:24], right[16:24])
    scales = dot_nn(
        jnp.concatenate([mine[8:16], other_base, halo_base], axis=0)[:, SENT - LINES :], inner
    )
    slot_scale = scales[: 2 * SLOTS]
    halo_scale = scales[2 * SLOTS :] + dot_nn(halo_rim[:, SENT - LINES :], rim)

    own_w = mine[8:16] + slot_scale[:SLOTS] * added[:SLOTS] + apart[:SLOTS]
    other_w = other_base + slot_scale[SLOTS:] * added[SLOTS:] - apart[:SLOTS]
    apart_w = penalty_weight * (own_w - other_w)

    target = iota((2 * SLOTS, SLOTS), 1)
    from_left = iota((2 * SLOTS, SLOTS), 0) < SLOTS
    chosen = (edge_line(target) == line[SLOTS:]) & ((target < 3) == from_left)
    halo_apart = dot_tn(chosen.astype(f32), apart[SLOTS:])
    halo_w = halo_base + halo_scale * mine[16:24] + halo_apart
    halo_v = jnp.where(row8 < 6, halo_scale * halo_w, 0.0)

    lane = iota((SLOTS, LINES), 1)
    low8 = iota((SLOTS, LINES), 0)
    at_slot = (lane == line[:SLOTS]).astype(f32)
    at_edge = (lane == edge_line(low8)).astype(f32)
    none = jnp.zeros((SLOTS, LINES), f32)
    arrived = jnp.where(row8 < 3, right[16:24], left[16:24])
    first = dot_tn(
        jnp.concatenate([apart[:SLOTS], arrived], axis=0),
        jnp.concatenate(
            [
                jnp.concatenate([at_slot, none], axis=1),
                jnp.concatenate([none, at_edge], axis=1),
            ],
            axis=0,
        ),
    )
    distance = jnp.abs(outer_line(low8) - lane)
    second = dot_tn(
        jnp.concatenate([halo_v, apart_w], axis=0),
        jnp.concatenate(
            [
                jnp.concatenate(
                    [taps_at(distance, mass_taps), taps_at(distance, bend_taps), none], axis=1
                ),
                jnp.concatenate([none, none, at_slot], axis=1),
            ],
            axis=0,
        ),
    )
    scale = rows_of(below_ref, s_ref, above_ref, DEEP * COLS, NEAR)
    images, masses, bends = [], [], []
    for row in range(WIDE):
        cut = slice(row * COLS, (row + 1) * COLS)
        scale_row = spread(scale[row])
        image = base_ref[cut, :] + first[cut, :LINES] + scale_row * first[cut, LINES:]
        value = scale_row * image
        mass, bend = mass_taps[0] * value, bend_taps[0] * value
        for step in range(1, 4):
            pair = pair_of(value, step)
            mass = mass + mass_taps[step] * pair
            if bend_taps[step] != 0.0:
                bend = bend + bend_taps[step] * pair
        images.append(image)
        masses.append(mass + second[cut, :LINES])
        bends.append(bend + second[cut, LINES : 2 * LINES])
    seconds = []
    for row in range(ROWS):
        at_row = row + NEAR
        cut = slice(at_row * COLS, (at_row + 1) * COLS)
        total = row_stencil(masses, at_row, bend_taps) + row_stencil(bends, at_row, mass_taps)
        product = (
            spread(scale[at_row]) * total
            + spread(d_ref[row : row + 1, :]) * images[at_row]
            + second[cut, 2 * LINES :]
        )
        w_ref[pl.ds(row * COLS, COLS), :] = images[at_row]
        z_ref[pl.ds(row * COLS, COLS), :] = product
        seconds.append(product)
    r = jnp.concatenate([field_ref[pl.ds(k * COLS, COLS), :] for k in range(ROWS)], axis=1)
    w = jnp.concatenate(images[NEAR : NEAR + ROWS], axis=1)
    z = jnp.concatenate(seconds, axis=1)
    gram = jnp.concatenate(
        [
            dot_nt(r, jnp.concatenate([r, w], axis=0)),
            dot_nt(w, jnp.concatenate([w, z], axis=0)),
        ],
        axis=1,
    )
    gram = jnp.concatenate([gram[:8], gram[8:]], axis=1)
    for device in range(gram_ref.shape[0]):
        gram_ref[device] = gram


def total_kernel(parts_ref, out_ref):
    total = jnp.sum(parts_ref[...], axis=0)
    for device in range(out_ref.shape[0]):
        out_ref[device] = total


def finish_kernel(parts_ref, field_ref, w_ref, z_ref, x_ref, res_ref):
    packed = jnp.sum(parts_ref[...], axis=0)
    gram = jnp.concatenate([packed[:, : 4 * COLS], packed[:, 4 * COLS :]], axis=0)
    g00, g01 = gram[:, :COLS], gram[:, COLS : 2 * COLS]
    g11, g12 = gram[:, 2 * COLS : 3 * COLS], gram[:, 3 * COLS :]
    work = jnp.concatenate(
        [
            jnp.concatenate([g01, g11], axis=1),
            jnp.concatenate([g11, g12], axis=1),
            jnp.concatenate([g00, g01], axis=1),
        ],
        axis=0,
    )
    lane = iota((1, 2 * COLS), 1)
    for step in range(2 * COLS):
        row = work[step : step + 1, :]
        column = work[:, step : step + 1] / row[:, step : step + 1]
        work = jnp.where(lane == step, column, work - column * row)
    coeffs = work[2 * COLS :, :]
    r = jnp.concatenate([field_ref[pl.ds(k * COLS, COLS), :] for k in range(ROWS)], axis=1)
    w = jnp.concatenate([w_ref[pl.ds(k * COLS, COLS), :] for k in range(ROWS)], axis=1)
    z = jnp.concatenate([z_ref[pl.ds(k * COLS, COLS), :] for k in range(ROWS)], axis=1)
    x = dot_nn(coeffs, jnp.concatenate([r, w], axis=0))
    res = r - dot_nn(coeffs, jnp.concatenate([w, z], axis=0))
    for row in range(ROWS):
        cut = slice(row * LINES, (row + 1) * LINES)
        x_ref[pl.ds(row, COLS, stride=ROWS), :] = x[:, cut]
        res_ref[pl.ds(row, COLS, stride=ROWS), :] = res[:, cut]


def call(kernel, shapes, smem=0):
    def run(*args):
        specs = [pl.BlockSpec(memory_space=pltpu.SMEM)] * smem
        specs += [pl.BlockSpec(memory_space=pltpu.VMEM)] * (len(args) - smem)
        return pl.pallas_call(
            kernel,
            out_shape=[jax.ShapeDtypeStruct(shape, f32) for shape in shapes],
            in_specs=specs,
            out_specs=[pl.BlockSpec(memory_space=pltpu.VMEM)] * len(shapes),
            interpret=INTERPRET,
        )(*args)

    return run


def body(right_side, stiff_scale, extra_diag, iface_line, partner):
    span = lax.axis_size(SPAN)
    plane = lax.axis_size(("core", "chord"))
    depth = lax.axis_size("z")
    cells = right_side.reshape(COLS * ROWS, LINES)
    halo = (DEEP * COLS + 16, LINES)
    flat = (ROWS * COLS, LINES)
    field, up, down = call(pack_kernel, [flat, halo, halo])(cells, stiff_scale, extra_diag)
    below = lax.ppermute(up, SPAN, [(i, i + 1) for i in range(span - 1)])
    above = lax.ppermute(down, SPAN, [(i + 1, i) for i in range(span - 1)])
    line = iface_line.reshape(SLOTS, 1)
    base, message = call(send_kernel, [(FLAT, LINES), (CHORD, SPARE, SENT)])(
        field, stiff_scale, extra_diag, below, above, line, partner.reshape(SLOTS, 1)
    )
    got = lax.all_to_all(message, "chord", 0, 0)
    here = lax.axis_index("chord").reshape(1)
    w, z, gram = call(apply_kernel, [flat, flat, (plane, 8, LINES)], smem=1)(
        here, got, field, base, stiff_scale, extra_diag, below, above, line
    )
    gram = lax.all_to_all(gram, ("core", "chord"), 0, 0)
    (gram,) = call(total_kernel, [(depth, 8, LINES)])(gram)
    gram = lax.all_to_all(gram, "z", 0, 0)
    x, res = call(finish_kernel, [flat, flat])(gram, field, w, z)
    return (x.reshape(COLS, ROWS, LINES), res.reshape(COLS, ROWS, LINES))


def solution(mesh):
    chord = mesh.devices.shape[1]
    fine = Mesh(mesh.devices.reshape(-1, 2, chord), ("z", "core", "chord"))
    return jax.shard_map(
        body,
        mesh=fine,
        in_specs=(
            P(None, SPAN, "chord"),
            P(SPAN, "chord"),
            P(SPAN, "chord"),
            P("chord"),
            P("chord"),
        ),
        out_specs=(P(None, SPAN, "chord"), P(None, SPAN, "chord")),
        check_vma=False,
    )
```

```python
import jax
import jax.numpy as jnp
from jax import lax
from jax.experimental import pallas as pl
from jax.experimental.pallas import tpu as pltpu
from jax.sharding import Mesh
from jax.sharding import PartitionSpec as P

SPAN = ("z", "core")
COLS = 16
ROWS = 32
LINES = 128
SLOTS = 8
CHORD = 16
DEEP = 6
NEAR = 3
WIDE = ROWS + 2 * NEAR
FLAT = WIDE * COLS
SENT = 640
SPARE = 32

mass_taps = (2416.0 / 5040.0, 1191.0 / 5040.0, 120.0 / 5040.0, 1.0 / 5040.0)
bend_taps = (8.0 / 3.0, -1.5, 0.0, 1.0 / 6.0)
penalty_weight = 4.0

f32 = jnp.float32
KERNEL_BYTES = 24 << 20
INTERPRET = False


def dot(left, right, contract):
    return lax.dot_general(
        left,
        right,
        (contract, ((), ())),
        precision=lax.Precision.HIGHEST,
        preferred_element_type=f32,
    )


def dot_nn(left, right):
    return dot(left, right, ((1,), (0,)))


def dot_nt(left, right):
    return dot(left, right, ((1,), (1,)))


def dot_tn(left, right):
    return dot(left, right, ((0,), (0,)))


def iota(shape, dim):
    return lax.broadcasted_iota(jnp.int32, shape, dim)


def taps_at(distance, taps):
    value = jnp.zeros(distance.shape, f32)
    for step in range(4):
        if taps[step] != 0.0:
            value = jnp.where(distance == step, taps[step], value)
    return value


def outer_line(row):
    return jnp.where(row < 3, row - 3, jnp.where(row < 6, row + LINES - 3, 4 * LINES))


def edge_line(row):
    return jnp.where(row < 3, row + LINES - 3, jnp.where(row < 6, row - 3, 4 * LINES))


def pair_of(field, step):
    lane = iota((COLS, LINES), 1)
    ahead = jnp.where(lane < LINES - step, pltpu.roll(field, LINES - step, 1), 0.0)
    behind = jnp.where(lane >= step, pltpu.roll(field, step, 1), 0.0)
    return ahead + behind


def row_stencil(rows, at, taps):
    total = taps[0] * rows[at]
    for step in range(1, 4):
        if taps[step] != 0.0:
            total = total + taps[step] * (rows[at - step] + rows[at + step])
    return total


def spread(row):
    return jnp.broadcast_to(row, (COLS, LINES))


def pack_kernel(r_ref, s_ref, d_ref, field_ref, up_ref, down_ref):
    for row in range(ROWS):
        cells = r_ref[pl.ds(row, COLS, stride=ROWS), :]
        field_ref[pl.ds(row * COLS, COLS), :] = cells
        if row < DEEP:
            down_ref[pl.ds(row * COLS, COLS), :] = cells
        if row >= ROWS - DEEP:
            up_ref[pl.ds((row - ROWS + DEEP) * COLS, COLS), :] = cells
    pad = jnp.zeros((2, LINES), f32)
    start = DEEP * COLS
    low, high = slice(0, DEEP), slice(ROWS - DEEP, ROWS)
    down_ref[start : start + 16, :] = jnp.concatenate(
        [s_ref[low, :], pad, d_ref[low, :], pad], axis=0
    )
    up_ref[start : start + 16, :] = jnp.concatenate(
        [s_ref[high, :], pad, d_ref[high, :], pad], axis=0
    )


def rows_of(below, own, above, first, reach):
    rows = [below[first + DEEP - reach + k : first + DEEP - reach + k + 1, :] for k in range(reach)]
    rows += [own[k : k + 1, :] for k in range(ROWS)]
    rows += [above[first + k : first + k + 1, :] for k in range(reach)]
    return rows


def column_of(scalars_ref, width):
    row = iota((SLOTS, width), 0)
    value = jnp.zeros((SLOTS, width), jnp.int32)
    for slot in range(SLOTS):
        value = jnp.where(row == slot, scalars_ref[slot], value)
    return value


def send_kernel(
    line_ref, partner_ref, field_ref, s_ref, d_ref, below_ref, above_ref, base_ref, message_ref
):
    start = DEEP * COLS
    scale = rows_of(below_ref, s_ref, above_ref, start, DEEP)
    extra = rows_of(below_ref, d_ref, above_ref, start + 8, NEAR)
    cells = [below_ref[pl.ds(k * COLS, COLS), :] for k in range(DEEP)]
    cells += [field_ref[pl.ds(k * COLS, COLS), :] for k in range(ROWS)]
    cells += [above_ref[pl.ds(k * COLS, COLS), :] for k in range(DEEP)]
    weighted = [spread(scale[k]) * cells[k] for k in range(ROWS + 2 * DEEP)]
    masses, bends, bases = [], [], []
    for row in range(WIDE):
        mass = row_stencil(weighted, row + NEAR, mass_taps)
        bend = row_stencil(weighted, row + NEAR, bend_taps)
        total = mass_taps[0] * bend + bend_taps[0] * mass
        for step in range(1, 4):
            mixed = mass_taps[step] * bend
            if bend_taps[step] != 0.0:
                mixed = mixed + bend_taps[step] * mass
            total = total + pair_of(mixed, step)
        base = spread(scale[row + NEAR]) * total + spread(extra[row]) * cells[row + NEAR]
        masses.append(mass)
        bends.append(bend)
        bases.append(base)
        base_ref[pl.ds(row * COLS, COLS), :] = base
    own_scale = s_ref[...]
    blank = jnp.zeros((SENT - FLAT, LINES), f32)
    lane = iota((SLOTS, LINES), 1)
    row8 = iota((SLOTS, LINES), 0)
    at_slot = (lane == column_of(line_ref, LINES)).astype(f32)
    at_edge = (lane == edge_line(row8)).astype(f32)
    values = jnp.concatenate(cells[NEAR : NEAR + WIDE] + [blank], axis=0)
    sent_cells = dot_nt(at_slot, values)
    wide_lane = iota((SLOTS, SENT), 1)
    sent_cells = jnp.where(wide_lane == FLAT, column_of(partner_ref, SENT).astype(f32), sent_cells)
    sent_cells = jnp.where(wide_lane == FLAT + 1, column_of(line_ref, SENT).astype(f32), sent_cells)
    sent_base = dot_nt(
        jnp.concatenate([at_slot, at_edge], axis=0),
        jnp.concatenate(bases + [own_scale], axis=0),
    )
    distance = jnp.abs(outer_line(row8) - lane)
    rim = [scale[NEAR + k] for k in (0, 1, 2, WIDE - 3, WIDE - 2, WIDE - 1)]
    rim_stack = jnp.concatenate(rim + [jnp.zeros((SENT - FLAT - 6, LINES), f32)], axis=0)
    reach = jnp.concatenate(
        [taps_at(distance, mass_taps), taps_at(distance, bend_taps)], axis=1
    )
    sent_reach = dot_nt(
        jnp.concatenate([reach, at_edge], axis=1),
        jnp.concatenate(
            [
                jnp.concatenate(bends + [blank], axis=0),
                jnp.concatenate(masses + [blank], axis=0),
                jnp.concatenate([jnp.zeros((FLAT, LINES), f32), rim_stack], axis=0),
            ],
            axis=1,
        ),
    )
    message = jnp.concatenate([sent_cells, sent_base[:SLOTS], sent_reach, sent_base[SLOTS:]], axis=0)
    for device in range(CHORD):
        message_ref[device] = message


def apply_kernel(
    here_ref, got_ref, field_ref, base_ref, s_ref, d_ref, below_ref, above_ref, w_ref, z_ref, gram_ref
):
    here = here_ref[0]
    mine = got_ref[here]
    left = got_ref[lax.rem(here + CHORD - 1, CHORD)]
    right = got_ref[lax.rem(here + 1, CHORD)]
    all_cells = got_ref[:, 0:8, :].reshape(CHORD * SLOTS, SENT)
    all_base = got_ref[:, 8:16, :].reshape(CHORD * SLOTS, SENT)
    all_reach = got_ref[:, 16:24, :].reshape(CHORD * SLOTS, SENT)

    slots = jnp.concatenate([mine[0:8], left[0:8], right[0:8]], axis=0)
    partner = slots[:, FLAT : FLAT + 1].astype(jnp.int32)
    line = slots[:, FLAT + 1 : FLAT + 2].astype(jnp.int32)
    pick = (iota((3 * SLOTS, LINES), 1) == partner).astype(f32)
    other = dot_nn(pick, all_cells)
    apart = penalty_weight * (slots - other)
    other_line = other[:SLOTS, FLAT + 1 : FLAT + 2].astype(jnp.int32)
    other_device = partner[:SLOTS] // SLOTS
    other_base = dot_nn(pick[:SLOTS], all_base)

    device = jnp.concatenate([jnp.full((SLOTS, 1), here, jnp.int32), other_device], axis=0)
    at = jnp.concatenate([line[:SLOTS], other_line], axis=0)
    before = lax.rem(device + CHORD - 1, CHORD) * SLOTS + NEAR + at
    after = lax.rem(device + 1, CHORD) * SLOTS + at - (LINES - NEAR)
    source = jnp.where(at < NEAR, before, jnp.where(at >= LINES - NEAR, after, -1))
    added = dot_nn((iota((2 * SLOTS, LINES), 1) == source).astype(f32), all_reach)

    spot = iota((LINES, SENT), 0) - (LINES - ROWS)
    row_at = iota((LINES, SENT), 1) // COLS - NEAR
    inner = ((spot == row_at) & (spot >= 0)).astype(f32)
    rim_row = jnp.where(spot < NEAR, spot - NEAR, spot + ROWS - NEAR)
    rim = ((rim_row == row_at) & (spot >= 0) & (spot < 2 * NEAR)).astype(f32)
    row8 = iota((SLOTS, SENT), 0)
    halo_base = jnp.where(row8 < 3, left[24:32], right[24:32])
    halo_rim = jnp.where(row8 < 3, left[16:24], right[16:24])
    scales = dot_nn(
        jnp.concatenate([mine[8:16], other_base, halo_base], axis=0)[:, SENT - LINES :], inner
    )
    slot_scale = scales[: 2 * SLOTS]
    halo_scale = scales[2 * SLOTS :] + dot_nn(halo_rim[:, SENT - LINES :], rim)

    own_w = mine[8:16] + slot_scale[:SLOTS] * added[:SLOTS] + apart[:SLOTS]
    other_w = other_base + slot_scale[SLOTS:] * added[SLOTS:] - apart[:SLOTS]
    apart_w = penalty_weight * (own_w - other_w)

    target = iota((2 * SLOTS, SLOTS), 1)
    from_left = iota((2 * SLOTS, SLOTS), 0) < SLOTS
    chosen = (edge_line(target) == line[SLOTS:]) & ((target < 3) == from_left)
    halo_apart = dot_tn(chosen.astype(f32), apart[SLOTS:])
    halo_w = halo_base + halo_scale * mine[16:24] + halo_apart
    halo_v = jnp.where(row8 < 6, halo_scale * halo_w, 0.0)

    lane = iota((SLOTS, LINES), 1)
    low8 = iota((SLOTS, LINES), 0)
    at_slot = (lane == line[:SLOTS]).astype(f32)
    at_edge = (lane == edge_line(low8)).astype(f32)
    none = jnp.zeros((SLOTS, LINES), f32)
    arrived = jnp.where(row8 < 3, right[16:24], left[16:24])
    first = dot_tn(
        jnp.concatenate([apart[:SLOTS], arrived], axis=0),
        jnp.concatenate(
            [
                jnp.concatenate([at_slot, none], axis=1),
                jnp.concatenate([none, at_edge], axis=1),
            ],
            axis=0,
        ),
    )
    distance = jnp.abs(outer_line(low8) - lane)
    second = dot_tn(
        jnp.concatenate([halo_v, apart_w], axis=0),
        jnp.concatenate(
            [
                jnp.concatenate(
                    [taps_at(distance, mass_taps), taps_at(distance, bend_taps), none], axis=1
                ),
                jnp.concatenate([none, none, at_slot], axis=1),
            ],
            axis=0,
        ),
    )
    scale = rows_of(below_ref, s_ref, above_ref, DEEP * COLS, NEAR)
    images, masses, bends = [], [], []
    for row in range(WIDE):
        cut = slice(row * COLS, (row + 1) * COLS)
        scale_row = spread(scale[row])
        image = base_ref[cut, :] + first[cut, :LINES] + scale_row * first[cut, LINES:]
        value = scale_row * image
        mass, bend = mass_taps[0] * value, bend_taps[0] * value
        for step in range(1, 4):
            pair = pair_of(value, step)
            mass = mass + mass_taps[step] * pair
            if bend_taps[step] != 0.0:
                bend = bend + bend_taps[step] * pair
        images.append(image)
        masses.append(mass + second[cut, :LINES])
        bends.append(bend + second[cut, LINES : 2 * LINES])
    seconds = []
    for row in range(ROWS):
        at_row = row + NEAR
        cut = slice(at_row * COLS, (at_row + 1) * COLS)
        total = row_stencil(masses, at_row, bend_taps) + row_stencil(bends, at_row, mass_taps)
        product = (
            spread(scale[at_row]) * total
            + spread(d_ref[row : row + 1, :]) * images[at_row]
            + second[cut, 2 * LINES :]
        )
        w_ref[pl.ds(row * COLS, COLS), :] = images[at_row]
        z_ref[pl.ds(row * COLS, COLS), :] = product
        seconds.append(product)
    r = jnp.concatenate([field_ref[pl.ds(k * COLS, COLS), :] for k in range(ROWS)], axis=1)
    w = jnp.concatenate(images[NEAR : NEAR + ROWS], axis=1)
    z = jnp.concatenate(seconds, axis=1)
    gram = jnp.concatenate(
        [
            dot_nt(r, jnp.concatenate([r, w], axis=0)),
            dot_nt(w, jnp.concatenate([w, z], axis=0)),
        ],
        axis=1,
    )
    gram = jnp.concatenate([gram[:8], gram[8:]], axis=1)
    for device in range(gram_ref.shape[0]):
        gram_ref[device] = gram


def total_kernel(parts_ref, out_ref):
    total = jnp.sum(parts_ref[...], axis=0)
    for device in range(out_ref.shape[0]):
        out_ref[device] = total


def finish_kernel(parts_ref, field_ref, w_ref, z_ref, x_ref, res_ref):
    packed = jnp.sum(parts_ref[...], axis=0)
    gram = jnp.concatenate([packed[:, : 4 * COLS], packed[:, 4 * COLS :]], axis=0)
    g00, g01 = gram[:, :COLS], gram[:, COLS : 2 * COLS]
    g11, g12 = gram[:, 2 * COLS : 3 * COLS], gram[:, 3 * COLS :]
    work = jnp.concatenate(
        [
            jnp.concatenate([g01, g11], axis=1),
            jnp.concatenate([g11, g12], axis=1),
            jnp.concatenate([g00, g01], axis=1),
        ],
        axis=0,
    )
    lane = iota((1, 2 * COLS), 1)
    for step in range(2 * COLS):
        row = work[step : step + 1, :]
        column = work[:, step : step + 1] / row[:, step : step + 1]
        work = jnp.where(lane == step, column, work - column * row)
    coeffs = work[2 * COLS :, :]
    r = jnp.concatenate([field_ref[pl.ds(k * COLS, COLS), :] for k in range(ROWS)], axis=1)
    w = jnp.concatenate([w_ref[pl.ds(k * COLS, COLS), :] for k in range(ROWS)], axis=1)
    z = jnp.concatenate([z_ref[pl.ds(k * COLS, COLS), :] for k in range(ROWS)], axis=1)
    x = dot_nn(coeffs, jnp.concatenate([r, w], axis=0))
    res = r - dot_nn(coeffs, jnp.concatenate([w, z], axis=0))
    for row in range(ROWS):
        cut = slice(row * LINES, (row + 1) * LINES)
        x_ref[pl.ds(row, COLS, stride=ROWS), :] = x[:, cut]
        res_ref[pl.ds(row, COLS, stride=ROWS), :] = res[:, cut]


def call(kernel, shapes, smem=0):
    def run(*args):
        specs = [pl.BlockSpec(memory_space=pltpu.SMEM)] * smem
        specs += [pl.BlockSpec(memory_space=pltpu.VMEM)] * (len(args) - smem)
        return pl.pallas_call(
            kernel,
            out_shape=[jax.ShapeDtypeStruct(shape, f32) for shape in shapes],
            in_specs=specs,
            out_specs=[pl.BlockSpec(memory_space=pltpu.VMEM)] * len(shapes),
            interpret=INTERPRET,
            compiler_params=pltpu.CompilerParams(vmem_limit_bytes=KERNEL_BYTES),
        )(*args)

    return run


def body(right_side, stiff_scale, extra_diag, iface_line, partner):
    span = lax.axis_size(SPAN)
    plane = lax.axis_size(("core", "chord"))
    depth = lax.axis_size("z")
    cells = right_side.reshape(COLS * ROWS, LINES)
    halo = (DEEP * COLS + 16, LINES)
    flat = (ROWS * COLS, LINES)
    field, up, down = call(pack_kernel, [flat, halo, halo])(cells, stiff_scale, extra_diag)
    below = lax.ppermute(up, SPAN, [(i, i + 1) for i in range(span - 1)])
    above = lax.ppermute(down, SPAN, [(i + 1, i) for i in range(span - 1)])
    base, message = call(send_kernel, [(FLAT, LINES), (CHORD, SPARE, SENT)], smem=2)(
        iface_line, partner, field, stiff_scale, extra_diag, below, above
    )
    here = lax.axis_index("chord").reshape(1)
    message, here = lax.optimization_barrier((message, here))
    got = lax.all_to_all(message, "chord", 0, 0)
    w, z, gram = call(apply_kernel, [flat, flat, (plane, 8, LINES)], smem=1)(
        here, got, field, base, stiff_scale, extra_diag, below, above
    )
    gram = lax.all_to_all(gram, ("core", "chord"), 0, 0)
    (gram,) = call(total_kernel, [(depth, 8, LINES)])(gram)
    gram = lax.all_to_all(gram, "z", 0, 0)
    x, res = call(finish_kernel, [flat, flat])(gram, field, w, z)
    return (x.reshape(COLS, ROWS, LINES), res.reshape(COLS, ROWS, LINES))


def solution(mesh):
    chord = mesh.devices.shape[1]
    fine = Mesh(mesh.devices.reshape(-1, 2, chord), ("z", "core", "chord"))
    return jax.shard_map(
        body,
        mesh=fine,
        in_specs=(
            P(None, SPAN, "chord"),
            P(SPAN, "chord"),
            P(SPAN, "chord"),
            P("chord"),
            P("chord"),
        ),
        out_specs=(P(None, SPAN, "chord"), P(None, SPAN, "chord")),
        check_vma=False,
    )
```

```python
import jax
import jax.numpy as jnp
from jax import lax
from jax.experimental import pallas as pl
from jax.experimental.pallas import tpu as pltpu
from jax.sharding import Mesh
from jax.sharding import PartitionSpec as P

SPAN = ("z", "core")
COLS = 16
ROWS = 32
LINES = 128
SLOTS = 8
CHORD = 16
DEEP = 6
NEAR = 3
WIDE = ROWS + 2 * NEAR
FLAT = WIDE * COLS
SENT = 640
SPARE = 32

mass_taps = (2416.0 / 5040.0, 1191.0 / 5040.0, 120.0 / 5040.0, 1.0 / 5040.0)
bend_taps = (8.0 / 3.0, -1.5, 0.0, 1.0 / 6.0)
penalty_weight = 4.0

f32 = jnp.float32
KERNEL_BYTES = 24 << 20
INTERPRET = False


def dot(left, right, contract):
    return lax.dot_general(
        left,
        right,
        (contract, ((), ())),
        precision=lax.Precision.HIGHEST,
        preferred_element_type=f32,
    )


def dot_nn(left, right):
    return dot(left, right, ((1,), (0,)))


def dot_nt(left, right):
    return dot(left, right, ((1,), (1,)))


def dot_tn(left, right):
    return dot(left, right, ((0,), (0,)))


def iota(shape, dim):
    return lax.broadcasted_iota(jnp.int32, shape, dim)


def taps_at(distance, taps):
    value = jnp.zeros(distance.shape, f32)
    for step in range(4):
        if taps[step] != 0.0:
            value = jnp.where(distance == step, taps[step], value)
    return value


def outer_line(row):
    return jnp.where(row < 3, row - 3, jnp.where(row < 6, row + LINES - 3, 4 * LINES))


def edge_line(row):
    return jnp.where(row < 3, row + LINES - 3, jnp.where(row < 6, row - 3, 4 * LINES))


def pair_of(field, step):
    lane = iota((COLS, LINES), 1)
    ahead = jnp.where(lane < LINES - step, pltpu.roll(field, LINES - step, 1), 0.0)
    behind = jnp.where(lane >= step, pltpu.roll(field, step, 1), 0.0)
    return ahead + behind


def row_stencil(rows, at, taps):
    total = taps[0] * rows[at]
    for step in range(1, 4):
        if taps[step] != 0.0:
            total = total + taps[step] * (rows[at - step] + rows[at + step])
    return total


def spread(row):
    return jnp.broadcast_to(row, (COLS, LINES))


def pack_kernel(
    line_hbm, partner_hbm, r_hbm, s_hbm, d_hbm,
    field_ref, far_ref, near_ref, s_ref, d_ref, slots_ref,
    r_ref, line_ref, partner_ref, sems
):
    copies = [
        pltpu.make_async_copy(source, target, sems.at[k])
        for k, (source, target) in enumerate(
            [
                (r_hbm, r_ref),
                (s_hbm, s_ref),
                (d_hbm, d_ref),
                (line_hbm, line_ref),
                (partner_hbm, partner_ref),
            ]
        )
    ]
    for copy in copies:
        copy.start()
    for copy in copies:
        copy.wait()
    first_core = lax.axis_index("core") == 0
    rows = []
    for row in range(ROWS):
        cells = r_ref[pl.ds(row, COLS, stride=ROWS), :]
        field_ref[pl.ds(row * COLS, COLS), :] = cells
        rows.append(cells)
    pad = jnp.zeros((2, LINES), f32)
    low, high = slice(0, DEEP), slice(ROWS - DEEP, ROWS)
    ends = [
        jnp.concatenate(rows[cut] + [s_ref[cut, :], pad, d_ref[cut, :], pad], axis=0)
        for cut in (low, high)
    ]
    far_ref[...] = jnp.where(first_core, ends[0], ends[1])
    near_ref[...] = jnp.where(first_core, ends[1], ends[0])
    row = iota((SLOTS, LINES), 0)
    for k, scalars in enumerate((line_ref, partner_ref)):
        value = jnp.zeros((SLOTS, LINES), jnp.int32)
        for slot in range(SLOTS):
            value = jnp.where(row == slot, scalars[slot], value)
        slots_ref[k] = value


def send_kernel(
    field_ref, s_ref, d_ref, far_ref, near_ref, slots_ref, base_ref, scale_ref, message_ref
):
    first_core = lax.axis_index("core") == 0
    below = jnp.where(first_core, far_ref[...], near_ref[...])
    above = jnp.where(first_core, near_ref[...], far_ref[...])
    start = DEEP * COLS
    scale_ref[0:DEEP, :] = below[start : start + DEEP]
    scale_ref[DEEP : DEEP + ROWS, :] = s_ref[...]
    scale_ref[DEEP + ROWS : 2 * DEEP + ROWS, :] = above[start : start + DEEP]
    scale = [below[start + k : start + k + 1] for k in range(DEEP)]
    scale += [s_ref[k : k + 1, :] for k in range(ROWS)]
    scale += [above[start + k : start + k + 1] for k in range(DEEP)]
    start += 8
    extra = [below[start + k : start + k + 1] for k in range(DEEP - NEAR, DEEP)]
    extra += [d_ref[k : k + 1, :] for k in range(ROWS)]
    extra += [above[start + k : start + k + 1] for k in range(NEAR)]
    cells = [below[k * COLS : (k + 1) * COLS] for k in range(DEEP)]
    cells += [field_ref[pl.ds(k * COLS, COLS), :] for k in range(ROWS)]
    cells += [above[k * COLS : (k + 1) * COLS] for k in range(DEEP)]
    weighted = [spread(scale[k]) * cells[k] for k in range(ROWS + 2 * DEEP)]
    masses, bends, bases = [], [], []
    for row in range(WIDE):
        mass = row_stencil(weighted, row + NEAR, mass_taps)
        bend = row_stencil(weighted, row + NEAR, bend_taps)
        total = mass_taps[0] * bend + bend_taps[0] * mass
        for step in range(1, 4):
            mixed = mass_taps[step] * bend
            if bend_taps[step] != 0.0:
                mixed = mixed + bend_taps[step] * mass
            total = total + pair_of(mixed, step)
        base = spread(scale[row + NEAR]) * total + spread(extra[row]) * cells[row + NEAR]
        masses.append(mass)
        bends.append(bend)
        bases.append(base)
        base_ref[pl.ds(row * COLS, COLS), :] = base
    own_scale = s_ref[...]
    blank = jnp.zeros((SENT - FLAT, LINES), f32)
    lane = iota((SLOTS, LINES), 1)
    row8 = iota((SLOTS, LINES), 0)
    at_slot = (lane == slots_ref[0]).astype(f32)
    at_edge = (lane == edge_line(row8)).astype(f32)
    values = jnp.concatenate(cells[NEAR : NEAR + WIDE] + [blank], axis=0)
    sent_cells = dot_nt(at_slot, values)
    wide_lane = iota((SLOTS, SENT), 1)
    slot_numbers = [
        jnp.concatenate([slots_ref[k].astype(f32)] * (SENT // LINES), axis=1) for k in range(2)
    ]
    sent_cells = jnp.where(wide_lane == FLAT, slot_numbers[1], sent_cells)
    sent_cells = jnp.where(wide_lane == FLAT + 1, slot_numbers[0], sent_cells)
    sent_base = dot_nt(
        jnp.concatenate([at_slot, at_edge], axis=0),
        jnp.concatenate(bases + [own_scale], axis=0),
    )
    distance = jnp.abs(outer_line(row8) - lane)
    rim = [scale[NEAR + k] for k in (0, 1, 2, WIDE - 3, WIDE - 2, WIDE - 1)]
    rim_stack = jnp.concatenate(rim + [jnp.zeros((SENT - FLAT - 6, LINES), f32)], axis=0)
    reach = jnp.concatenate(
        [taps_at(distance, mass_taps), taps_at(distance, bend_taps)], axis=1
    )
    sent_reach = dot_nt(
        jnp.concatenate([reach, at_edge], axis=1),
        jnp.concatenate(
            [
                jnp.concatenate(bends + [blank], axis=0),
                jnp.concatenate(masses + [blank], axis=0),
                jnp.concatenate([jnp.zeros((FLAT, LINES), f32), rim_stack], axis=0),
            ],
            axis=1,
        ),
    )
    message = jnp.concatenate([sent_cells, sent_base[:SLOTS], sent_reach, sent_base[SLOTS:]], axis=0)
    for device in range(CHORD):
        message_ref[device] = message


def apply_kernel(
    got_ref, field_ref, base_ref, scale_ref, d_ref, w_ref, z_ref, gram_ref
):
    here = lax.axis_index("chord")
    mine = got_ref[here]
    left = got_ref[lax.rem(here + CHORD - 1, CHORD)]
    right = got_ref[lax.rem(here + 1, CHORD)]
    all_cells = got_ref[:, 0:8, :].reshape(CHORD * SLOTS, SENT)
    all_base = got_ref[:, 8:16, :].reshape(CHORD * SLOTS, SENT)
    all_reach = got_ref[:, 16:24, :].reshape(CHORD * SLOTS, SENT)

    slots = jnp.concatenate([mine[0:8], left[0:8], right[0:8]], axis=0)
    partner = slots[:, FLAT : FLAT + 1].astype(jnp.int32)
    line = slots[:, FLAT + 1 : FLAT + 2].astype(jnp.int32)
    pick = (iota((3 * SLOTS, LINES), 1) == partner).astype(f32)
    other = dot_nn(pick, all_cells)
    apart = penalty_weight * (slots - other)
    other_line = other[:SLOTS, FLAT + 1 : FLAT + 2].astype(jnp.int32)
    other_device = partner[:SLOTS] // SLOTS
    other_base = dot_nn(pick[:SLOTS], all_base)

    device = jnp.concatenate([jnp.full((SLOTS, 1), here, jnp.int32), other_device], axis=0)
    at = jnp.concatenate([line[:SLOTS], other_line], axis=0)
    before = lax.rem(device + CHORD - 1, CHORD) * SLOTS + NEAR + at
    after = lax.rem(device + 1, CHORD) * SLOTS + at - (LINES - NEAR)
    source = jnp.where(at < NEAR, before, jnp.where(at >= LINES - NEAR, after, -1))
    added = dot_nn((iota((2 * SLOTS, LINES), 1) == source).astype(f32), all_reach)

    spot = iota((LINES, SENT), 0) - (LINES - ROWS)
    row_at = iota((LINES, SENT), 1) // COLS - NEAR
    inner = ((spot == row_at) & (spot >= 0)).astype(f32)
    rim_row = jnp.where(spot < NEAR, spot - NEAR, spot + ROWS - NEAR)
    rim = ((rim_row == row_at) & (spot >= 0) & (spot < 2 * NEAR)).astype(f32)
    row8 = iota((SLOTS, SENT), 0)
    halo_base = jnp.where(row8 < 3, left[24:32], right[24:32])
    halo_rim = jnp.where(row8 < 3, left[16:24], right[16:24])
    scales = dot_nn(
        jnp.concatenate([mine[8:16], other_base, halo_base], axis=0)[:, SENT - LINES :], inner
    )
    slot_scale = scales[: 2 * SLOTS]
    halo_scale = scales[2 * SLOTS :] + dot_nn(halo_rim[:, SENT - LINES :], rim)

    own_w = mine[8:16] + slot_scale[:SLOTS] * added[:SLOTS] + apart[:SLOTS]
    other_w = other_base + slot_scale[SLOTS:] * added[SLOTS:] - apart[:SLOTS]
    apart_w = penalty_weight * (own_w - other_w)

    target = iota((2 * SLOTS, SLOTS), 1)
    from_left = iota((2 * SLOTS, SLOTS), 0) < SLOTS
    chosen = (edge_line(target) == line[SLOTS:]) & ((target < 3) == from_left)
    halo_apart = dot_tn(chosen.astype(f32), apart[SLOTS:])
    halo_w = halo_base + halo_scale * mine[16:24] + halo_apart
    halo_v = jnp.where(row8 < 6, halo_scale * halo_w, 0.0)

    lane = iota((SLOTS, LINES), 1)
    low8 = iota((SLOTS, LINES), 0)
    at_slot = (lane == line[:SLOTS]).astype(f32)
    at_edge = (lane == edge_line(low8)).astype(f32)
    none = jnp.zeros((SLOTS, LINES), f32)
    arrived = jnp.where(row8 < 3, right[16:24], left[16:24])
    first = dot_tn(
        jnp.concatenate([apart[:SLOTS], arrived], axis=0),
        jnp.concatenate(
            [
                jnp.concatenate([at_slot, none], axis=1),
                jnp.concatenate([none, at_edge], axis=1),
            ],
            axis=0,
        ),
    )
    distance = jnp.abs(outer_line(low8) - lane)
    second = dot_tn(
        jnp.concatenate([halo_v, apart_w], axis=0),
        jnp.concatenate(
            [
                jnp.concatenate(
                    [taps_at(distance, mass_taps), taps_at(distance, bend_taps), none], axis=1
                ),
                jnp.concatenate([none, none, at_slot], axis=1),
            ],
            axis=0,
        ),
    )
    scale = [scale_ref[NEAR + k : NEAR + k + 1, :] for k in range(WIDE)]
    images, masses, bends = [], [], []
    for row in range(WIDE):
        cut = slice(row * COLS, (row + 1) * COLS)
        scale_row = spread(scale[row])
        image = base_ref[cut, :] + first[cut, :LINES] + scale_row * first[cut, LINES:]
        value = scale_row * image
        mass, bend = mass_taps[0] * value, bend_taps[0] * value
        for step in range(1, 4):
            pair = pair_of(value, step)
            mass = mass + mass_taps[step] * pair
            if bend_taps[step] != 0.0:
                bend = bend + bend_taps[step] * pair
        images.append(image)
        masses.append(mass + second[cut, :LINES])
        bends.append(bend + second[cut, LINES : 2 * LINES])
    seconds = []
    for row in range(ROWS):
        at_row = row + NEAR
        cut = slice(at_row * COLS, (at_row + 1) * COLS)
        total = row_stencil(masses, at_row, bend_taps) + row_stencil(bends, at_row, mass_taps)
        product = (
            spread(scale[at_row]) * total
            + spread(d_ref[row : row + 1, :]) * images[at_row]
            + second[cut, 2 * LINES :]
        )
        w_ref[pl.ds(row * COLS, COLS), :] = images[at_row]
        z_ref[pl.ds(row * COLS, COLS), :] = product
        seconds.append(product)
    r = jnp.concatenate([field_ref[pl.ds(k * COLS, COLS), :] for k in range(ROWS)], axis=1)
    w = jnp.concatenate(images[NEAR : NEAR + ROWS], axis=1)
    z = jnp.concatenate(seconds, axis=1)
    gram = jnp.concatenate(
        [
            dot_nt(r, jnp.concatenate([r, w], axis=0)),
            dot_nt(w, jnp.concatenate([w, z], axis=0)),
        ],
        axis=1,
    )
    gram = jnp.concatenate([gram[:8], gram[8:]], axis=1)
    for device in range(gram_ref.shape[0]):
        gram_ref[device] = gram


def total_kernel(parts_ref, out_ref):
    total = jnp.sum(parts_ref[...], axis=0)
    for device in range(out_ref.shape[0]):
        out_ref[device] = total


def finish_kernel(parts_ref, field_ref, w_ref, z_ref, x_ref, res_ref):
    packed = jnp.sum(parts_ref[...], axis=0)
    gram = jnp.concatenate([packed[:, : 4 * COLS], packed[:, 4 * COLS :]], axis=0)
    g00, g01 = gram[:, :COLS], gram[:, COLS : 2 * COLS]
    g11, g12 = gram[:, 2 * COLS : 3 * COLS], gram[:, 3 * COLS :]
    work = jnp.concatenate(
        [
            jnp.concatenate([g01, g11], axis=1),
            jnp.concatenate([g11, g12], axis=1),
            jnp.concatenate([g00, g01], axis=1),
        ],
        axis=0,
    )
    lane = iota((1, 2 * COLS), 1)
    for step in range(0, 2 * COLS, 2):
        row0, row1 = work[step : step + 1, :], work[step + 1 : step + 2, :]
        column0, column1 = work[:, step : step + 1], work[:, step + 1 : step + 2]
        a, b = row0[:, step : step + 1], row0[:, step + 1 : step + 2]
        c, d = row1[:, step : step + 1], row1[:, step + 1 : step + 2]
        over_a, over_d = 1.0 / a, 1.0 / d
        rest = 1.0 / (1.0 - (b * over_a) * (c * over_d))
        i00, i11 = over_a * rest, over_d * rest
        i01, i10 = -(b * over_d) * i00, -(c * over_a) * i11
        is0, is1 = lane == step, lane == step + 1
        row0 = jnp.where(is0, -1.0, jnp.where(is1, 0.0, row0))
        row1 = jnp.where(is1, -1.0, jnp.where(is0, 0.0, row1))
        kept = jnp.where(is0 | is1, 0.0, work)
        work = kept - column0 * (i00 * row0 + i01 * row1) - column1 * (i10 * row0 + i11 * row1)
    coeffs = work[2 * COLS :, :]
    r = jnp.concatenate([field_ref[pl.ds(k * COLS, COLS), :] for k in range(ROWS)], axis=1)
    w = jnp.concatenate([w_ref[pl.ds(k * COLS, COLS), :] for k in range(ROWS)], axis=1)
    z = jnp.concatenate([z_ref[pl.ds(k * COLS, COLS), :] for k in range(ROWS)], axis=1)
    x = dot_nn(coeffs, jnp.concatenate([r, w], axis=0))
    res = r - dot_nn(coeffs, jnp.concatenate([w, z], axis=0))
    for row in range(ROWS):
        cut = slice(row * LINES, (row + 1) * LINES)
        x_ref[pl.ds(row, COLS, stride=ROWS), :] = x[:, cut]
        res_ref[pl.ds(row, COLS, stride=ROWS), :] = res[:, cut]


def call(kernel, shapes, hbm=False, scratch=()):
    def run(*args):
        if hbm and not INTERPRET:
            args = [pltpu.with_memory_space_constraint(arg, pltpu.HBM) for arg in args]
        return pl.pallas_call(
            kernel,
            out_shape=[
                jax.ShapeDtypeStruct(shape, kind) for shape, kind in map(typed, shapes)
            ],
            in_specs=[pl.BlockSpec(memory_space=pltpu.HBM if hbm else pltpu.VMEM)] * len(args),
            out_specs=[pl.BlockSpec(memory_space=pltpu.VMEM)] * len(shapes),
            scratch_shapes=scratch,
            interpret=INTERPRET,
            compiler_params=pltpu.CompilerParams(vmem_limit_bytes=KERNEL_BYTES),
        )(*args)

    return run


def typed(shape):
    return shape if isinstance(shape[0], tuple) else (shape, f32)


def body(right_side, stiff_scale, extra_diag, iface_line, partner):
    span = lax.axis_size(SPAN)
    plane = lax.axis_size(("core", "chord"))
    depth = lax.axis_size("z")
    cells = right_side.reshape(COLS * ROWS, LINES)
    halo = (DEEP * COLS + 16, LINES)
    flat = (ROWS * COLS, LINES)
    one = (ROWS, LINES)
    field, far, near, scale, extra, slots = call(
        pack_kernel,
        [flat, halo, halo, one, one, ((2, SLOTS, LINES), jnp.int32)],
        hbm=True,
        scratch=[
            pltpu.VMEM(flat, f32),
            pltpu.SMEM((SLOTS,), jnp.int32),
            pltpu.SMEM((SLOTS,), jnp.int32),
            pltpu.SemaphoreType.DMA((5,)),
        ],
    )(iface_line, partner, cells, stiff_scale, extra_diag)
    swaps = [(i, i + 1) for i in range(1, span - 1, 2)]
    far = lax.ppermute(far, SPAN, swaps + [(b, a) for a, b in swaps])
    swaps = [(i, i + 1) for i in range(0, span, 2)]
    near = lax.ppermute(near, SPAN, swaps + [(b, a) for a, b in swaps])
    base, scale, message = call(
        send_kernel, [(FLAT, LINES), (ROWS + 2 * DEEP, LINES), (CHORD, SPARE, SENT)]
    )(field, scale, extra, far, near, slots)
    got = lax.all_to_all(message, "chord", 0, 0)
    w, z, gram = call(apply_kernel, [flat, flat, (plane, 8, LINES)])(
        got, field, base, scale, extra
    )
    gram = lax.all_to_all(gram, ("core", "chord"), 0, 0)
    (gram,) = call(total_kernel, [(depth, 8, LINES)])(gram)
    gram = lax.all_to_all(gram, "z", 0, 0)
    x, res = call(finish_kernel, [flat, flat])(gram, field, w, z)
    return (x.reshape(COLS, ROWS, LINES), res.reshape(COLS, ROWS, LINES))


def solution(mesh):
    chord = mesh.devices.shape[1]
    fine = Mesh(mesh.devices.reshape(-1, 2, chord), ("z", "core", "chord"))
    return jax.shard_map(
        body,
        mesh=fine,
        in_specs=(
            P(None, SPAN, "chord"),
            P(SPAN, "chord"),
            P(SPAN, "chord"),
            P("chord"),
            P("chord"),
        ),
        out_specs=(P(None, SPAN, "chord"), P(None, SPAN, "chord")),
        check_vma=False,
    )
```

```python
import jax
import jax.numpy as jnp
from jax import lax
from jax.experimental import pallas as pl
from jax.experimental.pallas import tpu as pltpu
from jax.sharding import Mesh
from jax.sharding import PartitionSpec as P

SPAN = ("z", "core")
COLS = 16
ROWS = 32
LINES = 128
SLOTS = 8
CHORD = 16
DEEP = 6
NEAR = 3
WIDE = ROWS + 2 * NEAR
FLAT = WIDE * COLS
SENT = 640
PANEL = 16
SPARE = 32

mass_taps = (2416.0 / 5040.0, 1191.0 / 5040.0, 120.0 / 5040.0, 1.0 / 5040.0)
bend_taps = (8.0 / 3.0, -1.5, 0.0, 1.0 / 6.0)
penalty_weight = 4.0

f32 = jnp.float32
KERNEL_BYTES = 24 << 20
INTERPRET = False


def dot(left, right, contract):
    return lax.dot_general(
        left,
        right,
        (contract, ((), ())),
        precision=lax.Precision.HIGHEST,
        preferred_element_type=f32,
    )


def dot_nn(left, right):
    return dot(left, right, ((1,), (0,)))


def dot_nt(left, right):
    return dot(left, right, ((1,), (1,)))


def dot_tn(left, right):
    return dot(left, right, ((0,), (0,)))


def iota(shape, dim):
    return lax.broadcasted_iota(jnp.int32, shape, dim)


def taps_at(distance, taps):
    value = jnp.zeros(distance.shape, f32)
    for step in range(4):
        if taps[step] != 0.0:
            value = jnp.where(distance == step, taps[step], value)
    return value


def outer_line(row):
    return jnp.where(row < 3, row - 3, jnp.where(row < 6, row + LINES - 3, 4 * LINES))


def edge_line(row):
    return jnp.where(row < 3, row + LINES - 3, jnp.where(row < 6, row - 3, 4 * LINES))


def pair_of(field, step):
    lane = iota((COLS, LINES), 1)
    ahead = jnp.where(lane < LINES - step, pltpu.roll(field, LINES - step, 1), 0.0)
    behind = jnp.where(lane >= step, pltpu.roll(field, step, 1), 0.0)
    return ahead + behind


def row_stencil(rows, at, taps):
    total = taps[0] * rows[at]
    for step in range(1, 4):
        if taps[step] != 0.0:
            total = total + taps[step] * (rows[at - step] + rows[at + step])
    return total


def spread(row):
    return jnp.broadcast_to(row, (COLS, LINES))


def pack_kernel(
    line_hbm, partner_hbm, r_hbm, s_hbm, d_hbm,
    field_ref, far_ref, near_ref, s_ref, d_ref, slots_ref,
    r_ref, line_ref, partner_ref, sems
):
    copies = [
        pltpu.make_async_copy(source, target, sems.at[k])
        for k, (source, target) in enumerate(
            [
                (r_hbm, r_ref),
                (s_hbm, s_ref),
                (d_hbm, d_ref),
                (line_hbm, line_ref),
                (partner_hbm, partner_ref),
            ]
        )
    ]
    for copy in copies:
        copy.start()
    for copy in copies:
        copy.wait()
    first_core = lax.axis_index("core") == 0
    rows = []
    for row in range(ROWS):
        cells = r_ref[pl.ds(row, COLS, stride=ROWS), :]
        field_ref[pl.ds(row * COLS, COLS), :] = cells
        rows.append(cells)
    pad = jnp.zeros((2, LINES), f32)
    low, high = slice(0, DEEP), slice(ROWS - DEEP, ROWS)
    ends = [
        jnp.concatenate(rows[cut] + [s_ref[cut, :], pad, d_ref[cut, :], pad], axis=0)
        for cut in (low, high)
    ]
    far_ref[...] = jnp.where(first_core, ends[0], ends[1])
    near_ref[...] = jnp.where(first_core, ends[1], ends[0])
    row = iota((SLOTS, LINES), 0)
    for k, scalars in enumerate((line_ref, partner_ref)):
        value = jnp.zeros((SLOTS, LINES), jnp.int32)
        for slot in range(SLOTS):
            value = jnp.where(row == slot, scalars[slot], value)
        slots_ref[k] = value


def send_kernel(
    field_ref, s_ref, d_ref, far_ref, near_ref, slots_ref, base_ref, scale_ref, message_ref
):
    first_core = lax.axis_index("core") == 0
    below = jnp.where(first_core, far_ref[...], near_ref[...])
    above = jnp.where(first_core, near_ref[...], far_ref[...])
    start = DEEP * COLS
    scale_ref[0:DEEP, :] = below[start : start + DEEP]
    scale_ref[DEEP : DEEP + ROWS, :] = s_ref[...]
    scale_ref[DEEP + ROWS : 2 * DEEP + ROWS, :] = above[start : start + DEEP]
    scale = [below[start + k : start + k + 1] for k in range(DEEP)]
    scale += [s_ref[k : k + 1, :] for k in range(ROWS)]
    scale += [above[start + k : start + k + 1] for k in range(DEEP)]
    start += 8
    extra = [below[start + k : start + k + 1] for k in range(DEEP - NEAR, DEEP)]
    extra += [d_ref[k : k + 1, :] for k in range(ROWS)]
    extra += [above[start + k : start + k + 1] for k in range(NEAR)]
    cells = [below[k * COLS : (k + 1) * COLS] for k in range(DEEP)]
    cells += [field_ref[pl.ds(k * COLS, COLS), :] for k in range(ROWS)]
    cells += [above[k * COLS : (k + 1) * COLS] for k in range(DEEP)]
    weighted = [spread(scale[k]) * cells[k] for k in range(ROWS + 2 * DEEP)]
    masses, bends, bases = [], [], []
    for row in range(WIDE):
        mass = row_stencil(weighted, row + NEAR, mass_taps)
        bend = row_stencil(weighted, row + NEAR, bend_taps)
        total = mass_taps[0] * bend + bend_taps[0] * mass
        for step in range(1, 4):
            mixed = mass_taps[step] * bend
            if bend_taps[step] != 0.0:
                mixed = mixed + bend_taps[step] * mass
            total = total + pair_of(mixed, step)
        base = spread(scale[row + NEAR]) * total + spread(extra[row]) * cells[row + NEAR]
        masses.append(mass)
        bends.append(bend)
        bases.append(base)
        base_ref[pl.ds(row * COLS, COLS), :] = base
    own_scale = s_ref[...]
    blank = jnp.zeros((SENT - FLAT, LINES), f32)
    lane = iota((SLOTS, LINES), 1)
    row8 = iota((SLOTS, LINES), 0)
    at_slot = (lane == slots_ref[0]).astype(f32)
    at_edge = (lane == edge_line(row8)).astype(f32)
    values = jnp.concatenate(cells[NEAR : NEAR + WIDE] + [blank], axis=0)
    sent_cells = dot_nt(at_slot, values)
    wide_lane = iota((SLOTS, SENT), 1)
    slot_numbers = [
        jnp.concatenate([slots_ref[k].astype(f32)] * (SENT // LINES), axis=1) for k in range(2)
    ]
    sent_cells = jnp.where(wide_lane == FLAT, slot_numbers[1], sent_cells)
    sent_cells = jnp.where(wide_lane == FLAT + 1, slot_numbers[0], sent_cells)
    sent_base = dot_nt(
        jnp.concatenate([at_slot, at_edge], axis=0),
        jnp.concatenate(bases + [own_scale], axis=0),
    )
    distance = jnp.abs(outer_line(row8) - lane)
    rim = [scale[NEAR + k] for k in (0, 1, 2, WIDE - 3, WIDE - 2, WIDE - 1)]
    rim_stack = jnp.concatenate(rim + [jnp.zeros((SENT - FLAT - 6, LINES), f32)], axis=0)
    reach = jnp.concatenate(
        [taps_at(distance, mass_taps), taps_at(distance, bend_taps)], axis=1
    )
    sent_reach = dot_nt(
        jnp.concatenate([reach, at_edge], axis=1),
        jnp.concatenate(
            [
                jnp.concatenate(bends + [blank], axis=0),
                jnp.concatenate(masses + [blank], axis=0),
                jnp.concatenate([jnp.zeros((FLAT, LINES), f32), rim_stack], axis=0),
            ],
            axis=1,
        ),
    )
    message = jnp.concatenate([sent_cells, sent_base[:SLOTS], sent_reach, sent_base[SLOTS:]], axis=0)
    for device in range(CHORD):
        message_ref[device] = message


def apply_kernel(
    got_ref, field_ref, base_ref, scale_ref, d_ref, w_ref, z_ref, gram_ref
):
    here = lax.axis_index("chord")
    mine = got_ref[here]
    left = got_ref[lax.rem(here + CHORD - 1, CHORD)]
    right = got_ref[lax.rem(here + 1, CHORD)]
    all_cells = got_ref[:, 0:8, :].reshape(CHORD * SLOTS, SENT)
    all_base = got_ref[:, 8:16, :].reshape(CHORD * SLOTS, SENT)
    all_reach = got_ref[:, 16:24, :].reshape(CHORD * SLOTS, SENT)

    slots = jnp.concatenate([mine[0:8], left[0:8], right[0:8]], axis=0)
    partner = slots[:, FLAT : FLAT + 1].astype(jnp.int32)
    line = slots[:, FLAT + 1 : FLAT + 2].astype(jnp.int32)
    pick = (iota((3 * SLOTS, LINES), 1) == partner).astype(f32)
    other = dot_nn(pick, all_cells)
    apart = penalty_weight * (slots - other)
    other_line = other[:SLOTS, FLAT + 1 : FLAT + 2].astype(jnp.int32)
    other_device = partner[:SLOTS] // SLOTS
    other_base = dot_nn(pick[:SLOTS], all_base)

    device = jnp.concatenate([jnp.full((SLOTS, 1), here, jnp.int32), other_device], axis=0)
    at = jnp.concatenate([line[:SLOTS], other_line], axis=0)
    before = lax.rem(device + CHORD - 1, CHORD) * SLOTS + NEAR + at
    after = lax.rem(device + 1, CHORD) * SLOTS + at - (LINES - NEAR)
    source = jnp.where(at < NEAR, before, jnp.where(at >= LINES - NEAR, after, -1))
    added = dot_nn((iota((2 * SLOTS, LINES), 1) == source).astype(f32), all_reach)

    spot = iota((LINES, SENT), 0) - (LINES - ROWS)
    row_at = iota((LINES, SENT), 1) // COLS - NEAR
    inner = ((spot == row_at) & (spot >= 0)).astype(f32)
    rim_row = jnp.where(spot < NEAR, spot - NEAR, spot + ROWS - NEAR)
    rim = ((rim_row == row_at) & (spot >= 0) & (spot < 2 * NEAR)).astype(f32)
    row8 = iota((SLOTS, SENT), 0)
    halo_base = jnp.where(row8 < 3, left[24:32], right[24:32])
    halo_rim = jnp.where(row8 < 3, left[16:24], right[16:24])
    scales = dot_nn(
        jnp.concatenate([mine[8:16], other_base, halo_base], axis=0)[:, SENT - LINES :], inner
    )
    slot_scale = scales[: 2 * SLOTS]
    halo_scale = scales[2 * SLOTS :] + dot_nn(halo_rim[:, SENT - LINES :], rim)

    own_w = mine[8:16] + slot_scale[:SLOTS] * added[:SLOTS] + apart[:SLOTS]
    other_w = other_base + slot_scale[SLOTS:] * added[SLOTS:] - apart[:SLOTS]
    apart_w = penalty_weight * (own_w - other_w)

    target = iota((2 * SLOTS, SLOTS), 1)
    from_left = iota((2 * SLOTS, SLOTS), 0) < SLOTS
    chosen = (edge_line(target) == line[SLOTS:]) & ((target < 3) == from_left)
    halo_apart = dot_tn(chosen.astype(f32), apart[SLOTS:])
    halo_w = halo_base + halo_scale * mine[16:24] + halo_apart
    halo_v = jnp.where(row8 < 6, halo_scale * halo_w, 0.0)

    lane = iota((SLOTS, LINES), 1)
    low8 = iota((SLOTS, LINES), 0)
    at_slot = (lane == line[:SLOTS]).astype(f32)
    at_edge = (lane == edge_line(low8)).astype(f32)
    none = jnp.zeros((SLOTS, LINES), f32)
    arrived = jnp.where(row8 < 3, right[16:24], left[16:24])
    first = dot_tn(
        jnp.concatenate([apart[:SLOTS], arrived], axis=0),
        jnp.concatenate(
            [
                jnp.concatenate([at_slot, none], axis=1),
                jnp.concatenate([none, at_edge], axis=1),
            ],
            axis=0,
        ),
    )
    distance = jnp.abs(outer_line(low8) - lane)
    second = dot_tn(
        jnp.concatenate([halo_v, apart_w], axis=0),
        jnp.concatenate(
            [
                jnp.concatenate(
                    [taps_at(distance, mass_taps), taps_at(distance, bend_taps), none], axis=1
                ),
                jnp.concatenate([none, none, at_slot], axis=1),
            ],
            axis=0,
        ),
    )
    scale = [scale_ref[NEAR + k : NEAR + k + 1, :] for k in range(WIDE)]
    images, masses, bends = [], [], []
    for row in range(WIDE):
        cut = slice(row * COLS, (row + 1) * COLS)
        scale_row = spread(scale[row])
        image = base_ref[cut, :] + first[cut, :LINES] + scale_row * first[cut, LINES:]
        value = scale_row * image
        mass, bend = mass_taps[0] * value, bend_taps[0] * value
        for step in range(1, 4):
            pair = pair_of(value, step)
            mass = mass + mass_taps[step] * pair
            if bend_taps[step] != 0.0:
                bend = bend + bend_taps[step] * pair
        images.append(image)
        masses.append(mass + second[cut, :LINES])
        bends.append(bend + second[cut, LINES : 2 * LINES])
    seconds = []
    for row in range(ROWS):
        at_row = row + NEAR
        cut = slice(at_row * COLS, (at_row + 1) * COLS)
        total = row_stencil(masses, at_row, bend_taps) + row_stencil(bends, at_row, mass_taps)
        product = (
            spread(scale[at_row]) * total
            + spread(d_ref[row : row + 1, :]) * images[at_row]
            + second[cut, 2 * LINES :]
        )
        w_ref[pl.ds(row * COLS, COLS), :] = images[at_row]
        z_ref[pl.ds(row * COLS, COLS), :] = product
        seconds.append(product)
    r = jnp.concatenate([field_ref[pl.ds(k * COLS, COLS), :] for k in range(ROWS)], axis=1)
    w = jnp.concatenate(images[NEAR : NEAR + ROWS], axis=1)
    z = jnp.concatenate(seconds, axis=1)
    gram = jnp.concatenate(
        [
            dot_nt(r, jnp.concatenate([r, w], axis=0)),
            dot_nt(w, jnp.concatenate([w, z], axis=0)),
        ],
        axis=1,
    )
    gram = jnp.concatenate([gram[:8], gram[8:]], axis=1)
    for device in range(gram_ref.shape[0]):
        gram_ref[device] = gram


def total_kernel(parts_ref, out_ref):
    total = jnp.sum(parts_ref[...], axis=0)
    for device in range(out_ref.shape[0]):
        out_ref[device] = total


def spd_solve(matrix, right):
    size, width = matrix.shape[0], right.shape[1]
    blank = jnp.zeros((size, LINES - size - width), f32)
    work = jnp.concatenate([matrix, right, blank], axis=1)
    row = iota((size, LINES), 0)
    for start in range(0, size, PANEL):
        columns = [
            jnp.broadcast_to(work[:, start + k : start + k + 1], (size, LINES))
            for k in range(PANEL)
        ]
        for k in range(PANEL):
            at = start + k
            column = columns[k]
            scale = 1.0 / column[at : at + 1, :]

            def eliminate(block):
                pivot_row = block[at : at + 1, :] * scale
                return jnp.where(row == at, pivot_row, block - column * pivot_row)

            work = eliminate(work)
            columns = [eliminate(block) if j > k else block for j, block in enumerate(columns)]
    return work[:, size : size + width]


def finish_kernel(parts_ref, field_ref, w_ref, z_ref, x_ref, res_ref):
    packed = jnp.sum(parts_ref[...], axis=0)
    gram = jnp.concatenate([packed[:, : 4 * COLS], packed[:, 4 * COLS :]], axis=0)
    g00, g01 = gram[:, :COLS], gram[:, COLS : 2 * COLS]
    g11, g12 = gram[:, 2 * COLS : 3 * COLS], gram[:, 3 * COLS :]
    coeffs = spd_solve(
        jnp.concatenate(
            [
                jnp.concatenate([g01, g11], axis=1),
                jnp.concatenate([g11, g12], axis=1),
            ],
            axis=0,
        ),
        jnp.concatenate([g00, g01], axis=0),
    )
    r = jnp.concatenate([field_ref[pl.ds(k * COLS, COLS), :] for k in range(ROWS)], axis=1)
    w = jnp.concatenate([w_ref[pl.ds(k * COLS, COLS), :] for k in range(ROWS)], axis=1)
    z = jnp.concatenate([z_ref[pl.ds(k * COLS, COLS), :] for k in range(ROWS)], axis=1)
    x = dot_tn(coeffs, jnp.concatenate([r, w], axis=0))
    res = r - dot_tn(coeffs, jnp.concatenate([w, z], axis=0))
    for row in range(ROWS):
        cut = slice(row * LINES, (row + 1) * LINES)
        x_ref[pl.ds(row, COLS, stride=ROWS), :] = x[:, cut]
        res_ref[pl.ds(row, COLS, stride=ROWS), :] = res[:, cut]


def call(kernel, shapes, hbm=False, scratch=()):
    def run(*args):
        if hbm and not INTERPRET:
            args = [pltpu.with_memory_space_constraint(arg, pltpu.HBM) for arg in args]
        return pl.pallas_call(
            kernel,
            out_shape=[
                jax.ShapeDtypeStruct(shape, kind) for shape, kind in map(typed, shapes)
            ],
            in_specs=[pl.BlockSpec(memory_space=pltpu.HBM if hbm else pltpu.VMEM)] * len(args),
            out_specs=[pl.BlockSpec(memory_space=pltpu.VMEM)] * len(shapes),
            scratch_shapes=scratch,
            interpret=INTERPRET,
            compiler_params=pltpu.CompilerParams(vmem_limit_bytes=KERNEL_BYTES),
        )(*args)

    return run


def typed(shape):
    return shape if isinstance(shape[0], tuple) else (shape, f32)


def body(right_side, stiff_scale, extra_diag, iface_line, partner):
    span = lax.axis_size(SPAN)
    plane = lax.axis_size(("core", "chord"))
    depth = lax.axis_size("z")
    cells = right_side.reshape(COLS * ROWS, LINES)
    halo = (DEEP * COLS + 16, LINES)
    flat = (ROWS * COLS, LINES)
    one = (ROWS, LINES)
    field, far, near, scale, extra, slots = call(
        pack_kernel,
        [flat, halo, halo, one, one, ((2, SLOTS, LINES), jnp.int32)],
        hbm=True,
        scratch=[
            pltpu.VMEM(flat, f32),
            pltpu.SMEM((SLOTS,), jnp.int32),
            pltpu.SMEM((SLOTS,), jnp.int32),
            pltpu.SemaphoreType.DMA((5,)),
        ],
    )(iface_line, partner, cells, stiff_scale, extra_diag)
    swaps = [(i, i + 1) for i in range(1, span - 1, 2)]
    far = lax.ppermute(far, SPAN, swaps + [(b, a) for a, b in swaps])
    swaps = [(i, i + 1) for i in range(0, span, 2)]
    near = lax.ppermute(near, SPAN, swaps + [(b, a) for a, b in swaps])
    base, scale, message = call(
        send_kernel, [(FLAT, LINES), (ROWS + 2 * DEEP, LINES), (CHORD, SPARE, SENT)]
    )(field, scale, extra, far, near, slots)
    got = lax.all_to_all(message, "chord", 0, 0)
    w, z, gram = call(apply_kernel, [flat, flat, (plane, 8, LINES)])(
        got, field, base, scale, extra
    )
    gram = lax.all_to_all(gram, ("core", "chord"), 0, 0)
    (gram,) = call(total_kernel, [(depth, 8, LINES)])(gram)
    gram = lax.all_to_all(gram, "z", 0, 0)
    x, res = call(finish_kernel, [flat, flat])(gram, field, w, z)
    return (x.reshape(COLS, ROWS, LINES), res.reshape(COLS, ROWS, LINES))


def solution(mesh):
    chord = mesh.devices.shape[1]
    fine = Mesh(mesh.devices.reshape(-1, 2, chord), ("z", "core", "chord"))
    return jax.shard_map(
        body,
        mesh=fine,
        in_specs=(
            P(None, SPAN, "chord"),
            P(SPAN, "chord"),
            P(SPAN, "chord"),
            P("chord"),
            P("chord"),
        ),
        out_specs=(P(None, SPAN, "chord"), P(None, SPAN, "chord")),
        check_vma=False,
    )
```

```python
import jax
import jax.numpy as jnp
from jax import lax
from jax.experimental import pallas as pl
from jax.experimental.pallas import tpu as pltpu
from jax.sharding import Mesh
from jax.sharding import PartitionSpec as P

SPAN = ("z", "core")
COLS = 16
ROWS = 32
LINES = 128
SLOTS = 8
CHORD = 16
DEEP = 6
NEAR = 3
WIDE = ROWS + 2 * NEAR
FLAT = WIDE * COLS
INNER = ROWS * COLS
SENT = 640
PARTNER_LANE = 104
LINE_LANE = 105
PANEL = 16
SPARE = 128

mass_taps = (2416.0 / 5040.0, 1191.0 / 5040.0, 120.0 / 5040.0, 1.0 / 5040.0)
bend_taps = (8.0 / 3.0, -1.5, 0.0, 1.0 / 6.0)
penalty_weight = 4.0

f32 = jnp.float32
KERNEL_BYTES = 24 << 20
INTERPRET = False


def dot(left, right, contract):
    return lax.dot_general(
        left,
        right,
        (contract, ((), ())),
        precision=lax.Precision.HIGHEST,
        preferred_element_type=f32,
    )


def dot_nn(left, right):
    return dot(left, right, ((1,), (0,)))


def dot_nt(left, right):
    return dot(left, right, ((1,), (1,)))


def dot_tn(left, right):
    return dot(left, right, ((0,), (0,)))


def iota(shape, dim):
    return lax.broadcasted_iota(jnp.int32, shape, dim)


def taps_at(distance, taps):
    value = jnp.zeros(distance.shape, f32)
    for step in range(4):
        if taps[step] != 0.0:
            value = jnp.where(distance == step, taps[step], value)
    return value


def outer_line(row):
    return jnp.where(row < 3, row - 3, jnp.where(row < 6, row + LINES - 3, 4 * LINES))


def edge_line(row):
    return jnp.where(row < 3, row + LINES - 3, jnp.where(row < 6, row - 3, 4 * LINES))


def pair_of(field, step):
    lane = iota((COLS, LINES), 1)
    ahead = jnp.where(lane < LINES - step, pltpu.roll(field, LINES - step, 1), 0.0)
    behind = jnp.where(lane >= step, pltpu.roll(field, step, 1), 0.0)
    return ahead + behind


def row_stencil(rows, at, taps):
    total = taps[0] * rows[at]
    for step in range(1, 4):
        if taps[step] != 0.0:
            total = total + taps[step] * (rows[at - step] + rows[at + step])
    return total


def spread(row):
    return jnp.broadcast_to(row, (COLS, LINES))


def pack_kernel(
    line_hbm, partner_hbm, r_hbm, s_hbm, d_hbm,
    field_ref, far_ref, near_ref, s_ref, d_ref, slots_ref,
    r_ref, line_ref, partner_ref, sems
):
    copies = [
        pltpu.make_async_copy(source, target, sems.at[k])
        for k, (source, target) in enumerate(
            [
                (r_hbm, r_ref),
                (s_hbm, s_ref),
                (d_hbm, d_ref),
                (line_hbm, line_ref),
                (partner_hbm, partner_ref),
            ]
        )
    ]
    for copy in copies:
        copy.start()
    for copy in copies:
        copy.wait()
    first_core = lax.axis_index("core") == 0
    rows = []
    for row in range(ROWS):
        cells = r_ref[pl.ds(row, COLS, stride=ROWS), :]
        field_ref[pl.ds(row * COLS, COLS), :] = cells
        rows.append(cells)
    pad = jnp.zeros((2, LINES), f32)
    low, high = slice(0, DEEP), slice(ROWS - DEEP, ROWS)
    ends = [
        jnp.concatenate(rows[cut] + [s_ref[cut, :], pad, d_ref[cut, :], pad], axis=0)
        for cut in (low, high)
    ]
    far_ref[...] = jnp.where(first_core, ends[0], ends[1])
    near_ref[...] = jnp.where(first_core, ends[1], ends[0])
    row = iota((SLOTS, LINES), 0)
    for k, scalars in enumerate((line_ref, partner_ref)):
        value = jnp.zeros((SLOTS, LINES), jnp.int32)
        for slot in range(SLOTS):
            value = jnp.where(row == slot, scalars[slot], value)
        slots_ref[k] = value


def send_kernel(
    field_ref, s_ref, d_ref, far_ref, near_ref, slots_ref, base_ref, scale_ref, message_ref
):
    first_core = lax.axis_index("core") == 0
    below = jnp.where(first_core, far_ref[...], near_ref[...])
    above = jnp.where(first_core, near_ref[...], far_ref[...])
    start = DEEP * COLS
    scale_ref[0:DEEP, :] = below[start : start + DEEP]
    scale_ref[DEEP : DEEP + ROWS, :] = s_ref[...]
    scale_ref[DEEP + ROWS : 2 * DEEP + ROWS, :] = above[start : start + DEEP]
    scale = [below[start + k : start + k + 1] for k in range(DEEP)]
    scale += [s_ref[k : k + 1, :] for k in range(ROWS)]
    scale += [above[start + k : start + k + 1] for k in range(DEEP)]
    start += 8
    extra = [below[start + k : start + k + 1] for k in range(DEEP - NEAR, DEEP)]
    extra += [d_ref[k : k + 1, :] for k in range(ROWS)]
    extra += [above[start + k : start + k + 1] for k in range(NEAR)]
    cells = [below[k * COLS : (k + 1) * COLS] for k in range(DEEP)]
    cells += [field_ref[pl.ds(k * COLS, COLS), :] for k in range(ROWS)]
    cells += [above[k * COLS : (k + 1) * COLS] for k in range(DEEP)]
    weighted = [spread(scale[k]) * cells[k] for k in range(ROWS + 2 * DEEP)]
    masses, bends, bases = [], [], []
    for row in range(WIDE):
        mass = row_stencil(weighted, row + NEAR, mass_taps)
        bend = row_stencil(weighted, row + NEAR, bend_taps)
        total = mass_taps[0] * bend + bend_taps[0] * mass
        for step in range(1, 4):
            mixed = mass_taps[step] * bend
            if bend_taps[step] != 0.0:
                mixed = mixed + bend_taps[step] * mass
            total = total + pair_of(mixed, step)
        base = spread(scale[row + NEAR]) * total + spread(extra[row]) * cells[row + NEAR]
        masses.append(mass)
        bends.append(bend)
        bases.append(base)
        base_ref[pl.ds(row * COLS, COLS), :] = base
    blank = jnp.zeros((SENT - FLAT, LINES), f32)
    own_scale = jnp.concatenate([jnp.zeros((FLAT, LINES), f32), s_ref[...]], axis=0)
    rim = [scale[NEAR + k] for k in (0, 1, 2, WIDE - 3, WIDE - 2, WIDE - 1)]
    rim_scale = jnp.concatenate(
        [jnp.zeros((FLAT, LINES), f32)] + rim + [jnp.zeros((SENT - FLAT - 6, LINES), f32)], axis=0
    )
    lane = iota((SLOTS, LINES), 1)
    row8 = iota((SLOTS, LINES), 0)
    at_slot = (lane == slots_ref[0]).astype(f32)
    at_edge = (lane == edge_line(row8)).astype(f32)
    other_edge = (
        ((lane == row8 + 1) & (row8 < 2)) | ((lane == row8 + LINES - 9) & (row8 >= 6))
    ).astype(f32)
    sent_cells = dot_nt(
        jnp.concatenate([at_slot, at_edge], axis=1),
        jnp.concatenate([stack(cells[NEAR : NEAR + WIDE], blank), own_scale], axis=1),
    )
    sent_base = dot_nt(jnp.concatenate([at_slot, other_edge], axis=0), stack(bases, blank))
    distance = jnp.abs(outer_line(row8) - lane)
    reach = jnp.concatenate(
        [taps_at(distance, mass_taps), taps_at(distance, bend_taps), at_edge], axis=1
    )
    sent_reach = dot_nt(
        reach, jnp.concatenate([stack(bends, blank), stack(masses, blank), rim_scale], axis=1)
    )
    slot_base, edge_base = sent_base[:SLOTS], sent_base[SLOTS:]
    wide_row = iota((SLOTS, SENT), 0)
    wide_lane = iota((SLOTS, SENT), 1)
    third = jnp.where((wide_row < 6) | (wide_lane >= FLAT), sent_reach, edge_base)
    last = third[:, INNER:]
    last = jnp.where(lane == PARTNER_LANE, slots_ref[1].astype(f32), last)
    last = jnp.where(lane == LINE_LANE, slots_ref[0].astype(f32), last)

    def piece(block, at):
        return block[:, at * LINES : (at + 1) * LINES]

    def moved(block, at, shift):
        return pltpu.roll(piece(block, at), shift, 0)

    parts = []
    for at in range(4):
        parts += [piece(sent_cells, at), piece(slot_base, at), piece(third, at)]
    parts += [sent_cells[:, INNER:], last]
    parts += [
        jnp.where(
            row8 < 4,
            jnp.where(row8 < 2, piece(slot_base, 4), moved(edge_base, 4, 2)),
            jnp.where(row8 < 6, moved(edge_base, 0, 4), moved(edge_base, 1, 6)),
        ),
        jnp.where(row8 < 2, piece(edge_base, 2), moved(edge_base, 3, 2)),
    ]
    message = jnp.concatenate(parts, axis=0)
    for device in range(CHORD):
        message_ref[device] = message


def stack(rows, blank):
    return jnp.concatenate(rows[NEAR:-NEAR] + rows[:NEAR] + rows[-NEAR:] + [blank], axis=0)


def cut_of(row):
    place = row if 0 <= row < ROWS else ROWS + NEAR + row if row < 0 else NEAR + row
    return slice(place * COLS, (place + 1) * COLS)


def rim_spread():
    spot = iota((LINES, LINES), 0) - (FLAT - INNER)
    return ((spot == iota((LINES, LINES), 1) // COLS) & (spot < 2 * NEAR)).astype(f32)


def apply_kernel(
    got_ref, field_ref, base_ref, scale_ref, d_ref, w_ref, z_ref, gram_ref
):
    here = lax.axis_index("chord")
    devices = [here, lax.rem(here + CHORD - 1, CHORD), lax.rem(here + 1, CHORD)]
    mine, left, right = [got_ref[device] for device in devices]

    def group(block, first, tail):
        tiles = [block[first + 24 * k : first + 24 * k + 8] for k in range(4)]
        return jnp.concatenate(tiles + [block[tail : tail + 8]], axis=1)

    def everyone(at):
        return got_ref[:, at : at + 8, :].reshape(CHORD * SLOTS, LINES)

    all_cells = jnp.concatenate([everyone(at) for at in (0, 24, 48, 72, 96)], axis=1)
    all_base = jnp.concatenate([everyone(at) for at in (8, 32, 56, 80)], axis=1)
    all_reach = jnp.concatenate([everyone(at) for at in (16, 40, 64, 88)], axis=1)

    slots = jnp.concatenate([group(block, 0, 96) for block in (mine, left, right)], axis=0)
    numbers = jnp.concatenate([block[104:112] for block in (mine, left, right)], axis=0)
    partner = numbers[:, PARTNER_LANE : PARTNER_LANE + 1].astype(jnp.int32)
    line = numbers[:, LINE_LANE : LINE_LANE + 1].astype(jnp.int32)
    pick = (iota((3 * SLOTS, LINES), 1) == partner).astype(f32)
    other = dot_nn(pick, all_cells)
    apart = penalty_weight * (slots - other)
    other_numbers = dot_nn(pick[:SLOTS], everyone(104))
    other_line = other_numbers[:, LINE_LANE : LINE_LANE + 1].astype(jnp.int32)
    other_device = partner[:SLOTS] // SLOTS
    other_base = dot_nn(pick[:SLOTS], all_base)

    device = jnp.concatenate([jnp.full((SLOTS, 1), here, jnp.int32), other_device], axis=0)
    at = jnp.concatenate([line[:SLOTS], other_line], axis=0)
    before = lax.rem(device + CHORD - 1, CHORD) * SLOTS + NEAR + at
    after = lax.rem(device + 1, CHORD) * SLOTS + at - (LINES - NEAR)
    is_low, is_high = at < NEAR, at >= LINES - NEAR
    source = jnp.where(is_low, before, jnp.where(is_high, after, -1))
    added = dot_nn((iota((2 * SLOTS, LINES), 1) == source).astype(f32), all_reach)
    edge = device * SLOTS + jnp.where(is_low, at + NEAR, at - (LINES - NEAR))
    edge = jnp.where(is_low | is_high, edge, -1)
    spare = dot_nn((iota((2 * SLOTS, LINES), 1) == edge).astype(f32), everyone(96))

    low8 = iota((SLOTS, LINES), 0)
    row8 = iota((SLOTS, SENT), 0)
    halo_spare = jnp.where(low8 < 3, left[96:104], right[96:104])
    halo_rim = jnp.where(low8 < 3, left[104:112], right[104:112])
    inner = (
        iota((LINES, INNER), 0) == iota((LINES, INNER), 1) // COLS + (FLAT - INNER)
    ).astype(f32)
    scales = dot_nn(jnp.concatenate([spare, halo_spare], axis=0), inner)
    slot_scale = scales[: 2 * SLOTS]
    halo_scale = jnp.concatenate(
        [scales[2 * SLOTS :], dot_nn(halo_rim, rim_spread())], axis=1
    )
    reach = group(mine, 16, 104)
    arrived = jnp.where(row8 < 3, group(right, 16, 104), group(left, 16, 104))

    from_base = group(left, 8, 112)
    to_base = group(right, 8, 112)
    halo_base = jnp.where(
        row8 < 3,
        jnp.where(row8 < 2, pltpu.roll(group(left, 16, 104), 2, 0), pltpu.roll(from_base, 1, 0)),
        jnp.where(
            row8 < 4,
            pltpu.roll(to_base, 3, 0),
            jnp.concatenate(
                [
                    right[112:120],
                    pltpu.roll(right[112:120], 6, 0),
                    pltpu.roll(right[120:128], 4, 0),
                    pltpu.roll(right[120:128], 2, 0),
                    pltpu.roll(right[112:120], 2, 0),
                ],
                axis=1,
            ),
        ),
    )

    slot_base = group(mine, 8, 112)[:, :INNER]
    near = apart[:SLOTS, :INNER]
    own_w = slot_base + slot_scale[:SLOTS] * added[:SLOTS] + near
    other_w = other_base + slot_scale[SLOTS:] * added[SLOTS:] - near
    apart_w = penalty_weight * (own_w - other_w)
    apart_w = jnp.concatenate([apart_w, jnp.zeros((SLOTS, SENT - INNER), f32)], axis=1)

    target = iota((2 * SLOTS, SLOTS), 1)
    from_left = iota((2 * SLOTS, SLOTS), 0) < SLOTS
    chosen = (edge_line(target) == line[SLOTS:]) & ((target < 3) == from_left)
    halo_apart = dot_tn(chosen.astype(f32), apart[SLOTS:])
    halo_w = halo_base + halo_scale * reach + halo_apart
    halo_v = jnp.where(row8 < 6, halo_scale * halo_w, 0.0)

    lane = iota((SLOTS, LINES), 1)
    at_slot = (lane == line[:SLOTS]).astype(f32)
    at_edge = (lane == edge_line(low8)).astype(f32)
    none = jnp.zeros((SLOTS, LINES), f32)
    first = dot_tn(
        jnp.concatenate([apart[:SLOTS], arrived], axis=0),
        jnp.concatenate(
            [
                jnp.concatenate([at_slot, none], axis=1),
                jnp.concatenate([none, at_edge], axis=1),
            ],
            axis=0,
        ),
    )
    distance = jnp.abs(outer_line(low8) - lane)
    second = dot_tn(
        jnp.concatenate([halo_v, apart_w], axis=0),
        jnp.concatenate(
            [
                jnp.concatenate(
                    [taps_at(distance, mass_taps), taps_at(distance, bend_taps), none], axis=1
                ),
                jnp.concatenate([none, none, at_slot], axis=1),
            ],
            axis=0,
        ),
    )
    scale = [scale_ref[NEAR + k : NEAR + k + 1, :] for k in range(WIDE)]
    images, masses, bends = [], [], []
    for row in range(WIDE):
        cut = cut_of(row - NEAR)
        scale_row = spread(scale[row])
        image = base_ref[pl.ds(row * COLS, COLS), :] + first[cut, :LINES] + scale_row * first[cut, LINES:]
        value = scale_row * image
        mass, bend = mass_taps[0] * value, bend_taps[0] * value
        for step in range(1, 4):
            pair = pair_of(value, step)
            mass = mass + mass_taps[step] * pair
            if bend_taps[step] != 0.0:
                bend = bend + bend_taps[step] * pair
        images.append(image)
        masses.append(mass + second[cut, :LINES])
        bends.append(bend + second[cut, LINES : 2 * LINES])
    seconds = []
    for row in range(ROWS):
        at_row = row + NEAR
        cut = cut_of(row)
        total = row_stencil(masses, at_row, bend_taps) + row_stencil(bends, at_row, mass_taps)
        product = (
            spread(scale[at_row]) * total
            + spread(d_ref[row : row + 1, :]) * images[at_row]
            + second[cut, 2 * LINES :]
        )
        w_ref[pl.ds(row * COLS, COLS), :] = images[at_row]
        z_ref[pl.ds(row * COLS, COLS), :] = product
        seconds.append(product)
    r = jnp.concatenate([field_ref[pl.ds(k * COLS, COLS), :] for k in range(ROWS)], axis=1)
    w = jnp.concatenate(images[NEAR : NEAR + ROWS], axis=1)
    z = jnp.concatenate(seconds, axis=1)
    gram = jnp.concatenate(
        [
            dot_nt(r, jnp.concatenate([r, w], axis=0)),
            dot_nt(w, jnp.concatenate([w, z], axis=0)),
        ],
        axis=1,
    )
    gram = jnp.concatenate([gram[:8], gram[8:]], axis=1)
    for device in range(gram_ref.shape[0]):
        gram_ref[device] = gram


def total_kernel(parts_ref, out_ref):
    total = jnp.sum(parts_ref[...], axis=0)
    for device in range(out_ref.shape[0]):
        out_ref[device] = total


def spd_solve(matrix, right):
    size, width = matrix.shape[0], right.shape[1]
    blank = jnp.zeros((size, LINES - size - width), f32)
    work = jnp.concatenate([matrix, right, blank], axis=1)
    row = iota((size, LINES), 0)
    for start in range(0, size, PANEL):
        columns = [
            jnp.broadcast_to(work[:, start + k : start + k + 1], (size, LINES))
            for k in range(PANEL)
        ]
        for k in range(PANEL):
            at = start + k
            column = columns[k]
            scale = 1.0 / column[at : at + 1, :]

            def eliminate(block):
                pivot_row = block[at : at + 1, :] * scale
                return jnp.where(row == at, pivot_row, block - column * pivot_row)

            work = eliminate(work)
            columns = [eliminate(block) if j > k else block for j, block in enumerate(columns)]
    return work[:, size : size + width]


def finish_kernel(parts_ref, field_ref, w_ref, z_ref, x_ref, res_ref):
    packed = jnp.sum(parts_ref[...], axis=0)
    gram = jnp.concatenate([packed[:, : 4 * COLS], packed[:, 4 * COLS :]], axis=0)
    g00, g01 = gram[:, :COLS], gram[:, COLS : 2 * COLS]
    g11, g12 = gram[:, 2 * COLS : 3 * COLS], gram[:, 3 * COLS :]
    coeffs = spd_solve(
        jnp.concatenate(
            [
                jnp.concatenate([g01, g11], axis=1),
                jnp.concatenate([g11, g12], axis=1),
            ],
            axis=0,
        ),
        jnp.concatenate([g00, g01], axis=0),
    )
    r = jnp.concatenate([field_ref[pl.ds(k * COLS, COLS), :] for k in range(ROWS)], axis=1)
    w = jnp.concatenate([w_ref[pl.ds(k * COLS, COLS), :] for k in range(ROWS)], axis=1)
    z = jnp.concatenate([z_ref[pl.ds(k * COLS, COLS), :] for k in range(ROWS)], axis=1)
    x = dot_tn(coeffs, jnp.concatenate([r, w], axis=0))
    res = r - dot_tn(coeffs, jnp.concatenate([w, z], axis=0))
    for row in range(ROWS):
        cut = slice(row * LINES, (row + 1) * LINES)
        x_ref[pl.ds(row, COLS, stride=ROWS), :] = x[:, cut]
        res_ref[pl.ds(row, COLS, stride=ROWS), :] = res[:, cut]


def call(kernel, shapes, hbm=False, scratch=()):
    def run(*args):
        if hbm and not INTERPRET:
            args = [pltpu.with_memory_space_constraint(arg, pltpu.HBM) for arg in args]
        return pl.pallas_call(
            kernel,
            out_shape=[
                jax.ShapeDtypeStruct(shape, kind) for shape, kind in map(typed, shapes)
            ],
            in_specs=[pl.BlockSpec(memory_space=pltpu.HBM if hbm else pltpu.VMEM)] * len(args),
            out_specs=[pl.BlockSpec(memory_space=pltpu.VMEM)] * len(shapes),
            scratch_shapes=scratch,
            interpret=INTERPRET,
            compiler_params=pltpu.CompilerParams(vmem_limit_bytes=KERNEL_BYTES),
        )(*args)

    return run


def typed(shape):
    return shape if isinstance(shape[0], tuple) else (shape, f32)


def body(right_side, stiff_scale, extra_diag, iface_line, partner):
    span = lax.axis_size(SPAN)
    plane = lax.axis_size(("core", "chord"))
    depth = lax.axis_size("z")
    cells = right_side.reshape(COLS * ROWS, LINES)
    halo = (DEEP * COLS + 16, LINES)
    flat = (ROWS * COLS, LINES)
    one = (ROWS, LINES)
    field, far, near, scale, extra, slots = call(
        pack_kernel,
        [flat, halo, halo, one, one, ((2, SLOTS, LINES), jnp.int32)],
        hbm=True,
        scratch=[
            pltpu.VMEM(flat, f32),
            pltpu.SMEM((SLOTS,), jnp.int32),
            pltpu.SMEM((SLOTS,), jnp.int32),
            pltpu.SemaphoreType.DMA((5,)),
        ],
    )(iface_line, partner, cells, stiff_scale, extra_diag)
    swaps = [(i, i + 1) for i in range(1, span - 1, 2)]
    far = lax.ppermute(far, SPAN, swaps + [(b, a) for a, b in swaps])
    swaps = [(i, i + 1) for i in range(0, span, 2)]
    near = lax.ppermute(near, SPAN, swaps + [(b, a) for a, b in swaps])
    base, scale, message = call(
        send_kernel, [(FLAT, LINES), (ROWS + 2 * DEEP, LINES), (CHORD, SPARE, LINES)]
    )(field, scale, extra, far, near, slots)
    got = lax.all_to_all(message, "chord", 0, 0)
    w, z, gram = call(apply_kernel, [flat, flat, (plane, 8, LINES)])(
        got, field, base, scale, extra
    )
    gram = lax.all_to_all(gram, ("core", "chord"), 0, 0)
    (gram,) = call(total_kernel, [(depth, 8, LINES)])(gram)
    gram = lax.all_to_all(gram, "z", 0, 0)
    x, res = call(finish_kernel, [flat, flat])(gram, field, w, z)
    return (x.reshape(COLS, ROWS, LINES), res.reshape(COLS, ROWS, LINES))


def solution(mesh):
    chord = mesh.devices.shape[1]
    fine = Mesh(mesh.devices.reshape(-1, 2, chord), ("z", "core", "chord"))
    return jax.shard_map(
        body,
        mesh=fine,
        in_specs=(
            P(None, SPAN, "chord"),
            P(SPAN, "chord"),
            P(SPAN, "chord"),
            P("chord"),
            P("chord"),
        ),
        out_specs=(P(None, SPAN, "chord"), P(None, SPAN, "chord")),
        check_vma=False,
    )
```

```python
import jax
import jax.numpy as jnp
from jax import lax
from jax.experimental import pallas as pl
from jax.experimental.pallas import tpu as pltpu
from jax.sharding import Mesh
from jax.sharding import PartitionSpec as P

SPAN = ("z", "core")
COLS = 16
ROWS = 32
LINES = 128
SLOTS = 8
CHORD = 16
DEEP = 6
NEAR = 3
WIDE = ROWS + 2 * NEAR
FLAT = WIDE * COLS
INNER = ROWS * COLS
SENT = 640
PARTNER_LANE = 104
LINE_LANE = 105
PANEL = 16
SPARE = 128

mass_taps = (2416.0 / 5040.0, 1191.0 / 5040.0, 120.0 / 5040.0, 1.0 / 5040.0)
bend_taps = (8.0 / 3.0, -1.5, 0.0, 1.0 / 6.0)
penalty_weight = 4.0

f32 = jnp.float32
KERNEL_BYTES = 24 << 20
INTERPRET = False


def one_pass(left, right, contract):
    return lax.dot_general(
        left.astype(jnp.bfloat16),
        right.astype(jnp.bfloat16),
        (contract, ((), ())),
        preferred_element_type=f32,
    )


NN, NT, TN = ((1,), (0,)), ((1,), (1,)), ((0,), (0,))


def parts_of(value, count):
    parts = []
    for _ in range(count):
        parts.append(value.astype(jnp.bfloat16).astype(f32))
        value = value - parts[-1]
    return parts


def select(pick, data, contract):
    (left,), (right,) = contract
    return one_pass(
        jnp.concatenate([pick] * 3, axis=left),
        jnp.concatenate(parts_of(data, 3), axis=right),
        contract,
    )


def mix(left, right, contract, pairs):
    count = 1 + max(max(pair) for pair in pairs)
    lefts, rights = parts_of(left, count), parts_of(right, count)
    return one_pass(
        jnp.concatenate([lefts[a] for a, _ in pairs], axis=contract[0][0]),
        jnp.concatenate([rights[b] for _, b in pairs], axis=contract[1][0]),
        contract,
    )


SIX = ((0, 0), (0, 1), (1, 0), (1, 1), (0, 2), (2, 0))
THREE = ((0, 0), (0, 1), (1, 0))


def iota(shape, dim):
    return lax.broadcasted_iota(jnp.int32, shape, dim)


def taps_at(distance, taps):
    value = jnp.zeros(distance.shape, f32)
    for step in range(4):
        if taps[step] != 0.0:
            value = jnp.where(distance == step, taps[step], value)
    return value


def outer_line(row):
    return jnp.where(row < 3, row - 3, jnp.where(row < 6, row + LINES - 3, 4 * LINES))


def edge_line(row):
    return jnp.where(row < 3, row + LINES - 3, jnp.where(row < 6, row - 3, 4 * LINES))


def pair_of(field, step):
    lane = iota((COLS, LINES), 1)
    ahead = jnp.where(lane < LINES - step, pltpu.roll(field, LINES - step, 1), 0.0)
    behind = jnp.where(lane >= step, pltpu.roll(field, step, 1), 0.0)
    return ahead + behind


def row_stencil(rows, at, taps):
    total = taps[0] * rows[at]
    for step in range(1, 4):
        if taps[step] != 0.0:
            total = total + taps[step] * (rows[at - step] + rows[at + step])
    return total


def spread(row):
    return jnp.broadcast_to(row, (COLS, LINES))


def pack_kernel(
    line_hbm, partner_hbm, r_hbm, s_hbm, d_hbm,
    field_ref, far_ref, near_ref, s_ref, d_ref, slots_ref,
    r_ref, line_ref, partner_ref, sems
):
    copies = [
        pltpu.make_async_copy(source, target, sems.at[k])
        for k, (source, target) in enumerate(
            [
                (r_hbm, r_ref),
                (s_hbm, s_ref),
                (d_hbm, d_ref),
                (line_hbm, line_ref),
                (partner_hbm, partner_ref),
            ]
        )
    ]
    for copy in copies:
        copy.start()
    for copy in copies:
        copy.wait()
    first_core = lax.axis_index("core") == 0
    rows = []
    for row in range(ROWS):
        cells = r_ref[pl.ds(row, COLS, stride=ROWS), :]
        field_ref[pl.ds(row * COLS, COLS), :] = cells
        rows.append(cells)
    pad = jnp.zeros((2, LINES), f32)
    low, high = slice(0, DEEP), slice(ROWS - DEEP, ROWS)
    ends = [
        jnp.concatenate(rows[cut] + [s_ref[cut, :], pad, d_ref[cut, :], pad], axis=0)
        for cut in (low, high)
    ]
    far_ref[...] = jnp.where(first_core, ends[0], ends[1])
    near_ref[...] = jnp.where(first_core, ends[1], ends[0])
    row = iota((SLOTS, LINES), 0)
    for k, scalars in enumerate((line_ref, partner_ref)):
        value = jnp.zeros((SLOTS, LINES), jnp.int32)
        for slot in range(SLOTS):
            value = jnp.where(row == slot, scalars[slot], value)
        slots_ref[k] = value


def send_kernel(
    field_ref, s_ref, d_ref, far_ref, near_ref, slots_ref, base_ref, scale_ref, message_ref
):
    first_core = lax.axis_index("core") == 0
    below = jnp.where(first_core, far_ref[...], near_ref[...])
    above = jnp.where(first_core, near_ref[...], far_ref[...])
    start = DEEP * COLS
    scale_ref[0:DEEP, :] = below[start : start + DEEP]
    scale_ref[DEEP : DEEP + ROWS, :] = s_ref[...]
    scale_ref[DEEP + ROWS : 2 * DEEP + ROWS, :] = above[start : start + DEEP]
    scale = [below[start + k : start + k + 1] for k in range(DEEP)]
    scale += [s_ref[k : k + 1, :] for k in range(ROWS)]
    scale += [above[start + k : start + k + 1] for k in range(DEEP)]
    start += 8
    extra = [below[start + k : start + k + 1] for k in range(DEEP - NEAR, DEEP)]
    extra += [d_ref[k : k + 1, :] for k in range(ROWS)]
    extra += [above[start + k : start + k + 1] for k in range(NEAR)]
    cells = [below[k * COLS : (k + 1) * COLS] for k in range(DEEP)]
    cells += [field_ref[pl.ds(k * COLS, COLS), :] for k in range(ROWS)]
    cells += [above[k * COLS : (k + 1) * COLS] for k in range(DEEP)]
    weighted = [spread(scale[k]) * cells[k] for k in range(ROWS + 2 * DEEP)]
    masses, bends, bases = [], [], []
    for row in range(WIDE):
        mass = row_stencil(weighted, row + NEAR, mass_taps)
        bend = row_stencil(weighted, row + NEAR, bend_taps)
        total = mass_taps[0] * bend + bend_taps[0] * mass
        for step in range(1, 4):
            mixed = mass_taps[step] * bend
            if bend_taps[step] != 0.0:
                mixed = mixed + bend_taps[step] * mass
            total = total + pair_of(mixed, step)
        base = spread(scale[row + NEAR]) * total + spread(extra[row]) * cells[row + NEAR]
        masses.append(mass)
        bends.append(bend)
        bases.append(base)
        base_ref[pl.ds(row * COLS, COLS), :] = base
    blank = jnp.zeros((SENT - FLAT, LINES), f32)
    rim = [scale[NEAR + k] for k in (0, 1, 2, WIDE - 3, WIDE - 2, WIDE - 1)]
    tail = FLAT - INNER
    scales = jnp.concatenate(
        [jnp.zeros((tail, LINES), f32), s_ref[...], jnp.zeros((tail, LINES), f32)]
        + rim
        + [jnp.zeros((LINES - tail - 6, LINES), f32)],
        axis=0,
    )
    lane = iota((SLOTS, LINES), 1)
    row8 = iota((SLOTS, LINES), 0)
    at_slot = (lane == slots_ref[0]).astype(f32)
    at_edge = (lane == edge_line(row8)).astype(f32)
    other_edge = (
        ((lane == row8 + 1) & (row8 < 2)) | ((lane == row8 + LINES - 9) & (row8 >= 6))
    ).astype(f32)
    sent_cells = select(at_slot, stack(cells[NEAR : NEAR + WIDE], blank), NT)
    sent_base = select(
        jnp.concatenate([at_slot, other_edge], axis=0), stack(bases, blank), NT
    )
    sent_scale = select(at_edge, scales, NT)
    distance = jnp.abs(outer_line(row8) - lane)
    reach = jnp.concatenate([taps_at(distance, mass_taps), taps_at(distance, bend_taps)], axis=1)
    sent_reach = mix(
        reach,
        jnp.concatenate([stack(bends, blank), stack(masses, blank)], axis=1),
        NT,
        THREE,
    )
    slot_base, edge_base = sent_base[:SLOTS], sent_base[SLOTS:]
    wide_row = iota((SLOTS, SENT), 0)
    wide_lane = iota((SLOTS, SENT), 1)
    third = jnp.where((wide_row < 6) | (wide_lane >= FLAT), sent_reach, edge_base)
    last = third[:, INNER:] + sent_scale[:, LINES:]
    last = jnp.where(lane == PARTNER_LANE, slots_ref[1].astype(f32), last)
    last = jnp.where(lane == LINE_LANE, slots_ref[0].astype(f32), last)

    def piece(block, at):
        return block[:, at * LINES : (at + 1) * LINES]

    def moved(block, at, shift):
        return pltpu.roll(piece(block, at), shift, 0)

    parts = []
    for at in range(4):
        parts += [piece(sent_cells, at), piece(slot_base, at), piece(third, at)]
    parts += [sent_cells[:, INNER:] + sent_scale[:, :LINES], last]
    parts += [
        jnp.where(
            row8 < 4,
            jnp.where(row8 < 2, piece(slot_base, 4), moved(edge_base, 4, 2)),
            jnp.where(row8 < 6, moved(edge_base, 0, 4), moved(edge_base, 1, 6)),
        ),
        jnp.where(row8 < 2, piece(edge_base, 2), moved(edge_base, 3, 2)),
    ]
    message = jnp.concatenate(parts, axis=0)
    for device in range(CHORD):
        message_ref[device] = message


def stack(rows, blank):
    return jnp.concatenate(rows[NEAR:-NEAR] + rows[:NEAR] + rows[-NEAR:] + [blank], axis=0)


def cut_of(row):
    place = row if 0 <= row < ROWS else ROWS + NEAR + row if row < 0 else NEAR + row
    return slice(place * COLS, (place + 1) * COLS)


def expand(data, pattern):
    rows = data.shape[0]
    product = one_pass(jnp.concatenate(parts_of(data, 3), axis=0), pattern, NN)
    return product[:rows] + product[rows : 2 * rows] + product[2 * rows :]


def spread_lines(data, pattern):
    return one_pass(
        jnp.concatenate(parts_of(data, 3), axis=0), jnp.concatenate([pattern] * 3, axis=0), TN
    )


def rim_spread():
    spot = iota((LINES, LINES), 0) - (FLAT - INNER)
    return ((spot == iota((LINES, LINES), 1) // COLS) & (spot < 2 * NEAR)).astype(f32)


def apply_kernel(
    got_ref, field_ref, base_ref, scale_ref, d_ref, w_ref, z_ref, gram_ref
):
    here = lax.axis_index("chord")
    devices = [here, lax.rem(here + CHORD - 1, CHORD), lax.rem(here + 1, CHORD)]
    mine, left, right = [got_ref[device] for device in devices]

    def group(block, first, tail):
        tiles = [block[first + 24 * k : first + 24 * k + 8] for k in range(4)]
        return jnp.concatenate(tiles + [block[tail : tail + 8]], axis=1)

    def everyone(at):
        return got_ref[:, at : at + 8, :].reshape(CHORD * SLOTS, LINES)

    all_cells = jnp.concatenate([everyone(at) for at in (0, 24, 48, 72, 96)], axis=1)
    all_base = jnp.concatenate([everyone(at) for at in (8, 32, 56, 80)], axis=1)
    all_reach = jnp.concatenate([everyone(at) for at in (16, 40, 64, 88)], axis=1)

    slots = jnp.concatenate([group(block, 0, 96) for block in (mine, left, right)], axis=0)
    numbers = jnp.concatenate([block[104:112] for block in (mine, left, right)], axis=0)
    partner = numbers[:, PARTNER_LANE : PARTNER_LANE + 1].astype(jnp.int32)
    line = numbers[:, LINE_LANE : LINE_LANE + 1].astype(jnp.int32)
    pick = (iota((3 * SLOTS, LINES), 1) == partner).astype(f32)
    other = select(pick, all_cells, NN)
    apart = penalty_weight * (slots - other)
    other_numbers = one_pass(pick[:SLOTS], everyone(104), NN)
    other_line = other_numbers[:, LINE_LANE : LINE_LANE + 1].astype(jnp.int32)
    other_device = partner[:SLOTS] // SLOTS
    other_base = select(pick[:SLOTS], all_base, NN)

    device = jnp.concatenate([jnp.full((SLOTS, 1), here, jnp.int32), other_device], axis=0)
    at = jnp.concatenate([line[:SLOTS], other_line], axis=0)
    before = lax.rem(device + CHORD - 1, CHORD) * SLOTS + NEAR + at
    after = lax.rem(device + 1, CHORD) * SLOTS + at - (LINES - NEAR)
    is_low, is_high = at < NEAR, at >= LINES - NEAR
    source = jnp.where(is_low, before, jnp.where(is_high, after, -1))
    added = select((iota((2 * SLOTS, LINES), 1) == source).astype(f32), all_reach, NN)
    edge = device * SLOTS + jnp.where(is_low, at + NEAR, at - (LINES - NEAR))
    edge = jnp.where(is_low | is_high, edge, -1)
    spare = select((iota((2 * SLOTS, LINES), 1) == edge).astype(f32), everyone(96), NN)

    low8 = iota((SLOTS, LINES), 0)
    row8 = iota((SLOTS, SENT), 0)
    halo_spare = jnp.where(low8 < 3, left[96:104], right[96:104])
    halo_rim = jnp.where(low8 < 3, left[104:112], right[104:112])
    inner = (
        iota((LINES, INNER), 0) == iota((LINES, INNER), 1) // COLS + (FLAT - INNER)
    ).astype(f32)
    scales = expand(jnp.concatenate([spare, halo_spare], axis=0), inner)
    slot_scale = scales[: 2 * SLOTS]
    halo_scale = jnp.concatenate(
        [scales[2 * SLOTS :], expand(halo_rim, rim_spread())], axis=1
    )
    reach = group(mine, 16, 104)
    arrived = jnp.where(row8 < 3, group(right, 16, 104), group(left, 16, 104))

    from_base = group(left, 8, 112)
    to_base = group(right, 8, 112)
    halo_base = jnp.where(
        row8 < 3,
        jnp.where(row8 < 2, pltpu.roll(group(left, 16, 104), 2, 0), pltpu.roll(from_base, 1, 0)),
        jnp.where(
            row8 < 4,
            pltpu.roll(to_base, 3, 0),
            jnp.concatenate(
                [
                    right[112:120],
                    pltpu.roll(right[112:120], 6, 0),
                    pltpu.roll(right[120:128], 4, 0),
                    pltpu.roll(right[120:128], 2, 0),
                    pltpu.roll(right[112:120], 2, 0),
                ],
                axis=1,
            ),
        ),
    )

    slot_base = group(mine, 8, 112)[:, :INNER]
    near = apart[:SLOTS, :INNER]
    own_w = slot_base + slot_scale[:SLOTS] * added[:SLOTS] + near
    other_w = other_base + slot_scale[SLOTS:] * added[SLOTS:] - near
    apart_w = penalty_weight * (own_w - other_w)
    apart_w = jnp.concatenate([apart_w, jnp.zeros((SLOTS, SENT - INNER), f32)], axis=1)

    target = iota((2 * SLOTS, SLOTS), 1)
    from_left = iota((2 * SLOTS, SLOTS), 0) < SLOTS
    chosen = (edge_line(target) == line[SLOTS:]) & ((target < 3) == from_left)
    halo_apart = select(chosen.astype(f32), apart[SLOTS:], TN)
    halo_w = halo_base + halo_scale * reach + halo_apart
    halo_v = jnp.where(row8 < 6, halo_scale * halo_w, 0.0)

    lane = iota((SLOTS, LINES), 1)
    at_slot = (lane == line[:SLOTS]).astype(f32)
    at_edge = (lane == edge_line(low8)).astype(f32)
    none = jnp.zeros((SLOTS, LINES), f32)
    first = spread_lines(
        jnp.concatenate([apart[:SLOTS], arrived], axis=0),
        jnp.concatenate(
            [
                jnp.concatenate([at_slot, none], axis=1),
                jnp.concatenate([none, at_edge], axis=1),
            ],
            axis=0,
        ),
    )
    distance = jnp.abs(outer_line(low8) - lane)
    second = mix(
        jnp.concatenate([halo_v, apart_w], axis=0),
        jnp.concatenate(
            [
                jnp.concatenate(
                    [taps_at(distance, mass_taps), taps_at(distance, bend_taps), none], axis=1
                ),
                jnp.concatenate([none, none, at_slot], axis=1),
            ],
            axis=0,
        ),
        TN,
        SIX,
    )
    scale = [scale_ref[NEAR + k : NEAR + k + 1, :] for k in range(WIDE)]
    images, masses, bends = [], [], []
    for row in range(WIDE):
        cut = cut_of(row - NEAR)
        scale_row = spread(scale[row])
        image = base_ref[pl.ds(row * COLS, COLS), :] + first[cut, :LINES] + scale_row * first[cut, LINES:]
        value = scale_row * image
        mass, bend = mass_taps[0] * value, bend_taps[0] * value
        for step in range(1, 4):
            pair = pair_of(value, step)
            mass = mass + mass_taps[step] * pair
            if bend_taps[step] != 0.0:
                bend = bend + bend_taps[step] * pair
        images.append(image)
        masses.append(mass + second[cut, :LINES])
        bends.append(bend + second[cut, LINES : 2 * LINES])
    seconds = []
    for row in range(ROWS):
        at_row = row + NEAR
        cut = cut_of(row)
        total = row_stencil(masses, at_row, bend_taps) + row_stencil(bends, at_row, mass_taps)
        product = (
            spread(scale[at_row]) * total
            + spread(d_ref[row : row + 1, :]) * images[at_row]
            + second[cut, 2 * LINES :]
        )
        w_ref[pl.ds(row * COLS, COLS), :] = images[at_row]
        z_ref[pl.ds(row * COLS, COLS), :] = product
        seconds.append(product)
    r = jnp.concatenate([field_ref[pl.ds(k * COLS, COLS), :] for k in range(ROWS)], axis=1)
    w = jnp.concatenate(images[NEAR : NEAR + ROWS], axis=1)
    z = jnp.concatenate(seconds, axis=1)
    fields = [part for field in (r, w, z) for part in parts_of(field, 2)]
    blank = jnp.zeros((2 * COLS, ROWS * LINES), f32)
    products = one_pass(
        jnp.concatenate(fields[:4], axis=0), jnp.concatenate(fields + [blank], axis=0), NT
    )
    by_r = products[:COLS] + products[COLS : 2 * COLS]
    by_w = products[2 * COLS : 3 * COLS] + products[3 * COLS :]
    by_r = by_r + pltpu.roll(by_r, LINES - COLS, 1)
    by_w = by_w + pltpu.roll(by_w, LINES - COLS, 1)
    lane16 = iota((COLS, LINES), 1)
    gram = jnp.where(lane16 // COLS % 2 == 0, by_r, pltpu.roll(by_w, LINES - COLS, 1))
    gram = jnp.where(lane < 4 * COLS, gram[:SLOTS], pltpu.roll(gram[SLOTS:], 4 * COLS, 1))
    for device in range(gram_ref.shape[0]):
        gram_ref[device] = gram


def total_kernel(parts_ref, out_ref):
    total = jnp.sum(parts_ref[...], axis=0)
    for device in range(out_ref.shape[0]):
        out_ref[device] = total


def spd_solve(matrix, right):
    size, width = matrix.shape[0], right.shape[1]
    blank = jnp.zeros((size, LINES - size - width), f32)
    work = jnp.concatenate([matrix, right, blank], axis=1)
    row = iota((size, LINES), 0)
    for start in range(0, size, PANEL):
        columns = [
            jnp.broadcast_to(work[:, start + k : start + k + 1], (size, LINES))
            for k in range(PANEL)
        ]
        for k in range(PANEL):
            at = start + k
            column = columns[k]
            scale = 1.0 / column[at : at + 1, :]

            def eliminate(block):
                pivot_row = block[at : at + 1, :] * scale
                return jnp.where(row == at, pivot_row, block - column * pivot_row)

            work = eliminate(work)
            columns = [eliminate(block) if j > k else block for j, block in enumerate(columns)]
    return work[:, size : size + width]


def finish_kernel(parts_ref, field_ref, w_ref, z_ref, x_ref, res_ref):
    packed = jnp.sum(parts_ref[...], axis=0)
    gram = jnp.concatenate([packed[:, : 4 * COLS], packed[:, 4 * COLS :]], axis=0)
    g00, g11 = gram[:, :COLS], gram[:, COLS : 2 * COLS]
    g01, g12 = gram[:, 2 * COLS : 3 * COLS], gram[:, 3 * COLS :]
    coeffs = spd_solve(
        jnp.concatenate(
            [
                jnp.concatenate([g01, g11], axis=1),
                jnp.concatenate([g11, g12], axis=1),
            ],
            axis=0,
        ),
        jnp.concatenate([g00, g01], axis=0),
    )
    r = jnp.concatenate([field_ref[pl.ds(k * COLS, COLS), :] for k in range(ROWS)], axis=1)
    w = jnp.concatenate([w_ref[pl.ds(k * COLS, COLS), :] for k in range(ROWS)], axis=1)
    z = jnp.concatenate([z_ref[pl.ds(k * COLS, COLS), :] for k in range(ROWS)], axis=1)
    none = jnp.zeros((COLS, COLS), f32)
    weights = jnp.concatenate(
        [
            jnp.concatenate([coeffs, none], axis=0),
            jnp.concatenate([none, -coeffs], axis=0),
        ],
        axis=1,
    )
    products = one_pass(
        jnp.concatenate([jnp.concatenate(parts_of(weights, 3), axis=1)] * 3, axis=0),
        jnp.concatenate(parts_of(jnp.concatenate([r, w, z], axis=0), 3), axis=0),
        TN,
    )
    products = products[: 2 * COLS] + products[2 * COLS : 4 * COLS] + products[4 * COLS :]
    x, res = products[:COLS], r + products[COLS:]
    for row in range(ROWS):
        cut = slice(row * LINES, (row + 1) * LINES)
        x_ref[pl.ds(row, COLS, stride=ROWS), :] = x[:, cut]
        res_ref[pl.ds(row, COLS, stride=ROWS), :] = res[:, cut]


def call(kernel, shapes, hbm=False, scratch=()):
    def run(*args):
        if hbm and not INTERPRET:
            args = [pltpu.with_memory_space_constraint(arg, pltpu.HBM) for arg in args]
        return pl.pallas_call(
            kernel,
            out_shape=[
                jax.ShapeDtypeStruct(shape, kind) for shape, kind in map(typed, shapes)
            ],
            in_specs=[pl.BlockSpec(memory_space=pltpu.HBM if hbm else pltpu.VMEM)] * len(args),
            out_specs=[pl.BlockSpec(memory_space=pltpu.VMEM)] * len(shapes),
            scratch_shapes=scratch,
            interpret=INTERPRET,
            compiler_params=pltpu.CompilerParams(vmem_limit_bytes=KERNEL_BYTES),
        )(*args)

    return run


def typed(shape):
    return shape if isinstance(shape[0], tuple) else (shape, f32)


def body(right_side, stiff_scale, extra_diag, iface_line, partner):
    span = lax.axis_size(SPAN)
    plane = lax.axis_size(("core", "chord"))
    depth = lax.axis_size("z")
    cells = right_side.reshape(COLS * ROWS, LINES)
    halo = (DEEP * COLS + 16, LINES)
    flat = (ROWS * COLS, LINES)
    one = (ROWS, LINES)
    field, far, near, scale, extra, slots = call(
        pack_kernel,
        [flat, halo, halo, one, one, ((2, SLOTS, LINES), jnp.int32)],
        hbm=True,
        scratch=[
            pltpu.VMEM(flat, f32),
            pltpu.SMEM((SLOTS,), jnp.int32),
            pltpu.SMEM((SLOTS,), jnp.int32),
            pltpu.SemaphoreType.DMA((5,)),
        ],
    )(iface_line, partner, cells, stiff_scale, extra_diag)
    swaps = [(i, i + 1) for i in range(1, span - 1, 2)]
    far = lax.ppermute(far, SPAN, swaps + [(b, a) for a, b in swaps])
    swaps = [(i, i + 1) for i in range(0, span, 2)]
    near = lax.ppermute(near, SPAN, swaps + [(b, a) for a, b in swaps])
    base, scale, message = call(
        send_kernel, [(FLAT, LINES), (ROWS + 2 * DEEP, LINES), (CHORD, SPARE, LINES)]
    )(field, scale, extra, far, near, slots)
    got = lax.all_to_all(message, "chord", 0, 0)
    w, z, gram = call(apply_kernel, [flat, flat, (plane, 8, LINES)])(
        got, field, base, scale, extra
    )
    gram = lax.all_to_all(gram, ("core", "chord"), 0, 0)
    (gram,) = call(total_kernel, [(depth, 8, LINES)])(gram)
    gram = lax.all_to_all(gram, "z", 0, 0)
    x, res = call(finish_kernel, [flat, flat])(gram, field, w, z)
    return (x.reshape(COLS, ROWS, LINES), res.reshape(COLS, ROWS, LINES))


def solution(mesh):
    chord = mesh.devices.shape[1]
    fine = Mesh(mesh.devices.reshape(-1, 2, chord), ("z", "core", "chord"))
    return jax.shard_map(
        body,
        mesh=fine,
        in_specs=(
            P(None, SPAN, "chord"),
            P(SPAN, "chord"),
            P(SPAN, "chord"),
            P("chord"),
            P("chord"),
        ),
        out_specs=(P(None, SPAN, "chord"), P(None, SPAN, "chord")),
        check_vma=False,
    )
```

```python
import jax
import jax.numpy as jnp
from jax import lax
from jax.experimental import pallas as pl
from jax.experimental.pallas import tpu as pltpu
from jax.sharding import Mesh
from jax.sharding import PartitionSpec as P

SPAN = ("z", "core")
COLS = 16
ROWS = 32
LINES = 128
SLOTS = 8
CHORD = 16
DEEP = 6
NEAR = 3
WIDE = ROWS + 2 * NEAR
FLAT = WIDE * COLS
INNER = ROWS * COLS
SENT = 640
PARTNER_LANE = 104
LINE_LANE = 105
PANEL = 16
SPARE = 128

mass_taps = (2416.0 / 5040.0, 1191.0 / 5040.0, 120.0 / 5040.0, 1.0 / 5040.0)
bend_taps = (8.0 / 3.0, -1.5, 0.0, 1.0 / 6.0)
penalty_weight = 4.0

f32 = jnp.float32
KERNEL_BYTES = 24 << 20
INTERPRET = False


def one_pass(left, right, contract):
    return lax.dot_general(
        left.astype(jnp.bfloat16),
        right.astype(jnp.bfloat16),
        (contract, ((), ())),
        preferred_element_type=f32,
    )


NN, NT, TN = ((1,), (0,)), ((1,), (1,)), ((0,), (0,))


def parts_of(value, count):
    parts = []
    for _ in range(count):
        parts.append(value.astype(jnp.bfloat16).astype(f32))
        value = value - parts[-1]
    return parts


def select(pick, data, contract):
    (left,), (right,) = contract
    return one_pass(
        jnp.concatenate([pick] * 3, axis=left),
        jnp.concatenate(parts_of(data, 3), axis=right),
        contract,
    )


def mix(left, right, contract, pairs):
    count = 1 + max(max(pair) for pair in pairs)
    lefts, rights = parts_of(left, count), parts_of(right, count)
    return one_pass(
        jnp.concatenate([lefts[a] for a, _ in pairs], axis=contract[0][0]),
        jnp.concatenate([rights[b] for _, b in pairs], axis=contract[1][0]),
        contract,
    )


SIX = ((0, 0), (0, 1), (1, 0), (1, 1), (0, 2), (2, 0))
THREE = ((0, 0), (0, 1), (1, 0))


def iota(shape, dim):
    return lax.broadcasted_iota(jnp.int32, shape, dim)


def taps_at(distance, taps):
    value = jnp.zeros(distance.shape, f32)
    for step in range(4):
        if taps[step] != 0.0:
            value = jnp.where(distance == step, taps[step], value)
    return value


def outer_line(row):
    return jnp.where(row < 3, row - 3, jnp.where(row < 6, row + LINES - 3, 4 * LINES))


def edge_line(row):
    return jnp.where(row < 3, row + LINES - 3, jnp.where(row < 6, row - 3, 4 * LINES))


def pair_of(field, step):
    lane = iota((COLS, LINES), 1)
    ahead = jnp.where(lane < LINES - step, pltpu.roll(field, LINES - step, 1), 0.0)
    behind = jnp.where(lane >= step, pltpu.roll(field, step, 1), 0.0)
    return ahead + behind


def row_stencil(rows, at, taps):
    total = taps[0] * rows[at]
    for step in range(1, 4):
        if taps[step] != 0.0:
            total = total + taps[step] * (rows[at - step] + rows[at + step])
    return total


def spread(row):
    return jnp.broadcast_to(row, (COLS, LINES))


def pack_kernel(
    line_hbm, partner_hbm, r_hbm, s_hbm, d_hbm,
    field_ref, far_ref, near_ref, s_ref, d_ref, slots_ref,
    r_ref, line_ref, partner_ref, sems
):
    copies = [
        pltpu.make_async_copy(source, target, sems.at[k])
        for k, (source, target) in enumerate(
            [
                (r_hbm, r_ref),
                (s_hbm, s_ref),
                (d_hbm, d_ref),
                (line_hbm, line_ref),
                (partner_hbm, partner_ref),
            ]
        )
    ]
    for copy in copies:
        copy.start()
    for copy in copies:
        copy.wait()
    first_core = lax.axis_index("core") == 0
    rows = []
    for row in range(ROWS):
        cells = r_ref[pl.ds(row, COLS, stride=ROWS), :]
        field_ref[pl.ds(row * COLS, COLS), :] = cells
        rows.append(cells)
    pad = jnp.zeros((2, LINES), f32)
    low, high = slice(0, DEEP), slice(ROWS - DEEP, ROWS)
    ends = [
        jnp.concatenate(rows[cut] + [s_ref[cut, :], pad, d_ref[cut, :], pad], axis=0)
        for cut in (low, high)
    ]
    far_ref[...] = jnp.where(first_core, ends[0], ends[1])
    near_ref[...] = jnp.where(first_core, ends[1], ends[0])
    row = iota((SLOTS, LINES), 0)
    for k, scalars in enumerate((line_ref, partner_ref)):
        value = jnp.zeros((SLOTS, LINES), jnp.int32)
        for slot in range(SLOTS):
            value = jnp.where(row == slot, scalars[slot], value)
        slots_ref[k] = value


def send_kernel(
    field_ref, s_ref, d_ref, far_ref, near_ref, slots_ref, base_ref, scale_ref, message_ref
):
    first_core = lax.axis_index("core") == 0
    below = jnp.where(first_core, far_ref[...], near_ref[...])
    above = jnp.where(first_core, near_ref[...], far_ref[...])
    start = DEEP * COLS
    scale_ref[0:DEEP, :] = below[start : start + DEEP]
    scale_ref[DEEP : DEEP + ROWS, :] = s_ref[...]
    scale_ref[DEEP + ROWS : 2 * DEEP + ROWS, :] = above[start : start + DEEP]
    scale = [below[start + k : start + k + 1] for k in range(DEEP)]
    scale += [s_ref[k : k + 1, :] for k in range(ROWS)]
    scale += [above[start + k : start + k + 1] for k in range(DEEP)]
    start += 8
    extra = [below[start + k : start + k + 1] for k in range(DEEP - NEAR, DEEP)]
    extra += [d_ref[k : k + 1, :] for k in range(ROWS)]
    extra += [above[start + k : start + k + 1] for k in range(NEAR)]
    cells = [below[k * COLS : (k + 1) * COLS] for k in range(DEEP)]
    cells += [field_ref[pl.ds(k * COLS, COLS), :] for k in range(ROWS)]
    cells += [above[k * COLS : (k + 1) * COLS] for k in range(DEEP)]
    weighted = [spread(scale[k]) * cells[k] for k in range(ROWS + 2 * DEEP)]
    masses, bends, bases = [], [], []
    for row in range(WIDE):
        mass = row_stencil(weighted, row + NEAR, mass_taps)
        bend = row_stencil(weighted, row + NEAR, bend_taps)
        total = mass_taps[0] * bend + bend_taps[0] * mass
        for step in range(1, 4):
            mixed = mass_taps[step] * bend
            if bend_taps[step] != 0.0:
                mixed = mixed + bend_taps[step] * mass
            total = total + pair_of(mixed, step)
        base = spread(scale[row + NEAR]) * total + spread(extra[row]) * cells[row + NEAR]
        masses.append(mass)
        bends.append(bend)
        bases.append(base)
        base_ref[pl.ds(row * COLS, COLS), :] = base
    blank = jnp.zeros((SENT - FLAT, LINES), f32)
    rim = [scale[NEAR + k] for k in (0, 1, 2, WIDE - 3, WIDE - 2, WIDE - 1)]
    tail = FLAT - INNER
    scales = jnp.concatenate(
        [jnp.zeros((tail, LINES), f32), s_ref[...], jnp.zeros((tail, LINES), f32)]
        + rim
        + [jnp.zeros((LINES - tail - 6, LINES), f32)],
        axis=0,
    )
    lane = iota((SLOTS, LINES), 1)
    row8 = iota((SLOTS, LINES), 0)
    at_slot = (lane == slots_ref[0]).astype(f32)
    at_edge = (lane == edge_line(row8)).astype(f32)
    other_edge = (
        ((lane == row8 + 1) & (row8 < 2)) | ((lane == row8 + LINES - 9) & (row8 >= 6))
    ).astype(f32)
    sent_cells = select(at_slot, stack(cells[NEAR : NEAR + WIDE], blank), NT)
    sent_base = select(
        jnp.concatenate([at_slot, other_edge], axis=0), stack(bases, blank), NT
    )
    sent_scale = select(at_edge, scales, NT)
    distance = jnp.abs(outer_line(row8) - lane)
    reach = jnp.concatenate([taps_at(distance, mass_taps), taps_at(distance, bend_taps)], axis=1)
    sent_reach = mix(
        reach,
        jnp.concatenate([stack(bends, blank), stack(masses, blank)], axis=1),
        NT,
        THREE,
    )
    slot_base, edge_base = sent_base[:SLOTS], sent_base[SLOTS:]
    wide_row = iota((SLOTS, SENT), 0)
    wide_lane = iota((SLOTS, SENT), 1)
    third = jnp.where((wide_row < 6) | (wide_lane >= FLAT), sent_reach, edge_base)
    last = third[:, INNER:] + sent_scale[:, LINES:]
    last = jnp.where(lane == PARTNER_LANE, slots_ref[1].astype(f32), last)
    last = jnp.where(lane == LINE_LANE, slots_ref[0].astype(f32), last)

    def piece(block, at):
        return block[:, at * LINES : (at + 1) * LINES]

    def moved(block, at, shift):
        return pltpu.roll(piece(block, at), shift, 0)

    parts = []
    for at in range(4):
        parts += [piece(sent_cells, at), piece(slot_base, at), piece(third, at)]
    parts += [sent_cells[:, INNER:] + sent_scale[:, :LINES], last]
    parts += [
        jnp.where(
            row8 < 4,
            jnp.where(row8 < 2, piece(slot_base, 4), moved(edge_base, 4, 2)),
            jnp.where(row8 < 6, moved(edge_base, 0, 4), moved(edge_base, 1, 6)),
        ),
        jnp.where(row8 < 2, piece(edge_base, 2), moved(edge_base, 3, 2)),
    ]
    message = jnp.concatenate(parts, axis=0)
    for device in range(CHORD):
        message_ref[device] = message


def stack(rows, blank):
    return jnp.concatenate(rows[NEAR:-NEAR] + rows[:NEAR] + rows[-NEAR:] + [blank], axis=0)


def cut_of(row):
    place = row if 0 <= row < ROWS else ROWS + NEAR + row if row < 0 else NEAR + row
    return slice(place * COLS, (place + 1) * COLS)


def expand(data, pattern):
    rows = data.shape[0]
    product = one_pass(jnp.concatenate(parts_of(data, 3), axis=0), pattern, NN)
    return product[:rows] + product[rows : 2 * rows] + product[2 * rows :]


def spread_lines(data, pattern):
    return one_pass(
        jnp.concatenate(parts_of(data, 3), axis=0), jnp.concatenate([pattern] * 3, axis=0), TN
    )


def rim_spread():
    spot = iota((LINES, LINES), 0) - (FLAT - INNER)
    return ((spot == iota((LINES, LINES), 1) // COLS) & (spot < 2 * NEAR)).astype(f32)


def apply_kernel(
    got_ref, field_ref, base_ref, scale_ref, d_ref, w_ref, z_ref, gram_ref
):
    here = lax.axis_index("chord")
    devices = [here, lax.rem(here + CHORD - 1, CHORD), lax.rem(here + 1, CHORD)]
    mine, left, right = [got_ref[device] for device in devices]

    def group(block, first, tail):
        tiles = [block[first + 24 * k : first + 24 * k + 8] for k in range(4)]
        return jnp.concatenate(tiles + [block[tail : tail + 8]], axis=1)

    def everyone(at):
        return got_ref[:, at : at + 8, :].reshape(CHORD * SLOTS, LINES)

    all_cells = jnp.concatenate([everyone(at) for at in (0, 24, 48, 72, 96)], axis=1)
    all_base = jnp.concatenate([everyone(at) for at in (8, 32, 56, 80)], axis=1)
    all_reach = jnp.concatenate([everyone(at) for at in (16, 40, 64, 88)], axis=1)

    slots = jnp.concatenate([group(block, 0, 96) for block in (mine, left, right)], axis=0)
    numbers = jnp.concatenate([block[104:112] for block in (mine, left, right)], axis=0)
    partner = numbers[:, PARTNER_LANE : PARTNER_LANE + 1].astype(jnp.int32)
    line = numbers[:, LINE_LANE : LINE_LANE + 1].astype(jnp.int32)
    pick = (iota((3 * SLOTS, LINES), 1) == partner).astype(f32)
    other = select(pick, all_cells, NN)
    apart = penalty_weight * (slots - other)
    other_numbers = one_pass(pick[:SLOTS], everyone(104), NN)
    other_line = other_numbers[:, LINE_LANE : LINE_LANE + 1].astype(jnp.int32)
    other_device = partner[:SLOTS] // SLOTS
    other_base = select(pick[:SLOTS], all_base, NN)

    device = jnp.concatenate([jnp.full((SLOTS, 1), here, jnp.int32), other_device], axis=0)
    at = jnp.concatenate([line[:SLOTS], other_line], axis=0)
    before = lax.rem(device + CHORD - 1, CHORD) * SLOTS + NEAR + at
    after = lax.rem(device + 1, CHORD) * SLOTS + at - (LINES - NEAR)
    is_low, is_high = at < NEAR, at >= LINES - NEAR
    source = jnp.where(is_low, before, jnp.where(is_high, after, -1))
    added = select((iota((2 * SLOTS, LINES), 1) == source).astype(f32), all_reach, NN)
    edge = device * SLOTS + jnp.where(is_low, at + NEAR, at - (LINES - NEAR))
    edge = jnp.where(is_low | is_high, edge, -1)
    spare = select((iota((2 * SLOTS, LINES), 1) == edge).astype(f32), everyone(96), NN)

    low8 = iota((SLOTS, LINES), 0)
    row8 = iota((SLOTS, SENT), 0)
    halo_spare = jnp.where(low8 < 3, left[96:104], right[96:104])
    halo_rim = jnp.where(low8 < 3, left[104:112], right[104:112])
    inner = (
        iota((LINES, INNER), 0) == iota((LINES, INNER), 1) // COLS + (FLAT - INNER)
    ).astype(f32)
    scales = expand(jnp.concatenate([spare, halo_spare], axis=0), inner)
    slot_scale = scales[: 2 * SLOTS]
    halo_scale = jnp.concatenate(
        [scales[2 * SLOTS :], expand(halo_rim, rim_spread())], axis=1
    )
    reach = group(mine, 16, 104)
    arrived = jnp.where(row8 < 3, group(right, 16, 104), group(left, 16, 104))

    from_base = group(left, 8, 112)
    to_base = group(right, 8, 112)
    halo_base = jnp.where(
        row8 < 3,
        jnp.where(row8 < 2, pltpu.roll(group(left, 16, 104), 2, 0), pltpu.roll(from_base, 1, 0)),
        jnp.where(
            row8 < 4,
            pltpu.roll(to_base, 3, 0),
            jnp.concatenate(
                [
                    right[112:120],
                    pltpu.roll(right[112:120], 6, 0),
                    pltpu.roll(right[120:128], 4, 0),
                    pltpu.roll(right[120:128], 2, 0),
                    pltpu.roll(right[112:120], 2, 0),
                ],
                axis=1,
            ),
        ),
    )

    slot_base = group(mine, 8, 112)[:, :INNER]
    near = apart[:SLOTS, :INNER]
    own_w = slot_base + slot_scale[:SLOTS] * added[:SLOTS] + near
    other_w = other_base + slot_scale[SLOTS:] * added[SLOTS:] - near
    apart_w = penalty_weight * (own_w - other_w)
    apart_w = jnp.concatenate([apart_w, jnp.zeros((SLOTS, SENT - INNER), f32)], axis=1)

    target = iota((2 * SLOTS, SLOTS), 1)
    from_left = iota((2 * SLOTS, SLOTS), 0) < SLOTS
    chosen = (edge_line(target) == line[SLOTS:]) & ((target < 3) == from_left)
    halo_apart = select(chosen.astype(f32), apart[SLOTS:], TN)
    halo_w = halo_base + halo_scale * reach + halo_apart
    halo_v = jnp.where(row8 < 6, halo_scale * halo_w, 0.0)

    lane = iota((SLOTS, LINES), 1)
    at_slot = (lane == line[:SLOTS]).astype(f32)
    at_edge = (lane == edge_line(low8)).astype(f32)
    none = jnp.zeros((SLOTS, LINES), f32)
    first = spread_lines(
        jnp.concatenate([apart[:SLOTS], arrived], axis=0),
        jnp.concatenate(
            [
                jnp.concatenate([at_slot, none], axis=1),
                jnp.concatenate([none, at_edge], axis=1),
            ],
            axis=0,
        ),
    )
    distance = jnp.abs(outer_line(low8) - lane)
    second = mix(
        jnp.concatenate([halo_v, apart_w], axis=0),
        jnp.concatenate(
            [
                jnp.concatenate(
                    [taps_at(distance, mass_taps), taps_at(distance, bend_taps), none], axis=1
                ),
                jnp.concatenate([none, none, at_slot], axis=1),
            ],
            axis=0,
        ),
        TN,
        SIX,
    )
    scale = [scale_ref[NEAR + k : NEAR + k + 1, :] for k in range(WIDE)]
    images, masses, bends = [], [], []
    for row in range(WIDE):
        cut = cut_of(row - NEAR)
        scale_row = spread(scale[row])
        image = base_ref[pl.ds(row * COLS, COLS), :] + first[cut, :LINES] + scale_row * first[cut, LINES:]
        value = scale_row * image
        mass, bend = mass_taps[0] * value, bend_taps[0] * value
        for step in range(1, 4):
            pair = pair_of(value, step)
            mass = mass + mass_taps[step] * pair
            if bend_taps[step] != 0.0:
                bend = bend + bend_taps[step] * pair
        images.append(image)
        masses.append(mass + second[cut, :LINES])
        bends.append(bend + second[cut, LINES : 2 * LINES])
    seconds = []
    for row in range(ROWS):
        at_row = row + NEAR
        cut = cut_of(row)
        total = row_stencil(masses, at_row, bend_taps) + row_stencil(bends, at_row, mass_taps)
        product = (
            spread(scale[at_row]) * total
            + spread(d_ref[row : row + 1, :]) * images[at_row]
            + second[cut, 2 * LINES :]
        )
        w_ref[pl.ds(row * COLS, COLS), :] = images[at_row]
        z_ref[pl.ds(row * COLS, COLS), :] = product
        seconds.append(product)
    r = jnp.concatenate([field_ref[pl.ds(k * COLS, COLS), :] for k in range(ROWS)], axis=1)
    w = jnp.concatenate(images[NEAR : NEAR + ROWS], axis=1)
    z = jnp.concatenate(seconds, axis=1)
    fields = [part for field in (r, w, z) for part in parts_of(field, 2)]
    blank = jnp.zeros((2 * COLS, ROWS * LINES), f32)
    products = one_pass(
        jnp.concatenate(fields[:4], axis=0), jnp.concatenate(fields + [blank], axis=0), NT
    )
    by_r = products[:COLS] + products[COLS : 2 * COLS]
    by_w = products[2 * COLS : 3 * COLS] + products[3 * COLS :]
    by_r = by_r + pltpu.roll(by_r, LINES - COLS, 1)
    by_w = by_w + pltpu.roll(by_w, LINES - COLS, 1)
    lane16 = iota((COLS, LINES), 1)
    gram = jnp.where(lane16 // COLS % 2 == 0, by_r, pltpu.roll(by_w, LINES - COLS, 1))
    gram = jnp.where(lane < 4 * COLS, gram[:SLOTS], pltpu.roll(gram[SLOTS:], 4 * COLS, 1))
    for device in range(gram_ref.shape[0]):
        gram_ref[device] = gram


def total_kernel(parts_ref, out_ref):
    total = jnp.sum(parts_ref[...], axis=0)
    for device in range(out_ref.shape[0]):
        out_ref[device] = total


def spd_solve(matrix, right):
    size, width = matrix.shape[0], right.shape[1]
    blank = jnp.zeros((size, LINES - size - width), f32)
    work = jnp.concatenate([matrix, right, blank], axis=1)
    row = iota((size, LINES), 0)
    for start in range(0, size, PANEL):
        columns = [
            jnp.broadcast_to(work[:, start + k : start + k + 1], (size, LINES))
            for k in range(PANEL)
        ]
        for k in range(PANEL):
            at = start + k
            column = columns[k]
            scale = 1.0 / column[at : at + 1, :]

            def eliminate(block):
                pivot_row = block[at : at + 1, :] * scale
                return jnp.where(row == at, pivot_row, block - column * pivot_row)

            work = eliminate(work)
            columns = [eliminate(block) if j > k else block for j, block in enumerate(columns)]
    return work[:, size : size + width]


def finish_kernel(parts_ref, field_ref, w_ref, z_ref, x_ref, res_ref):
    packed = jnp.sum(parts_ref[...], axis=0)
    gram = jnp.concatenate([packed[:, : 4 * COLS], packed[:, 4 * COLS :]], axis=0)
    g00, g11 = gram[:, :COLS], gram[:, COLS : 2 * COLS]
    g01, g12 = gram[:, 2 * COLS : 3 * COLS], gram[:, 3 * COLS :]
    coeffs = spd_solve(
        jnp.concatenate(
            [
                jnp.concatenate([g01, g11], axis=1),
                jnp.concatenate([g11, g12], axis=1),
            ],
            axis=0,
        ),
        jnp.concatenate([g00, g01], axis=0),
    )
    r = jnp.concatenate([field_ref[pl.ds(k * COLS, COLS), :] for k in range(ROWS)], axis=1)
    w = jnp.concatenate([w_ref[pl.ds(k * COLS, COLS), :] for k in range(ROWS)], axis=1)
    z = jnp.concatenate([z_ref[pl.ds(k * COLS, COLS), :] for k in range(ROWS)], axis=1)
    none = jnp.zeros((COLS, COLS), f32)
    weights = jnp.concatenate(
        [
            jnp.concatenate([coeffs, none], axis=0),
            jnp.concatenate([none, -coeffs], axis=0),
        ],
        axis=1,
    )
    products = one_pass(
        jnp.concatenate([jnp.concatenate(parts_of(weights, 3), axis=1)] * 3, axis=0),
        jnp.concatenate(parts_of(jnp.concatenate([r, w, z], axis=0), 3), axis=0),
        TN,
    )
    products = products[: 2 * COLS] + products[2 * COLS : 4 * COLS] + products[4 * COLS :]
    x, res = products[:COLS], r + products[COLS:]
    for row in range(ROWS):
        cut = slice(row * LINES, (row + 1) * LINES)
        x_ref[pl.ds(row, COLS, stride=ROWS), :] = x[:, cut]
        res_ref[pl.ds(row, COLS, stride=ROWS), :] = res[:, cut]


def call(kernel, shapes, hbm=False, scratch=()):
    def run(*args):
        if hbm and not INTERPRET:
            args = [pltpu.with_memory_space_constraint(arg, pltpu.HBM) for arg in args]
        return pl.pallas_call(
            kernel,
            out_shape=[
                jax.ShapeDtypeStruct(shape, kind) for shape, kind in map(typed, shapes)
            ],
            in_specs=[pl.BlockSpec(memory_space=pltpu.HBM if hbm else pltpu.VMEM)] * len(args),
            out_specs=[pl.BlockSpec(memory_space=pltpu.VMEM)] * len(shapes),
            scratch_shapes=scratch,
            interpret=INTERPRET,
            compiler_params=pltpu.CompilerParams(vmem_limit_bytes=KERNEL_BYTES),
        )(*args)

    return run


def typed(shape):
    return shape if isinstance(shape[0], tuple) else (shape, f32)


def body(right_side, stiff_scale, extra_diag, iface_line, partner):
    span = lax.axis_size(SPAN)
    plane = lax.axis_size(("core", "chord"))
    depth = lax.axis_size("z")
    cells = right_side.reshape(COLS * ROWS, LINES)
    halo = (DEEP * COLS + 16, LINES)
    flat = (ROWS * COLS, LINES)
    one = (ROWS, LINES)
    field, far, near, scale, extra, slots = call(
        pack_kernel,
        [flat, halo, halo, one, one, ((2, SLOTS, LINES), jnp.int32)],
        hbm=True,
        scratch=[
            pltpu.VMEM(flat, f32),
            pltpu.SMEM((SLOTS,), jnp.int32),
            pltpu.SMEM((SLOTS,), jnp.int32),
            pltpu.SemaphoreType.DMA((5,)),
        ],
    )(iface_line, partner, cells, stiff_scale, extra_diag)
    swaps = [(i, i + 1) for i in range(1, span - 1, 2)]
    far = lax.ppermute(far, SPAN, swaps + [(b, a) for a, b in swaps])
    swaps = [(i, i + 1) for i in range(0, span, 2)]
    near = lax.ppermute(near, SPAN, swaps + [(b, a) for a, b in swaps])
    base, scale, message = call(
        send_kernel, [(FLAT, LINES), (ROWS + 2 * DEEP, LINES), (CHORD, SPARE, LINES)]
    )(field, scale, extra, far, near, slots)
    got = lax.all_to_all(message, "chord", 0, 0)
    w, z, gram = call(apply_kernel, [flat, flat, (depth, 8, LINES)])(
        got, field, base, scale, extra
    )
    gram = lax.all_to_all(gram, "z", 0, 0)
    (gram,) = call(total_kernel, [(plane, 8, LINES)])(gram)
    gram = lax.all_to_all(gram, ("core", "chord"), 0, 0)
    x, res = call(finish_kernel, [flat, flat])(gram, field, w, z)
    return (x.reshape(COLS, ROWS, LINES), res.reshape(COLS, ROWS, LINES))


def solution(mesh):
    chord = mesh.devices.shape[1]
    fine = Mesh(mesh.devices.reshape(-1, 2, chord), ("z", "core", "chord"))
    return jax.shard_map(
        body,
        mesh=fine,
        in_specs=(
            P(None, SPAN, "chord"),
            P(SPAN, "chord"),
            P(SPAN, "chord"),
            P("chord"),
            P("chord"),
        ),
        out_specs=(P(None, SPAN, "chord"), P(None, SPAN, "chord")),
        check_vma=False,
    )
```

```python
import jax
import jax.numpy as jnp
from jax import lax
from jax.experimental import pallas as pl
from jax.experimental.pallas import tpu as pltpu
from jax.sharding import Mesh
from jax.sharding import PartitionSpec as P

SPAN = ("z", "core")
COLS = 16
ROWS = 32
LINES = 128
SLOTS = 8
CHORD = 16
DEEP = 6
NEAR = 3
WIDE = ROWS + 2 * NEAR
FLAT = WIDE * COLS
INNER = ROWS * COLS
SENT = 640
PARTNER_LANE = 104
LINE_LANE = 105
PANEL = 16
SPARE = 128

mass_taps = (2416.0 / 5040.0, 1191.0 / 5040.0, 120.0 / 5040.0, 1.0 / 5040.0)
bend_taps = (8.0 / 3.0, -1.5, 0.0, 1.0 / 6.0)
penalty_weight = 4.0

f32 = jnp.float32
KERNEL_BYTES = 24 << 20
INTERPRET = False


def one_pass(left, right, contract):
    return lax.dot_general(
        left.astype(jnp.bfloat16),
        right.astype(jnp.bfloat16),
        (contract, ((), ())),
        preferred_element_type=f32,
    )


NN, NT, TN = ((1,), (0,)), ((1,), (1,)), ((0,), (0,))


def parts_of(value, count):
    parts = []
    for _ in range(count):
        parts.append(value.astype(jnp.bfloat16).astype(f32))
        value = value - parts[-1]
    return parts


def select(pick, data, contract):
    (left,), (right,) = contract
    return one_pass(
        jnp.concatenate([pick] * 3, axis=left),
        jnp.concatenate(parts_of(data, 3), axis=right),
        contract,
    )


def mix(left, right, contract, pairs):
    count = 1 + max(max(pair) for pair in pairs)
    lefts, rights = parts_of(left, count), parts_of(right, count)
    return one_pass(
        jnp.concatenate([lefts[a] for a, _ in pairs], axis=contract[0][0]),
        jnp.concatenate([rights[b] for _, b in pairs], axis=contract[1][0]),
        contract,
    )


SIX = ((0, 0), (0, 1), (1, 0), (1, 1), (0, 2), (2, 0))
THREE = ((0, 0), (0, 1), (1, 0))


def iota(shape, dim):
    return lax.broadcasted_iota(jnp.int32, shape, dim)


def taps_at(distance, taps):
    value = jnp.zeros(distance.shape, f32)
    for step in range(4):
        if taps[step] != 0.0:
            value = jnp.where(distance == step, taps[step], value)
    return value


def outer_line(row):
    return jnp.where(row < 3, row - 3, jnp.where(row < 6, row + LINES - 3, 4 * LINES))


def edge_line(row):
    return jnp.where(row < 3, row + LINES - 3, jnp.where(row < 6, row - 3, 4 * LINES))


def pair_of(field, step):
    lane = iota((COLS, LINES), 1)
    ahead = jnp.where(lane < LINES - step, pltpu.roll(field, LINES - step, 1), 0.0)
    behind = jnp.where(lane >= step, pltpu.roll(field, step, 1), 0.0)
    return ahead + behind


def row_stencil(rows, at, taps):
    total = taps[0] * rows[at]
    for step in range(1, 4):
        if taps[step] != 0.0:
            total = total + taps[step] * (rows[at - step] + rows[at + step])
    return total


def spread(row):
    return jnp.broadcast_to(row, (COLS, LINES))


def pack_kernel(
    line_hbm, partner_hbm, r_hbm, s_hbm, d_hbm,
    field_ref, far_ref, near_ref, s_ref, d_ref, slots_ref,
    r_ref, line_ref, partner_ref, sems
):
    copies = [
        pltpu.make_async_copy(source, target, sems.at[k])
        for k, (source, target) in enumerate(
            [
                (r_hbm, r_ref),
                (s_hbm, s_ref),
                (d_hbm, d_ref),
                (line_hbm, line_ref),
                (partner_hbm, partner_ref),
            ]
        )
    ]
    for copy in copies:
        copy.start()
    for copy in copies:
        copy.wait()
    first_core = lax.axis_index("core") == 0
    rows = []
    for row in range(ROWS):
        cells = r_ref[pl.ds(row, COLS, stride=ROWS), :]
        field_ref[pl.ds(row * COLS, COLS), :] = cells
        rows.append(cells)
    pad = jnp.zeros((2, LINES), f32)
    low, high = slice(0, DEEP), slice(ROWS - DEEP, ROWS)
    ends = [
        jnp.concatenate(rows[cut] + [s_ref[cut, :], pad, d_ref[cut, :], pad], axis=0)
        for cut in (low, high)
    ]
    far_ref[...] = jnp.where(first_core, ends[0], ends[1])
    near_ref[...] = jnp.where(first_core, ends[1], ends[0])
    row = iota((SLOTS, LINES), 0)
    for k, scalars in enumerate((line_ref, partner_ref)):
        value = jnp.zeros((SLOTS, LINES), jnp.int32)
        for slot in range(SLOTS):
            value = jnp.where(row == slot, scalars[slot], value)
        slots_ref[k] = value


def send_kernel(
    field_ref, s_ref, d_ref, far_ref, near_ref, slots_ref, base_ref, scale_ref, message_ref
):
    first_core = lax.axis_index("core") == 0
    below = jnp.where(first_core, far_ref[...], near_ref[...])
    above = jnp.where(first_core, near_ref[...], far_ref[...])
    start = DEEP * COLS
    scale_ref[0:DEEP, :] = below[start : start + DEEP]
    scale_ref[DEEP : DEEP + ROWS, :] = s_ref[...]
    scale_ref[DEEP + ROWS : 2 * DEEP + ROWS, :] = above[start : start + DEEP]
    scale = [below[start + k : start + k + 1] for k in range(DEEP)]
    scale += [s_ref[k : k + 1, :] for k in range(ROWS)]
    scale += [above[start + k : start + k + 1] for k in range(DEEP)]
    start += 8
    extra = [below[start + k : start + k + 1] for k in range(DEEP - NEAR, DEEP)]
    extra += [d_ref[k : k + 1, :] for k in range(ROWS)]
    extra += [above[start + k : start + k + 1] for k in range(NEAR)]
    cells = [below[k * COLS : (k + 1) * COLS] for k in range(DEEP)]
    cells += [field_ref[pl.ds(k * COLS, COLS), :] for k in range(ROWS)]
    cells += [above[k * COLS : (k + 1) * COLS] for k in range(DEEP)]
    weighted = [spread(scale[k]) * cells[k] for k in range(ROWS + 2 * DEEP)]
    masses, bends, bases = [], [], []
    for row in range(WIDE):
        mass = row_stencil(weighted, row + NEAR, mass_taps)
        bend = row_stencil(weighted, row + NEAR, bend_taps)
        total = mass_taps[0] * bend + bend_taps[0] * mass
        for step in range(1, 4):
            mixed = mass_taps[step] * bend
            if bend_taps[step] != 0.0:
                mixed = mixed + bend_taps[step] * mass
            total = total + pair_of(mixed, step)
        base = spread(scale[row + NEAR]) * total + spread(extra[row]) * cells[row + NEAR]
        masses.append(mass)
        bends.append(bend)
        bases.append(base)
        base_ref[pl.ds(row * COLS, COLS), :] = base
    blank = jnp.zeros((SENT - FLAT, LINES), f32)
    rim = [scale[NEAR + k] for k in (0, 1, 2, WIDE - 3, WIDE - 2, WIDE - 1)]
    tail = FLAT - INNER
    scales = jnp.concatenate(
        [jnp.zeros((tail, LINES), f32), s_ref[...], jnp.zeros((tail, LINES), f32)]
        + rim
        + [jnp.zeros((LINES - tail - 6, LINES), f32)],
        axis=0,
    )
    lane = iota((SLOTS, LINES), 1)
    row8 = iota((SLOTS, LINES), 0)
    at_slot = (lane == slots_ref[0]).astype(f32)
    at_edge = (lane == edge_line(row8)).astype(f32)
    other_edge = (
        ((lane == row8 + 1) & (row8 < 2)) | ((lane == row8 + LINES - 9) & (row8 >= 6))
    ).astype(f32)
    sent_cells = select(at_slot, stack(cells[NEAR : NEAR + WIDE], blank), NT)
    sent_base = select(
        jnp.concatenate([at_slot, other_edge], axis=0), stack(bases, blank), NT
    )
    sent_scale = select(at_edge, scales, NT)
    distance = jnp.abs(outer_line(row8) - lane)
    reach = jnp.concatenate([taps_at(distance, mass_taps), taps_at(distance, bend_taps)], axis=1)
    sent_reach = mix(
        reach,
        jnp.concatenate([stack(bends, blank), stack(masses, blank)], axis=1),
        NT,
        THREE,
    )
    slot_base, edge_base = sent_base[:SLOTS], sent_base[SLOTS:]
    wide_row = iota((SLOTS, SENT), 0)
    wide_lane = iota((SLOTS, SENT), 1)
    third = jnp.where((wide_row < 6) | (wide_lane >= FLAT), sent_reach, edge_base)
    last = third[:, INNER:] + sent_scale[:, LINES:]
    last = jnp.where(lane == PARTNER_LANE, slots_ref[1].astype(f32), last)
    last = jnp.where(lane == LINE_LANE, slots_ref[0].astype(f32), last)

    def piece(block, at):
        return block[:, at * LINES : (at + 1) * LINES]

    def moved(block, at, shift):
        return pltpu.roll(piece(block, at), shift, 0)

    parts = []
    for at in range(4):
        parts += [piece(sent_cells, at), piece(slot_base, at), piece(third, at)]
    parts += [sent_cells[:, INNER:] + sent_scale[:, :LINES], last]
    parts += [
        jnp.where(
            row8 < 4,
            jnp.where(row8 < 2, piece(slot_base, 4), moved(edge_base, 4, 2)),
            jnp.where(row8 < 6, moved(edge_base, 0, 4), moved(edge_base, 1, 6)),
        ),
        jnp.where(row8 < 2, piece(edge_base, 2), moved(edge_base, 3, 2)),
    ]
    message = jnp.concatenate(parts, axis=0)
    for device in range(CHORD):
        message_ref[device] = message


def stack(rows, blank):
    return jnp.concatenate(rows[NEAR:-NEAR] + rows[:NEAR] + rows[-NEAR:] + [blank], axis=0)


def cut_of(row):
    place = row if 0 <= row < ROWS else ROWS + NEAR + row if row < 0 else NEAR + row
    return slice(place * COLS, (place + 1) * COLS)


def expand(data, pattern):
    rows = data.shape[0]
    product = one_pass(jnp.concatenate(parts_of(data, 3), axis=0), pattern, NN)
    return product[:rows] + product[rows : 2 * rows] + product[2 * rows :]


def spread_lines(data, pattern):
    return one_pass(
        jnp.concatenate(parts_of(data, 3), axis=0), jnp.concatenate([pattern] * 3, axis=0), TN
    )


def rim_spread():
    spot = iota((LINES, LINES), 0) - (FLAT - INNER)
    return ((spot == iota((LINES, LINES), 1) // COLS) & (spot < 2 * NEAR)).astype(f32)


def apply_kernel(
    got_ref, field_ref, base_ref, scale_ref, d_ref, w_ref, z_ref, gram_ref
):
    here = lax.axis_index("chord")
    devices = [here, lax.rem(here + CHORD - 1, CHORD), lax.rem(here + 1, CHORD)]
    mine, left, right = [got_ref[device] for device in devices]

    def group(block, first, tail):
        tiles = [block[first + 24 * k : first + 24 * k + 8] for k in range(4)]
        return jnp.concatenate(tiles + [block[tail : tail + 8]], axis=1)

    def everyone(at):
        return got_ref[:, at : at + 8, :].reshape(CHORD * SLOTS, LINES)

    all_cells = jnp.concatenate([everyone(at) for at in (0, 24, 48, 72, 96)], axis=1)
    all_base = jnp.concatenate([everyone(at) for at in (8, 32, 56, 80)], axis=1)
    all_reach = jnp.concatenate([everyone(at) for at in (16, 40, 64, 88)], axis=1)

    slots = jnp.concatenate([group(block, 0, 96) for block in (mine, left, right)], axis=0)
    numbers = jnp.concatenate([block[104:112] for block in (mine, left, right)], axis=0)
    partner = numbers[:, PARTNER_LANE : PARTNER_LANE + 1].astype(jnp.int32)
    line = numbers[:, LINE_LANE : LINE_LANE + 1].astype(jnp.int32)
    pick = (iota((3 * SLOTS, LINES), 1) == partner).astype(f32)
    other = select(pick, all_cells, NN)
    apart = penalty_weight * (slots - other)
    other_numbers = one_pass(pick[:SLOTS], everyone(104), NN)
    other_line = other_numbers[:, LINE_LANE : LINE_LANE + 1].astype(jnp.int32)
    other_device = partner[:SLOTS] // SLOTS
    other_base = select(pick[:SLOTS], all_base, NN)

    device = jnp.concatenate([jnp.full((SLOTS, 1), here, jnp.int32), other_device], axis=0)
    at = jnp.concatenate([line[:SLOTS], other_line], axis=0)
    before = lax.rem(device + CHORD - 1, CHORD) * SLOTS + NEAR + at
    after = lax.rem(device + 1, CHORD) * SLOTS + at - (LINES - NEAR)
    is_low, is_high = at < NEAR, at >= LINES - NEAR
    source = jnp.where(is_low, before, jnp.where(is_high, after, -1))
    added = select((iota((2 * SLOTS, LINES), 1) == source).astype(f32), all_reach, NN)
    edge = device * SLOTS + jnp.where(is_low, at + NEAR, at - (LINES - NEAR))
    edge = jnp.where(is_low | is_high, edge, -1)
    spare = select((iota((2 * SLOTS, LINES), 1) == edge).astype(f32), everyone(96), NN)

    low8 = iota((SLOTS, LINES), 0)
    row8 = iota((SLOTS, SENT), 0)
    halo_spare = jnp.where(low8 < 3, left[96:104], right[96:104])
    halo_rim = jnp.where(low8 < 3, left[104:112], right[104:112])
    inner = (
        iota((LINES, INNER), 0) == iota((LINES, INNER), 1) // COLS + (FLAT - INNER)
    ).astype(f32)
    scales = expand(jnp.concatenate([spare, halo_spare], axis=0), inner)
    slot_scale = scales[: 2 * SLOTS]
    halo_scale = jnp.concatenate(
        [scales[2 * SLOTS :], expand(halo_rim, rim_spread())], axis=1
    )
    reach = group(mine, 16, 104)
    arrived = jnp.where(row8 < 3, group(right, 16, 104), group(left, 16, 104))

    from_base = group(left, 8, 112)
    to_base = group(right, 8, 112)
    halo_base = jnp.where(
        row8 < 3,
        jnp.where(row8 < 2, pltpu.roll(group(left, 16, 104), 2, 0), pltpu.roll(from_base, 1, 0)),
        jnp.where(
            row8 < 4,
            pltpu.roll(to_base, 3, 0),
            jnp.concatenate(
                [
                    right[112:120],
                    pltpu.roll(right[112:120], 6, 0),
                    pltpu.roll(right[120:128], 4, 0),
                    pltpu.roll(right[120:128], 2, 0),
                    pltpu.roll(right[112:120], 2, 0),
                ],
                axis=1,
            ),
        ),
    )

    slot_base = group(mine, 8, 112)[:, :INNER]
    near = apart[:SLOTS, :INNER]
    own_w = slot_base + slot_scale[:SLOTS] * added[:SLOTS] + near
    other_w = other_base + slot_scale[SLOTS:] * added[SLOTS:] - near
    apart_w = penalty_weight * (own_w - other_w)
    apart_w = jnp.concatenate([apart_w, jnp.zeros((SLOTS, SENT - INNER), f32)], axis=1)

    target = iota((2 * SLOTS, SLOTS), 1)
    from_left = iota((2 * SLOTS, SLOTS), 0) < SLOTS
    chosen = (edge_line(target) == line[SLOTS:]) & ((target < 3) == from_left)
    halo_apart = select(chosen.astype(f32), apart[SLOTS:], TN)
    halo_w = halo_base + halo_scale * reach + halo_apart
    halo_v = jnp.where(row8 < 6, halo_scale * halo_w, 0.0)

    lane = iota((SLOTS, LINES), 1)
    at_slot = (lane == line[:SLOTS]).astype(f32)
    at_edge = (lane == edge_line(low8)).astype(f32)
    none = jnp.zeros((SLOTS, LINES), f32)
    first = spread_lines(
        jnp.concatenate([apart[:SLOTS], arrived], axis=0),
        jnp.concatenate(
            [
                jnp.concatenate([at_slot, none], axis=1),
                jnp.concatenate([none, at_edge], axis=1),
            ],
            axis=0,
        ),
    )
    distance = jnp.abs(outer_line(low8) - lane)
    second = mix(
        jnp.concatenate([halo_v, apart_w], axis=0),
        jnp.concatenate(
            [
                jnp.concatenate(
                    [taps_at(distance, mass_taps), taps_at(distance, bend_taps), none], axis=1
                ),
                jnp.concatenate([none, none, at_slot], axis=1),
            ],
            axis=0,
        ),
        TN,
        SIX,
    )
    scale = [scale_ref[NEAR + k : NEAR + k + 1, :] for k in range(WIDE)]
    images, masses, bends = [], [], []
    for row in range(WIDE):
        cut = cut_of(row - NEAR)
        scale_row = spread(scale[row])
        image = base_ref[pl.ds(row * COLS, COLS), :] + first[cut, :LINES] + scale_row * first[cut, LINES:]
        value = scale_row * image
        mass, bend = mass_taps[0] * value, bend_taps[0] * value
        for step in range(1, 4):
            pair = pair_of(value, step)
            mass = mass + mass_taps[step] * pair
            if bend_taps[step] != 0.0:
                bend = bend + bend_taps[step] * pair
        images.append(image)
        masses.append(mass + second[cut, :LINES])
        bends.append(bend + second[cut, LINES : 2 * LINES])
    seconds = []
    for row in range(ROWS):
        at_row = row + NEAR
        cut = cut_of(row)
        total = row_stencil(masses, at_row, bend_taps) + row_stencil(bends, at_row, mass_taps)
        product = (
            spread(scale[at_row]) * total
            + spread(d_ref[row : row + 1, :]) * images[at_row]
            + second[cut, 2 * LINES :]
        )
        w_ref[pl.ds(row * COLS, COLS), :] = images[at_row]
        z_ref[pl.ds(row * COLS, COLS), :] = product
        seconds.append(product)
    r = jnp.concatenate([field_ref[pl.ds(k * COLS, COLS), :] for k in range(ROWS)], axis=1)
    w = jnp.concatenate(images[NEAR : NEAR + ROWS], axis=1)
    z = jnp.concatenate(seconds, axis=1)
    fields = [part for field in (r, w, z) for part in parts_of(field, 2)]
    blank = jnp.zeros((2 * COLS, ROWS * LINES), f32)
    products = one_pass(
        jnp.concatenate(fields[:4], axis=0), jnp.concatenate(fields + [blank], axis=0), NT
    )
    by_r = products[:COLS] + products[COLS : 2 * COLS]
    by_w = products[2 * COLS : 3 * COLS] + products[3 * COLS :]
    by_r = by_r + pltpu.roll(by_r, LINES - COLS, 1)
    by_w = by_w + pltpu.roll(by_w, LINES - COLS, 1)
    lane16 = iota((COLS, LINES), 1)
    gram = jnp.where(lane16 // COLS % 2 == 0, by_r, pltpu.roll(by_w, LINES - COLS, 1))
    gram = jnp.where(lane < 4 * COLS, gram[:SLOTS], pltpu.roll(gram[SLOTS:], 4 * COLS, 1))
    for device in range(gram_ref.shape[0]):
        gram_ref[device] = gram


def total_kernel(parts_ref, out_ref):
    total = jnp.sum(parts_ref[...], axis=0)
    for device in range(out_ref.shape[0]):
        out_ref[device] = total


def spd_solve(matrix, right):
    size, width = matrix.shape[0], right.shape[1]
    blank = jnp.zeros((size, LINES - size - width), f32)
    work = jnp.concatenate([matrix, right, blank], axis=1)
    row = iota((size, LINES), 0)
    for start in range(0, size, PANEL):
        columns = [
            jnp.broadcast_to(work[:, start + k : start + k + 1], (size, LINES))
            for k in range(PANEL)
        ]
        for k in range(PANEL):
            at = start + k
            column = columns[k]
            scale = 1.0 / column[at : at + 1, :]

            def eliminate(block):
                pivot_row = block[at : at + 1, :] * scale
                return jnp.where(row == at, pivot_row, block - column * pivot_row)

            work = eliminate(work)
            columns = [eliminate(block) if j > k else block for j, block in enumerate(columns)]
    return work[:, size : size + width]


def layer_kernel(field_ref, w_ref, z_ref, layers_ref):
    for row in range(ROWS):
        cut = pl.ds(row * COLS, COLS)
        cells = jnp.concatenate([field_ref[cut, :], w_ref[cut, :], z_ref[cut, :]], axis=0)
        layers_ref[:, row * LINES : (row + 1) * LINES] = jnp.concatenate(
            parts_of(cells, 3), axis=0
        ).astype(jnp.bfloat16)


def finish_kernel(parts_ref, field_ref, layers_ref, x_hbm, res_hbm, x_ref, res_ref, sems):
    packed = jnp.sum(parts_ref[...], axis=0)
    gram = jnp.concatenate([packed[:, : 4 * COLS], packed[:, 4 * COLS :]], axis=0)
    g00, g11 = gram[:, :COLS], gram[:, COLS : 2 * COLS]
    g01, g12 = gram[:, 2 * COLS : 3 * COLS], gram[:, 3 * COLS :]
    coeffs = spd_solve(
        jnp.concatenate(
            [
                jnp.concatenate([g01, g11], axis=1),
                jnp.concatenate([g11, g12], axis=1),
            ],
            axis=0,
        ),
        jnp.concatenate([g00, g01], axis=0),
    )
    none = jnp.zeros((COLS, COLS), f32)
    weights = jnp.concatenate(
        [
            jnp.concatenate([coeffs, none], axis=0),
            jnp.concatenate([none, -coeffs], axis=0),
        ],
        axis=1,
    )
    weights = jnp.concatenate([jnp.concatenate(parts_of(weights, 3), axis=1)] * 3, axis=0)
    copies = []
    for piece in range(0, ROWS, 8):
        products = one_pass(
            weights, layers_ref[:, piece * LINES : (piece + 8) * LINES], TN
        )
        products = products[: 2 * COLS] + products[2 * COLS : 4 * COLS] + products[4 * COLS :]
        for row in range(piece, piece + 8):
            tile = products[:, (row - piece) * LINES : (row - piece + 1) * LINES]
            x_ref[pl.ds(row, COLS, stride=ROWS), :] = tile[:COLS]
            res_ref[pl.ds(row, COLS, stride=ROWS), :] = (
                field_ref[pl.ds(row * COLS, COLS), :] + tile[COLS:]
            )
        for source, target in ((x_ref, x_hbm), (res_ref, res_hbm)):
            copy = pltpu.make_async_copy(
                source.reshape(COLS, ROWS, LINES).at[:, pl.ds(piece, 8), :],
                target.at[:, pl.ds(piece, 8), :],
                sems.at[len(copies)],
            )
            copy.start()
            copies.append(copy)
    for copy in copies:
        copy.wait()


def call(kernel, shapes, hbm=False, scratch=(), out=pltpu.VMEM):
    def run(*args):
        if hbm and not INTERPRET:
            args = [pltpu.with_memory_space_constraint(arg, pltpu.HBM) for arg in args]
        return pl.pallas_call(
            kernel,
            out_shape=[
                jax.ShapeDtypeStruct(shape, kind) for shape, kind in map(typed, shapes)
            ],
            in_specs=[pl.BlockSpec(memory_space=pltpu.HBM if hbm else pltpu.VMEM)] * len(args),
            out_specs=[pl.BlockSpec(memory_space=out)] * len(shapes),
            scratch_shapes=scratch,
            interpret=INTERPRET,
            compiler_params=pltpu.CompilerParams(vmem_limit_bytes=KERNEL_BYTES),
        )(*args)

    return run


def typed(shape):
    return shape if isinstance(shape[0], tuple) else (shape, f32)


def body(right_side, stiff_scale, extra_diag, iface_line, partner):
    span = lax.axis_size(SPAN)
    plane = lax.axis_size(("core", "chord"))
    depth = lax.axis_size("z")
    cells = right_side.reshape(COLS * ROWS, LINES)
    halo = (DEEP * COLS + 16, LINES)
    flat = (ROWS * COLS, LINES)
    one = (ROWS, LINES)
    field, far, near, scale, extra, slots = call(
        pack_kernel,
        [flat, halo, halo, one, one, ((2, SLOTS, LINES), jnp.int32)],
        hbm=True,
        scratch=[
            pltpu.VMEM(flat, f32),
            pltpu.SMEM((SLOTS,), jnp.int32),
            pltpu.SMEM((SLOTS,), jnp.int32),
            pltpu.SemaphoreType.DMA((5,)),
        ],
    )(iface_line, partner, cells, stiff_scale, extra_diag)
    swaps = [(i, i + 1) for i in range(1, span - 1, 2)]
    far = lax.ppermute(far, SPAN, swaps + [(b, a) for a, b in swaps])
    swaps = [(i, i + 1) for i in range(0, span, 2)]
    near = lax.ppermute(near, SPAN, swaps + [(b, a) for a, b in swaps])
    base, scale, message = call(
        send_kernel, [(FLAT, LINES), (ROWS + 2 * DEEP, LINES), (CHORD, SPARE, LINES)]
    )(field, scale, extra, far, near, slots)
    got = lax.all_to_all(message, "chord", 0, 0)
    w, z, gram = call(apply_kernel, [flat, flat, (plane, 8, LINES)])(
        got, field, base, scale, extra
    )
    gram = lax.all_to_all(gram, ("core", "chord"), 0, 0)
    (gram,) = call(total_kernel, [(depth, 8, LINES)])(gram)
    gram = lax.all_to_all(gram, "z", 0, 0)
    (layers,) = call(layer_kernel, [((9 * COLS, ROWS * LINES), jnp.bfloat16)])(field, w, z)
    block = (COLS, ROWS, LINES)
    return tuple(
        call(
            finish_kernel,
            [block, block],
            scratch=[
                pltpu.VMEM(flat, f32),
                pltpu.VMEM(flat, f32),
                pltpu.SemaphoreType.DMA((8,)),
            ],
            out=pltpu.HBM,
        )(gram, field, layers)
    )


def solution(mesh):
    chord = mesh.devices.shape[1]
    fine = Mesh(mesh.devices.reshape(-1, 2, chord), ("z", "core", "chord"))
    return jax.shard_map(
        body,
        mesh=fine,
        in_specs=(
            P(None, SPAN, "chord"),
            P(SPAN, "chord"),
            P(SPAN, "chord"),
            P("chord"),
            P("chord"),
        ),
        out_specs=(P(None, SPAN, "chord"), P(None, SPAN, "chord")),
        check_vma=False,
    )
```

```python
import jax
import jax.numpy as jnp
from jax import lax
from jax.experimental import pallas as pl
from jax.experimental.pallas import tpu as pltpu
from jax.sharding import Mesh
from jax.sharding import PartitionSpec as P

SPAN = ("z", "core")
COLS = 16
ROWS = 32
LINES = 128
SLOTS = 8
CHORD = 16
DEEP = 6
NEAR = 3
WIDE = ROWS + 2 * NEAR
FLAT = WIDE * COLS
INNER = ROWS * COLS
SENT = 640
KEPT = [3, 4, 5, 6, 7, 24, 25, 26, 27, 28]
OUTER = [-3, -2, -1, 0, 1, 2, 29, 30, 31, 32, 33, 34]
PARTNER_LANE = 104
LINE_LANE = 105
PANEL = 16
SPARE = 128

mass_taps = (2416.0 / 5040.0, 1191.0 / 5040.0, 120.0 / 5040.0, 1.0 / 5040.0)
bend_taps = (8.0 / 3.0, -1.5, 0.0, 1.0 / 6.0)
penalty_weight = 4.0

f32 = jnp.float32
KERNEL_BYTES = 24 << 20
INTERPRET = False


def one_pass(left, right, contract):
    return lax.dot_general(
        left.astype(jnp.bfloat16),
        right.astype(jnp.bfloat16),
        (contract, ((), ())),
        preferred_element_type=f32,
    )


NN, NT, TN = ((1,), (0,)), ((1,), (1,)), ((0,), (0,))


def parts_of(value, count):
    parts = []
    for _ in range(count):
        parts.append(value.astype(jnp.bfloat16).astype(f32))
        value = value - parts[-1]
    return parts


def select(pick, data, contract):
    (left,), (right,) = contract
    return one_pass(
        jnp.concatenate([pick] * 2, axis=left),
        jnp.concatenate(parts_of(data, 2), axis=right),
        contract,
    )


def mix(left, right, contract, pairs):
    count = 1 + max(max(pair) for pair in pairs)
    lefts, rights = parts_of(left, count), parts_of(right, count)
    return one_pass(
        jnp.concatenate([lefts[a] for a, _ in pairs], axis=contract[0][0]),
        jnp.concatenate([rights[b] for _, b in pairs], axis=contract[1][0]),
        contract,
    )


THREE = ((0, 0), (0, 1), (1, 0))


def iota(shape, dim):
    return lax.broadcasted_iota(jnp.int32, shape, dim)


def taps_at(distance, taps):
    value = jnp.zeros(distance.shape, f32)
    for step in range(4):
        if taps[step] != 0.0:
            value = jnp.where(distance == step, taps[step], value)
    return value


def outer_line(row):
    return jnp.where(row < 3, row - 3, jnp.where(row < 6, row + LINES - 3, 4 * LINES))


def edge_line(row):
    return jnp.where(row < 3, row + LINES - 3, jnp.where(row < 6, row - 3, 4 * LINES))


def pair_of(field, step):
    lane = iota((COLS, LINES), 1)
    ahead = jnp.where(lane < LINES - step, pltpu.roll(field, LINES - step, 1), 0.0)
    behind = jnp.where(lane >= step, pltpu.roll(field, step, 1), 0.0)
    return ahead + behind


def row_stencil(rows, at, taps):
    total = taps[0] * rows[at]
    for step in range(1, 4):
        if taps[step] != 0.0:
            total = total + taps[step] * (rows[at - step] + rows[at + step])
    return total


def spread(row):
    return jnp.broadcast_to(row, (COLS, LINES))


def pack_kernel(
    line_hbm, partner_hbm, r_hbm, s_hbm, d_hbm,
    field_ref, far_ref, near_ref, s_ref, d_ref, slots_ref,
    r_ref, line_ref, partner_ref, sems
):
    copies = [
        pltpu.make_async_copy(source, target, sems.at[k])
        for k, (source, target) in enumerate(
            [
                (r_hbm, r_ref),
                (s_hbm, s_ref),
                (d_hbm, d_ref),
                (line_hbm, line_ref),
                (partner_hbm, partner_ref),
            ]
        )
    ]
    for copy in copies:
        copy.start()
    for copy in copies:
        copy.wait()
    first_core = lax.axis_index("core") == 0
    rows = []
    for row in range(ROWS):
        cells = r_ref[pl.ds(row, COLS, stride=ROWS), :]
        field_ref[pl.ds(row * COLS, COLS), :] = cells
        rows.append(cells)
    pad = jnp.zeros((2, LINES), f32)
    low, high = slice(0, DEEP), slice(ROWS - DEEP, ROWS)
    ends = [
        jnp.concatenate(rows[cut] + [s_ref[cut, :], pad, d_ref[cut, :], pad], axis=0)
        for cut in (low, high)
    ]
    far_ref[...] = jnp.where(first_core, ends[0], ends[1])
    near_ref[...] = jnp.where(first_core, ends[1], ends[0])
    row = iota((SLOTS, LINES), 0)
    for k, scalars in enumerate((line_ref, partner_ref)):
        value = jnp.zeros((SLOTS, LINES), jnp.int32)
        for slot in range(SLOTS):
            value = jnp.where(row == slot, scalars[slot], value)
        slots_ref[k] = value


def first_product(weighted, at, scale, extra, cells):
    mass = row_stencil(weighted, at, mass_taps)
    bend = row_stencil(weighted, at, bend_taps)
    total = mass_taps[0] * bend + bend_taps[0] * mass
    for step in range(1, 4):
        mixed = mass_taps[step] * bend
        if bend_taps[step] != 0.0:
            mixed = mixed + bend_taps[step] * mass
        total = total + pair_of(mixed, step)
    return mass, bend, spread(scale) * total + spread(extra) * cells


def line_picks(slots_ref):
    lane = iota((SLOTS, LINES), 1)
    row8 = iota((SLOTS, LINES), 0)
    at_slot = (lane == slots_ref[0]).astype(f32)
    at_edge = (lane == edge_line(row8)).astype(f32)
    other_edge = (
        ((lane == row8 + 1) & (row8 < 2)) | ((lane == row8 + LINES - 9) & (row8 >= 6))
    ).astype(f32)
    distance = jnp.abs(outer_line(row8) - lane)
    reach = jnp.concatenate([taps_at(distance, mass_taps), taps_at(distance, bend_taps)], axis=1)
    return at_slot, at_edge, jnp.concatenate([at_slot, other_edge], axis=0), reach


def reach_of(reach, bends, masses):
    return mix(reach, jnp.concatenate([bends, masses], axis=1), NT, THREE)


def inner_kernel(
    field_ref, s_ref, d_ref, slots_ref, base_ref, mass_ref, bend_ref, cells_ref, sent_ref, reach_ref
):
    cells = [field_ref[pl.ds(k * COLS, COLS), :] for k in range(ROWS)]
    weighted = [spread(s_ref[k : k + 1, :]) * cells[k] for k in range(ROWS)]
    masses, bends, bases = {}, {}, {}
    for row in range(NEAR, ROWS - NEAR):
        masses[row], bends[row], bases[row] = first_product(
            weighted, row, s_ref[row : row + 1, :], d_ref[row : row + 1, :], cells[row]
        )
        base_ref[pl.ds((row - NEAR) * COLS, COLS), :] = bases[row]
    for place, row in enumerate(KEPT):
        mass_ref[pl.ds(place * COLS, COLS), :] = masses[row]
        bend_ref[pl.ds(place * COLS, COLS), :] = bends[row]

    def middle(rows):
        return jnp.concatenate([rows[row] for row in range(8, ROWS - 8)], axis=0)

    at_slot, _, at_lines, reach = line_picks(slots_ref)
    cells_ref[...] = select(at_slot, jnp.concatenate(cells, axis=0), NT)
    sent_ref[...] = select(at_lines, middle(bases), NT)
    reach_ref[...] = reach_of(reach, middle(bends), middle(masses))


def send_kernel(
    field_ref, s_ref, d_ref, far_ref, near_ref, slots_ref,
    inner_ref, mass_ref, bend_ref, cells_ref, sent_ref, reach_ref,
    base_ref, scale_ref, message_ref
):
    first_core = lax.axis_index("core") == 0
    below = jnp.where(first_core, far_ref[...], near_ref[...])
    above = jnp.where(first_core, near_ref[...], far_ref[...])
    start = DEEP * COLS
    scale_ref[0:DEEP, :] = below[start : start + DEEP]
    scale_ref[DEEP : DEEP + ROWS, :] = s_ref[...]
    scale_ref[DEEP + ROWS : 2 * DEEP + ROWS, :] = above[start : start + DEEP]
    cells, scale, extra, weighted = {}, {}, {}, {}
    ends = list(range(-DEEP, DEEP)) + list(range(ROWS - DEEP, ROWS + DEEP))
    for row in ends:
        if row < 0:
            source, at = below, row + DEEP
        elif row >= ROWS:
            source, at = above, row - ROWS
        else:
            source, at = None, row
        if source is None:
            cells[row] = field_ref[pl.ds(at * COLS, COLS), :]
            scale[row], extra[row] = s_ref[at : at + 1, :], d_ref[at : at + 1, :]
        else:
            cells[row] = source[at * COLS : (at + 1) * COLS]
            scale[row] = source[start + at : start + at + 1]
            extra[row] = source[start + 8 + at : start + 9 + at]
        weighted[row] = spread(scale[row]) * cells[row]
    masses, bends, bases = {}, {}, {}
    for place, row in enumerate(OUTER):
        masses[row], bends[row], bases[row] = first_product(
            weighted, row, scale[row], extra[row], cells[row]
        )
        base_ref[pl.ds(place * COLS, COLS), :] = bases[row]
    for place, row in enumerate(KEPT):
        masses[row] = mass_ref[pl.ds(place * COLS, COLS), :]
        bends[row] = bend_ref[pl.ds(place * COLS, COLS), :]
        bases[row] = inner_ref[pl.ds((row - NEAR) * COLS, COLS), :]
    halo_rows = list(range(-NEAR, 0)) + list(range(ROWS, ROWS + NEAR))
    blank = jnp.zeros((SENT - FLAT, LINES), f32)
    tail = FLAT - INNER

    def outer(rows):
        listed = list(range(8)) + list(range(ROWS - 8, ROWS)) + halo_rows
        return jnp.concatenate([rows[row] for row in listed] + [blank], axis=0)

    scales = jnp.concatenate(
        [jnp.zeros((tail, LINES), f32), s_ref[...], jnp.zeros((tail, LINES), f32)]
        + [scale[row] for row in halo_rows]
        + [jnp.zeros((LINES - tail - 6, LINES), f32)],
        axis=0,
    )
    lane = iota((SLOTS, LINES), 1)
    row8 = iota((SLOTS, LINES), 0)
    at_slot, at_edge, at_lines, reach = line_picks(slots_ref)
    halo_cells = jnp.concatenate([cells[row] for row in halo_rows] + [blank], axis=0)
    sent_tail = select(at_slot, halo_cells, NT)
    sent_scale = select(at_edge, scales, NT)
    outer_base = select(at_lines, outer(bases), NT)
    outer_reach = reach_of(reach, outer(bends), outer(masses))

    def joined(outer_part, middle_part):
        return jnp.concatenate(
            [outer_part[:, :LINES], middle_part, outer_part[:, LINES:]], axis=1
        )

    sent_base = joined(outer_base, sent_ref[...])
    sent_reach = joined(outer_reach, reach_ref[...])
    slot_base, edge_base = sent_base[:SLOTS], sent_base[SLOTS:]
    wide_row = iota((SLOTS, SENT), 0)
    wide_lane = iota((SLOTS, SENT), 1)
    third = jnp.where((wide_row < 6) | (wide_lane >= FLAT), sent_reach, edge_base)
    last = third[:, INNER:] + sent_scale[:, LINES:]
    last = jnp.where(lane == PARTNER_LANE, slots_ref[1].astype(f32), last)
    last = jnp.where(lane == LINE_LANE, slots_ref[0].astype(f32), last)

    def piece(block, at):
        return block[:, at * LINES : (at + 1) * LINES]

    def moved(block, at, shift):
        return pltpu.roll(piece(block, at), shift, 0)

    parts = []
    for at in range(4):
        parts += [piece(cells_ref, at), piece(slot_base, at), piece(third, at)]
    parts += [sent_tail + sent_scale[:, :LINES], last]
    parts += [
        jnp.where(
            row8 < 4,
            jnp.where(row8 < 2, piece(slot_base, 4), moved(edge_base, 4, 2)),
            jnp.where(row8 < 6, moved(edge_base, 0, 4), moved(edge_base, 1, 6)),
        ),
        jnp.where(row8 < 2, piece(edge_base, 2), moved(edge_base, 3, 2)),
    ]
    message = jnp.concatenate(parts, axis=0)
    for device in range(CHORD):
        message_ref[device] = message


def cut_of(row):
    place = row if 0 <= row < ROWS else ROWS + NEAR + row if row < 0 else NEAR + row
    return slice(place * COLS, (place + 1) * COLS)


def expand(data, pattern):
    rows = data.shape[0]
    product = one_pass(jnp.concatenate(parts_of(data, 2), axis=0), pattern, NN)
    return product[:rows] + product[rows:]


def spread_lines(data, pattern):
    return one_pass(
        jnp.concatenate(parts_of(data, 2), axis=0), jnp.concatenate([pattern] * 2, axis=0), TN
    )


def rim_spread():
    spot = iota((LINES, LINES), 0) - (FLAT - INNER)
    return ((spot == iota((LINES, LINES), 1) // COLS) & (spot < 2 * NEAR)).astype(f32)


def apply_kernel(
    got_ref, field_ref, inner_ref, base_ref, scale_ref, d_ref, w_ref, z_ref, gram_ref
):
    here = lax.axis_index("chord")
    devices = [here, lax.rem(here + CHORD - 1, CHORD), lax.rem(here + 1, CHORD)]
    mine, left, right = [got_ref[device] for device in devices]

    def group(block, first, tail):
        tiles = [block[first + 24 * k : first + 24 * k + 8] for k in range(4)]
        return jnp.concatenate(tiles + [block[tail : tail + 8]], axis=1)

    def everyone(at):
        return got_ref[:, at : at + 8, :].reshape(CHORD * SLOTS, LINES)

    all_cells = jnp.concatenate([everyone(at) for at in (0, 24, 48, 72, 96)], axis=1)
    all_base = jnp.concatenate([everyone(at) for at in (8, 32, 56, 80)], axis=1)
    all_reach = jnp.concatenate([everyone(at) for at in (16, 40, 64, 88)], axis=1)

    slots = jnp.concatenate([group(block, 0, 96) for block in (mine, left, right)], axis=0)
    numbers = jnp.concatenate([block[104:112] for block in (mine, left, right)], axis=0)
    partner = numbers[:, PARTNER_LANE : PARTNER_LANE + 1].astype(jnp.int32)
    line = numbers[:, LINE_LANE : LINE_LANE + 1].astype(jnp.int32)
    pick = (iota((3 * SLOTS, LINES), 1) == partner).astype(f32)
    other = select(pick, all_cells, NN)
    apart = penalty_weight * (slots - other)
    other_numbers = one_pass(pick[:SLOTS], everyone(104), NN)
    other_line = other_numbers[:, LINE_LANE : LINE_LANE + 1].astype(jnp.int32)
    other_device = partner[:SLOTS] // SLOTS
    other_base = select(pick[:SLOTS], all_base, NN)

    device = jnp.concatenate([jnp.full((SLOTS, 1), here, jnp.int32), other_device], axis=0)
    at = jnp.concatenate([line[:SLOTS], other_line], axis=0)
    before = lax.rem(device + CHORD - 1, CHORD) * SLOTS + NEAR + at
    after = lax.rem(device + 1, CHORD) * SLOTS + at - (LINES - NEAR)
    is_low, is_high = at < NEAR, at >= LINES - NEAR
    source = jnp.where(is_low, before, jnp.where(is_high, after, -1))
    added = select((iota((2 * SLOTS, LINES), 1) == source).astype(f32), all_reach, NN)
    edge = device * SLOTS + jnp.where(is_low, at + NEAR, at - (LINES - NEAR))
    edge = jnp.where(is_low | is_high, edge, -1)
    spare = select((iota((2 * SLOTS, LINES), 1) == edge).astype(f32), everyone(96), NN)

    low8 = iota((SLOTS, LINES), 0)
    row8 = iota((SLOTS, SENT), 0)
    halo_spare = jnp.where(low8 < 3, left[96:104], right[96:104])
    halo_rim = jnp.where(low8 < 3, left[104:112], right[104:112])
    inner = (
        iota((LINES, INNER), 0) == iota((LINES, INNER), 1) // COLS + (FLAT - INNER)
    ).astype(f32)
    scales = expand(jnp.concatenate([spare, halo_spare], axis=0), inner)
    slot_scale = scales[: 2 * SLOTS]
    halo_scale = jnp.concatenate(
        [scales[2 * SLOTS :], expand(halo_rim, rim_spread())], axis=1
    )
    reach = group(mine, 16, 104)
    arrived = jnp.where(row8 < 3, group(right, 16, 104), group(left, 16, 104))

    from_base = group(left, 8, 112)
    to_base = group(right, 8, 112)
    halo_base = jnp.where(
        row8 < 3,
        jnp.where(row8 < 2, pltpu.roll(group(left, 16, 104), 2, 0), pltpu.roll(from_base, 1, 0)),
        jnp.where(
            row8 < 4,
            pltpu.roll(to_base, 3, 0),
            jnp.concatenate(
                [
                    right[112:120],
                    pltpu.roll(right[112:120], 6, 0),
                    pltpu.roll(right[120:128], 4, 0),
                    pltpu.roll(right[120:128], 2, 0),
                    pltpu.roll(right[112:120], 2, 0),
                ],
                axis=1,
            ),
        ),
    )

    slot_base = group(mine, 8, 112)[:, :INNER]
    near = apart[:SLOTS, :INNER]
    own_w = slot_base + slot_scale[:SLOTS] * added[:SLOTS] + near
    other_w = other_base + slot_scale[SLOTS:] * added[SLOTS:] - near
    apart_w = penalty_weight * (own_w - other_w)
    apart_w = jnp.concatenate([apart_w, jnp.zeros((SLOTS, SENT - INNER), f32)], axis=1)

    target = iota((2 * SLOTS, SLOTS), 1)
    from_left = iota((2 * SLOTS, SLOTS), 0) < SLOTS
    chosen = (edge_line(target) == line[SLOTS:]) & ((target < 3) == from_left)
    halo_apart = select(chosen.astype(f32), apart[SLOTS:], TN)
    halo_w = halo_base + halo_scale * reach + halo_apart
    halo_v = jnp.where(row8 < 6, halo_scale * halo_w, 0.0)

    lane = iota((SLOTS, LINES), 1)
    at_slot = (lane == line[:SLOTS]).astype(f32)
    at_edge = (lane == edge_line(low8)).astype(f32)
    none = jnp.zeros((SLOTS, LINES), f32)
    first = spread_lines(
        jnp.concatenate([apart[:SLOTS], arrived], axis=0),
        jnp.concatenate(
            [
                jnp.concatenate([at_slot, none], axis=1),
                jnp.concatenate([none, at_edge], axis=1),
            ],
            axis=0,
        ),
    )
    distance = jnp.abs(outer_line(low8) - lane)
    second = mix(
        jnp.concatenate([halo_v, apart_w], axis=0),
        jnp.concatenate(
            [
                jnp.concatenate(
                    [taps_at(distance, mass_taps), taps_at(distance, bend_taps), none], axis=1
                ),
                jnp.concatenate([none, none, at_slot], axis=1),
            ],
            axis=0,
        ),
        TN,
        THREE,
    )
    scale = [scale_ref[NEAR + k : NEAR + k + 1, :] for k in range(WIDE)]
    images, masses, bends = [], [], []
    for row in range(WIDE):
        cut = cut_of(row - NEAR)
        scale_row = spread(scale[row])
        place = row - NEAR
        if place in OUTER:
            base = base_ref[pl.ds(OUTER.index(place) * COLS, COLS), :]
        else:
            base = inner_ref[pl.ds((place - NEAR) * COLS, COLS), :]
        image = base + first[cut, :LINES] + scale_row * first[cut, LINES:]
        value = scale_row * image
        mass, bend = mass_taps[0] * value, bend_taps[0] * value
        for step in range(1, 4):
            pair = pair_of(value, step)
            mass = mass + mass_taps[step] * pair
            if bend_taps[step] != 0.0:
                bend = bend + bend_taps[step] * pair
        images.append(image)
        masses.append(mass + second[cut, :LINES])
        bends.append(bend + second[cut, LINES : 2 * LINES])
    seconds = []
    for row in range(ROWS):
        at_row = row + NEAR
        cut = cut_of(row)
        total = row_stencil(masses, at_row, bend_taps) + row_stencil(bends, at_row, mass_taps)
        product = (
            spread(scale[at_row]) * total
            + spread(d_ref[row : row + 1, :]) * images[at_row]
            + second[cut, 2 * LINES :]
        )
        w_ref[pl.ds(row * COLS, COLS), :] = images[at_row]
        z_ref[pl.ds(row * COLS, COLS), :] = product
        seconds.append(product)
    r = jnp.concatenate([field_ref[pl.ds(k * COLS, COLS), :] for k in range(ROWS)], axis=1)
    w = jnp.concatenate(images[NEAR : NEAR + ROWS], axis=1)
    z = jnp.concatenate(seconds, axis=1)
    fields = [part for field in (r, w, z) for part in parts_of(field, 2)]
    blank = jnp.zeros((2 * COLS, ROWS * LINES), f32)
    products = one_pass(
        jnp.concatenate(fields[:4], axis=0), jnp.concatenate(fields + [blank], axis=0), NT
    )
    by_r = products[:COLS] + products[COLS : 2 * COLS]
    by_w = products[2 * COLS : 3 * COLS] + products[3 * COLS :]
    by_r = by_r + pltpu.roll(by_r, LINES - COLS, 1)
    by_w = by_w + pltpu.roll(by_w, LINES - COLS, 1)
    lane16 = iota((COLS, LINES), 1)
    gram = jnp.where(lane16 // COLS % 2 == 0, by_r, pltpu.roll(by_w, LINES - COLS, 1))
    gram = jnp.where(lane < 4 * COLS, gram[:SLOTS], pltpu.roll(gram[SLOTS:], 4 * COLS, 1))
    for device in range(gram_ref.shape[0]):
        gram_ref[device] = gram


def total_kernel(parts_ref, out_ref):
    total = jnp.sum(parts_ref[...], axis=0)
    for device in range(out_ref.shape[0]):
        out_ref[device] = total


def spd_solve(matrix, right):
    size, width = matrix.shape[0], right.shape[1]
    blank = jnp.zeros((size, LINES - size - width), f32)
    work = jnp.concatenate([matrix, right, blank], axis=1)
    row = iota((size, LINES), 0)
    for start in range(0, size, PANEL):
        columns = [
            jnp.broadcast_to(work[:, start + k : start + k + 1], (size, LINES))
            for k in range(PANEL)
        ]
        for k in range(PANEL):
            at = start + k
            column = columns[k]
            scale = 1.0 / column[at : at + 1, :]

            def eliminate(block):
                pivot_row = block[at : at + 1, :] * scale
                return jnp.where(row == at, pivot_row, block - column * pivot_row)

            work = eliminate(work)
            columns = [eliminate(block) if j > k else block for j, block in enumerate(columns)]
    return work[:, size : size + width]


def finish_kernel(parts_ref, field_ref, w_ref, z_ref, x_ref, res_ref):
    packed = jnp.sum(parts_ref[...], axis=0)
    gram = jnp.concatenate([packed[:, : 4 * COLS], packed[:, 4 * COLS :]], axis=0)
    g00, g11 = gram[:, :COLS], gram[:, COLS : 2 * COLS]
    g01, g12 = gram[:, 2 * COLS : 3 * COLS], gram[:, 3 * COLS :]
    coeffs = spd_solve(
        jnp.concatenate(
            [
                jnp.concatenate([g01, g11], axis=1),
                jnp.concatenate([g11, g12], axis=1),
            ],
            axis=0,
        ),
        jnp.concatenate([g00, g01], axis=0),
    )
    r = jnp.concatenate([field_ref[pl.ds(k * COLS, COLS), :] for k in range(ROWS)], axis=1)
    w = jnp.concatenate([w_ref[pl.ds(k * COLS, COLS), :] for k in range(ROWS)], axis=1)
    z = jnp.concatenate([z_ref[pl.ds(k * COLS, COLS), :] for k in range(ROWS)], axis=1)
    none = jnp.zeros((COLS, COLS), f32)
    weights = jnp.concatenate(
        [
            jnp.concatenate([coeffs, none], axis=0),
            jnp.concatenate([none, -coeffs], axis=0),
        ],
        axis=1,
    )
    products = one_pass(
        jnp.concatenate([jnp.concatenate(parts_of(weights, 2), axis=1)] * 2, axis=0),
        jnp.concatenate(parts_of(jnp.concatenate([r, w, z], axis=0), 2), axis=0),
        TN,
    )
    products = products[: 2 * COLS] + products[2 * COLS :]
    x, res = products[:COLS], r + products[COLS:]
    for row in range(ROWS):
        cut = slice(row * LINES, (row + 1) * LINES)
        x_ref[pl.ds(row, COLS, stride=ROWS), :] = x[:, cut]
        res_ref[pl.ds(row, COLS, stride=ROWS), :] = res[:, cut]


def call(kernel, shapes, hbm=False, scratch=(), cost=None):
    def run(*args):
        if hbm and not INTERPRET:
            args = [pltpu.with_memory_space_constraint(arg, pltpu.HBM) for arg in args]
        return pl.pallas_call(
            kernel,
            out_shape=[
                jax.ShapeDtypeStruct(shape, kind) for shape, kind in map(typed, shapes)
            ],
            in_specs=[pl.BlockSpec(memory_space=pltpu.HBM if hbm else pltpu.VMEM)] * len(args),
            out_specs=[pl.BlockSpec(memory_space=pltpu.VMEM)] * len(shapes),
            scratch_shapes=scratch,
            interpret=INTERPRET,
            cost_estimate=cost,
            compiler_params=pltpu.CompilerParams(vmem_limit_bytes=KERNEL_BYTES),
        )(*args)

    return run


def typed(shape):
    return shape if isinstance(shape[0], tuple) else (shape, f32)


def body(right_side, stiff_scale, extra_diag, iface_line, partner):
    span = lax.axis_size(SPAN)
    plane = lax.axis_size(("core", "chord"))
    depth = lax.axis_size("z")
    cells = right_side.reshape(COLS * ROWS, LINES)
    halo = (DEEP * COLS + 16, LINES)
    flat = (ROWS * COLS, LINES)
    one = (ROWS, LINES)
    field, far, near, scale, extra, slots = call(
        pack_kernel,
        [flat, halo, halo, one, one, ((2, SLOTS, LINES), jnp.int32)],
        hbm=True,
        scratch=[
            pltpu.VMEM(flat, f32),
            pltpu.SMEM((SLOTS,), jnp.int32),
            pltpu.SMEM((SLOTS,), jnp.int32),
            pltpu.SemaphoreType.DMA((5,)),
        ],
    )(iface_line, partner, cells, stiff_scale, extra_diag)
    swaps = [(i, i + 1) for i in range(1, span - 1, 2)]
    far = lax.ppermute(far, SPAN, swaps + [(b, a) for a, b in swaps])
    swaps = [(i, i + 1) for i in range(0, span, 2)]
    near = lax.ppermute(near, SPAN, swaps + [(b, a) for a, b in swaps])
    kept = (len(KEPT) * COLS, LINES)
    inner = call(
        inner_kernel,
        [
            ((ROWS - 2 * NEAR) * COLS, LINES),
            kept,
            kept,
            (SLOTS, INNER),
            (2 * SLOTS, 2 * LINES),
            (SLOTS, 2 * LINES),
        ],
        cost=pl.CostEstimate(flops=40_000_000, bytes_accessed=2_000_000, transcendentals=0),
    )
    inner = inner(field, scale, extra, slots)
    base, scale, message = call(
        send_kernel,
        [(len(OUTER) * COLS, LINES), (ROWS + 2 * DEEP, LINES), (CHORD, SPARE, LINES)],
    )(field, scale, extra, far, near, slots, *inner)
    got = lax.all_to_all(message, "chord", 0, 0)
    w, z, gram = call(apply_kernel, [flat, flat, (plane, 8, LINES)])(
        got, field, inner[0], base, scale, extra
    )
    gram = lax.all_to_all(gram, ("core", "chord"), 0, 0)
    (gram,) = call(total_kernel, [(depth, 8, LINES)])(gram)
    gram = lax.all_to_all(gram, "z", 0, 0)
    x, res = call(finish_kernel, [flat, flat])(gram, field, w, z)
    return (x.reshape(COLS, ROWS, LINES), res.reshape(COLS, ROWS, LINES))


def solution(mesh):
    chord = mesh.devices.shape[1]
    fine = Mesh(mesh.devices.reshape(-1, 2, chord), ("z", "core", "chord"))
    return jax.shard_map(
        body,
        mesh=fine,
        in_specs=(
            P(None, SPAN, "chord"),
            P(SPAN, "chord"),
            P(SPAN, "chord"),
            P("chord"),
            P("chord"),
        ),
        out_specs=(P(None, SPAN, "chord"), P(None, SPAN, "chord")),
        check_vma=False,
    )
```

```python
import jax
import jax.numpy as jnp
from jax import lax
from jax.experimental import pallas as pl
from jax.experimental.pallas import tpu as pltpu
from jax.sharding import Mesh
from jax.sharding import PartitionSpec as P

SPAN = ("z", "core")
COLS = 16
ROWS = 32
LINES = 128
SLOTS = 8
CHORD = 16
DEEP = 6
NEAR = 3
WIDE = ROWS + 2 * NEAR
FLAT = WIDE * COLS
INNER = ROWS * COLS
SENT = 640
KEPT = [3, 4, 5, 6, 7, 24, 25, 26, 27, 28]
OUTER = [-3, -2, -1, 0, 1, 2, 29, 30, 31, 32, 33, 34]
PARTNER_LANE = 104
LINE_LANE = 105
PANEL = 16
SPARE = 128

mass_taps = (2416.0 / 5040.0, 1191.0 / 5040.0, 120.0 / 5040.0, 1.0 / 5040.0)
bend_taps = (8.0 / 3.0, -1.5, 0.0, 1.0 / 6.0)
penalty_weight = 4.0

f32 = jnp.float32
KERNEL_BYTES = 24 << 20
INTERPRET = False


def one_pass(left, right, contract):
    return lax.dot_general(
        left.astype(jnp.bfloat16),
        right.astype(jnp.bfloat16),
        (contract, ((), ())),
        preferred_element_type=f32,
    )


NN, NT, TN = ((1,), (0,)), ((1,), (1,)), ((0,), (0,))


def parts_of(value, count):
    parts = []
    for _ in range(count):
        parts.append(value.astype(jnp.bfloat16).astype(f32))
        value = value - parts[-1]
    return parts


def select(pick, data, contract):
    (left,), (right,) = contract
    return one_pass(
        jnp.concatenate([pick] * 2, axis=left),
        jnp.concatenate(parts_of(data, 2), axis=right),
        contract,
    )


def mix(left, right, contract, pairs):
    count = 1 + max(max(pair) for pair in pairs)
    lefts, rights = parts_of(left, count), parts_of(right, count)
    return one_pass(
        jnp.concatenate([lefts[a] for a, _ in pairs], axis=contract[0][0]),
        jnp.concatenate([rights[b] for _, b in pairs], axis=contract[1][0]),
        contract,
    )


THREE = ((0, 0), (0, 1), (1, 0))


def iota(shape, dim):
    return lax.broadcasted_iota(jnp.int32, shape, dim)


def taps_at(distance, taps):
    value = jnp.zeros(distance.shape, f32)
    for step in range(4):
        if taps[step] != 0.0:
            value = jnp.where(distance == step, taps[step], value)
    return value


def outer_line(row):
    return jnp.where(row < 3, row - 3, jnp.where(row < 6, row + LINES - 3, 4 * LINES))


def edge_line(row):
    return jnp.where(row < 3, row + LINES - 3, jnp.where(row < 6, row - 3, 4 * LINES))


def pair_of(field, step):
    lane = iota((COLS, LINES), 1)
    ahead = jnp.where(lane < LINES - step, pltpu.roll(field, LINES - step, 1), 0.0)
    behind = jnp.where(lane >= step, pltpu.roll(field, step, 1), 0.0)
    return ahead + behind


def row_stencil(rows, at, taps):
    total = taps[0] * rows[at]
    for step in range(1, 4):
        if taps[step] != 0.0:
            total = total + taps[step] * (rows[at - step] + rows[at + step])
    return total


def spread(row):
    return jnp.broadcast_to(row, (COLS, LINES))


def pack_kernel(
    line_hbm, partner_hbm, r_hbm, s_hbm, d_hbm,
    field_ref, far_ref, near_ref, s_ref, d_ref, slots_ref,
    r_ref, line_ref, partner_ref, sems
):
    copies = [
        pltpu.make_async_copy(source, target, sems.at[k])
        for k, (source, target) in enumerate(
            [
                (r_hbm, r_ref),
                (s_hbm, s_ref),
                (d_hbm, d_ref),
                (line_hbm, line_ref),
                (partner_hbm, partner_ref),
            ]
        )
    ]
    for copy in copies:
        copy.start()
    for copy in copies:
        copy.wait()
    first_core = lax.axis_index("core") == 0
    rows = []
    for row in range(ROWS):
        cells = r_ref[pl.ds(row, COLS, stride=ROWS), :]
        field_ref[pl.ds(row * COLS, COLS), :] = cells
        rows.append(cells)
    pad = jnp.zeros((2, LINES), f32)
    low, high = slice(0, DEEP), slice(ROWS - DEEP, ROWS)
    ends = [
        jnp.concatenate(rows[cut] + [s_ref[cut, :], pad, d_ref[cut, :], pad], axis=0)
        for cut in (low, high)
    ]
    far_ref[...] = jnp.where(first_core, ends[0], ends[1])
    near_ref[...] = jnp.where(first_core, ends[1], ends[0])
    row = iota((SLOTS, LINES), 0)
    for k, scalars in enumerate((line_ref, partner_ref)):
        value = jnp.zeros((SLOTS, LINES), jnp.int32)
        for slot in range(SLOTS):
            value = jnp.where(row == slot, scalars[slot], value)
        slots_ref[k] = value


def first_product(weighted, at, scale, extra, cells):
    mass = row_stencil(weighted, at, mass_taps)
    bend = row_stencil(weighted, at, bend_taps)
    total = mass_taps[0] * bend + bend_taps[0] * mass
    for step in range(1, 4):
        mixed = mass_taps[step] * bend
        if bend_taps[step] != 0.0:
            mixed = mixed + bend_taps[step] * mass
        total = total + pair_of(mixed, step)
    return mass, bend, spread(scale) * total + spread(extra) * cells


def line_picks(slots_ref):
    lane = iota((SLOTS, LINES), 1)
    row8 = iota((SLOTS, LINES), 0)
    at_slot = (lane == slots_ref[0]).astype(f32)
    at_edge = (lane == edge_line(row8)).astype(f32)
    other_edge = (
        ((lane == row8 + 1) & (row8 < 2)) | ((lane == row8 + LINES - 9) & (row8 >= 6))
    ).astype(f32)
    distance = jnp.abs(outer_line(row8) - lane)
    reach = jnp.concatenate([taps_at(distance, mass_taps), taps_at(distance, bend_taps)], axis=1)
    return at_slot, at_edge, jnp.concatenate([at_slot, other_edge], axis=0), reach


def reach_of(reach, bends, masses):
    return mix(reach, jnp.concatenate([bends, masses], axis=1), NT, THREE)


def inner_kernel(
    field_ref, s_ref, d_ref, slots_ref, base_ref, mass_ref, bend_ref, cells_ref, sent_ref, reach_ref
):
    cells = [field_ref[pl.ds(k * COLS, COLS), :] for k in range(ROWS)]
    weighted = [spread(s_ref[k : k + 1, :]) * cells[k] for k in range(ROWS)]
    masses, bends, bases = {}, {}, {}
    for row in range(NEAR, ROWS - NEAR):
        masses[row], bends[row], bases[row] = first_product(
            weighted, row, s_ref[row : row + 1, :], d_ref[row : row + 1, :], cells[row]
        )
        base_ref[pl.ds((row - NEAR) * COLS, COLS), :] = bases[row]
    for place, row in enumerate(KEPT):
        mass_ref[pl.ds(place * COLS, COLS), :] = masses[row]
        bend_ref[pl.ds(place * COLS, COLS), :] = bends[row]

    def middle(rows):
        return jnp.concatenate([rows[row] for row in range(8, ROWS - 8)], axis=0)

    at_slot, _, at_lines, reach = line_picks(slots_ref)
    cells_ref[...] = select(at_slot, jnp.concatenate(cells, axis=0), NT)
    sent_ref[...] = select(at_lines, middle(bases), NT)
    reach_ref[...] = reach_of(reach, middle(bends), middle(masses))


def send_kernel(
    field_ref, s_ref, d_ref, far_ref, near_ref, slots_ref,
    inner_ref, mass_ref, bend_ref, cells_ref, sent_ref, reach_ref,
    base_ref, scale_ref, message_ref
):
    first_core = lax.axis_index("core") == 0
    below = jnp.where(first_core, far_ref[...], near_ref[...])
    above = jnp.where(first_core, near_ref[...], far_ref[...])
    start = DEEP * COLS
    scale_ref[0:DEEP, :] = below[start : start + DEEP]
    scale_ref[DEEP : DEEP + ROWS, :] = s_ref[...]
    scale_ref[DEEP + ROWS : 2 * DEEP + ROWS, :] = above[start : start + DEEP]
    cells, scale, extra, weighted = {}, {}, {}, {}
    ends = list(range(-DEEP, DEEP)) + list(range(ROWS - DEEP, ROWS + DEEP))
    for row in ends:
        if row < 0:
            source, at = below, row + DEEP
        elif row >= ROWS:
            source, at = above, row - ROWS
        else:
            source, at = None, row
        if source is None:
            cells[row] = field_ref[pl.ds(at * COLS, COLS), :]
            scale[row], extra[row] = s_ref[at : at + 1, :], d_ref[at : at + 1, :]
        else:
            cells[row] = source[at * COLS : (at + 1) * COLS]
            scale[row] = source[start + at : start + at + 1]
            extra[row] = source[start + 8 + at : start + 9 + at]
        weighted[row] = spread(scale[row]) * cells[row]
    masses, bends, bases = {}, {}, {}
    for place, row in enumerate(OUTER):
        masses[row], bends[row], bases[row] = first_product(
            weighted, row, scale[row], extra[row], cells[row]
        )
        base_ref[pl.ds(place * COLS, COLS), :] = bases[row]
    for place, row in enumerate(KEPT):
        masses[row] = mass_ref[pl.ds(place * COLS, COLS), :]
        bends[row] = bend_ref[pl.ds(place * COLS, COLS), :]
        bases[row] = inner_ref[pl.ds((row - NEAR) * COLS, COLS), :]
    halo_rows = list(range(-NEAR, 0)) + list(range(ROWS, ROWS + NEAR))
    blank = jnp.zeros((SENT - FLAT, LINES), f32)
    tail = FLAT - INNER

    def outer(rows):
        listed = list(range(8)) + list(range(ROWS - 8, ROWS)) + halo_rows
        return jnp.concatenate([rows[row] for row in listed] + [blank], axis=0)

    scales = jnp.concatenate(
        [jnp.zeros((tail, LINES), f32), s_ref[...], jnp.zeros((tail, LINES), f32)]
        + [scale[row] for row in halo_rows]
        + [jnp.zeros((LINES - tail - 6, LINES), f32)],
        axis=0,
    )
    lane = iota((SLOTS, LINES), 1)
    row8 = iota((SLOTS, LINES), 0)
    at_slot, at_edge, at_lines, reach = line_picks(slots_ref)
    halo_cells = jnp.concatenate([cells[row] for row in halo_rows] + [blank], axis=0)
    sent_tail = select(at_slot, halo_cells, NT)
    sent_scale = select(at_edge, scales, NT)
    outer_base = select(at_lines, outer(bases), NT)
    outer_reach = reach_of(reach, outer(bends), outer(masses))

    def joined(outer_part, middle_part):
        return jnp.concatenate(
            [outer_part[:, :LINES], middle_part, outer_part[:, LINES:]], axis=1
        )

    sent_base = joined(outer_base, sent_ref[...])
    sent_reach = joined(outer_reach, reach_ref[...])
    slot_base, edge_base = sent_base[:SLOTS], sent_base[SLOTS:]
    wide_row = iota((SLOTS, SENT), 0)
    wide_lane = iota((SLOTS, SENT), 1)
    third = jnp.where((wide_row < 6) | (wide_lane >= FLAT), sent_reach, edge_base)
    last = third[:, INNER:] + sent_scale[:, LINES:]
    last = jnp.where(lane == PARTNER_LANE, slots_ref[1].astype(f32), last)
    last = jnp.where(lane == LINE_LANE, slots_ref[0].astype(f32), last)

    def piece(block, at):
        return block[:, at * LINES : (at + 1) * LINES]

    def moved(block, at, shift):
        return pltpu.roll(piece(block, at), shift, 0)

    parts = []
    for at in range(4):
        parts += [piece(cells_ref, at), piece(slot_base, at), piece(third, at)]
    parts += [sent_tail + sent_scale[:, :LINES], last]
    parts += [
        jnp.where(
            row8 < 4,
            jnp.where(row8 < 2, piece(slot_base, 4), moved(edge_base, 4, 2)),
            jnp.where(row8 < 6, moved(edge_base, 0, 4), moved(edge_base, 1, 6)),
        ),
        jnp.where(row8 < 2, piece(edge_base, 2), moved(edge_base, 3, 2)),
    ]
    message = jnp.concatenate(parts, axis=0)
    for device in range(CHORD):
        message_ref[device] = message


def cut_of(row):
    place = row if 0 <= row < ROWS else ROWS + NEAR + row if row < 0 else NEAR + row
    return slice(place * COLS, (place + 1) * COLS)


def expand(data, pattern):
    rows = data.shape[0]
    product = one_pass(jnp.concatenate(parts_of(data, 2), axis=0), pattern, NN)
    return product[:rows] + product[rows:]


def spread_lines(data, pattern):
    return one_pass(
        jnp.concatenate(parts_of(data, 2), axis=0), jnp.concatenate([pattern] * 2, axis=0), TN
    )


def rim_spread():
    spot = iota((LINES, LINES), 0) - (FLAT - INNER)
    return ((spot == iota((LINES, LINES), 1) // COLS) & (spot < 2 * NEAR)).astype(f32)


def apply_kernel(
    got_ref, field_ref, inner_ref, base_ref, scale_ref, d_ref, w_ref, z_ref, gram_ref
):
    here = lax.axis_index("chord")
    devices = [here, lax.rem(here + CHORD - 1, CHORD), lax.rem(here + 1, CHORD)]
    mine, left, right = [got_ref[device] for device in devices]

    def group(block, first, tail):
        tiles = [block[first + 24 * k : first + 24 * k + 8] for k in range(4)]
        return jnp.concatenate(tiles + [block[tail : tail + 8]], axis=1)

    def everyone(at):
        return got_ref[:, at : at + 8, :].reshape(CHORD * SLOTS, LINES)

    all_cells = jnp.concatenate([everyone(at) for at in (0, 24, 48, 72, 96)], axis=1)
    all_base = jnp.concatenate([everyone(at) for at in (8, 32, 56, 80)], axis=1)
    all_reach = jnp.concatenate([everyone(at) for at in (16, 40, 64, 88)], axis=1)

    slots = jnp.concatenate([group(block, 0, 96) for block in (mine, left, right)], axis=0)
    numbers = jnp.concatenate([block[104:112] for block in (mine, left, right)], axis=0)
    partner = numbers[:, PARTNER_LANE : PARTNER_LANE + 1].astype(jnp.int32)
    line = numbers[:, LINE_LANE : LINE_LANE + 1].astype(jnp.int32)
    pick = (iota((3 * SLOTS, LINES), 1) == partner).astype(f32)
    other = select(pick, all_cells, NN)
    apart = penalty_weight * (slots - other)
    other_numbers = one_pass(pick[:SLOTS], everyone(104), NN)
    other_line = other_numbers[:, LINE_LANE : LINE_LANE + 1].astype(jnp.int32)
    other_device = partner[:SLOTS] // SLOTS
    other_base = select(pick[:SLOTS], all_base, NN)

    device = jnp.concatenate([jnp.full((SLOTS, 1), here, jnp.int32), other_device], axis=0)
    at = jnp.concatenate([line[:SLOTS], other_line], axis=0)
    before = lax.rem(device + CHORD - 1, CHORD) * SLOTS + NEAR + at
    after = lax.rem(device + 1, CHORD) * SLOTS + at - (LINES - NEAR)
    is_low, is_high = at < NEAR, at >= LINES - NEAR
    source = jnp.where(is_low, before, jnp.where(is_high, after, -1))
    added = select((iota((2 * SLOTS, LINES), 1) == source).astype(f32), all_reach, NN)
    edge = device * SLOTS + jnp.where(is_low, at + NEAR, at - (LINES - NEAR))
    edge = jnp.where(is_low | is_high, edge, -1)
    spare = select((iota((2 * SLOTS, LINES), 1) == edge).astype(f32), everyone(96), NN)

    low8 = iota((SLOTS, LINES), 0)
    row8 = iota((SLOTS, SENT), 0)
    halo_spare = jnp.where(low8 < 3, left[96:104], right[96:104])
    halo_rim = jnp.where(low8 < 3, left[104:112], right[104:112])
    inner = (
        iota((LINES, INNER), 0) == iota((LINES, INNER), 1) // COLS + (FLAT - INNER)
    ).astype(f32)
    scales = expand(jnp.concatenate([spare, halo_spare], axis=0), inner)
    slot_scale = scales[: 2 * SLOTS]
    halo_scale = jnp.concatenate(
        [scales[2 * SLOTS :], expand(halo_rim, rim_spread())], axis=1
    )
    reach = group(mine, 16, 104)
    arrived = jnp.where(row8 < 3, group(right, 16, 104), group(left, 16, 104))

    from_base = group(left, 8, 112)
    to_base = group(right, 8, 112)
    halo_base = jnp.where(
        row8 < 3,
        jnp.where(row8 < 2, pltpu.roll(group(left, 16, 104), 2, 0), pltpu.roll(from_base, 1, 0)),
        jnp.where(
            row8 < 4,
            pltpu.roll(to_base, 3, 0),
            jnp.concatenate(
                [
                    right[112:120],
                    pltpu.roll(right[112:120], 6, 0),
                    pltpu.roll(right[120:128], 4, 0),
                    pltpu.roll(right[120:128], 2, 0),
                    pltpu.roll(right[112:120], 2, 0),
                ],
                axis=1,
            ),
        ),
    )

    slot_base = group(mine, 8, 112)[:, :INNER]
    near = apart[:SLOTS, :INNER]
    own_w = slot_base + slot_scale[:SLOTS] * added[:SLOTS] + near
    other_w = other_base + slot_scale[SLOTS:] * added[SLOTS:] - near
    apart_w = penalty_weight * (own_w - other_w)
    apart_w = jnp.concatenate([apart_w, jnp.zeros((SLOTS, SENT - INNER), f32)], axis=1)

    target = iota((2 * SLOTS, SLOTS), 1)
    from_left = iota((2 * SLOTS, SLOTS), 0) < SLOTS
    chosen = (edge_line(target) == line[SLOTS:]) & ((target < 3) == from_left)
    halo_apart = select(chosen.astype(f32), apart[SLOTS:], TN)
    halo_w = halo_base + halo_scale * reach + halo_apart
    halo_v = jnp.where(row8 < 6, halo_scale * halo_w, 0.0)

    lane = iota((SLOTS, LINES), 1)
    at_slot = (lane == line[:SLOTS]).astype(f32)
    at_edge = (lane == edge_line(low8)).astype(f32)
    none = jnp.zeros((SLOTS, LINES), f32)
    first = spread_lines(
        jnp.concatenate([apart[:SLOTS], arrived], axis=0),
        jnp.concatenate(
            [
                jnp.concatenate([at_slot, none], axis=1),
                jnp.concatenate([none, at_edge], axis=1),
            ],
            axis=0,
        ),
    )
    distance = jnp.abs(outer_line(low8) - lane)
    second = mix(
        jnp.concatenate([halo_v, apart_w], axis=0),
        jnp.concatenate(
            [
                jnp.concatenate(
                    [taps_at(distance, mass_taps), taps_at(distance, bend_taps), none], axis=1
                ),
                jnp.concatenate([none, none, at_slot], axis=1),
            ],
            axis=0,
        ),
        TN,
        THREE,
    )
    scale = [scale_ref[NEAR + k : NEAR + k + 1, :] for k in range(WIDE)]
    images, masses, bends = [], [], []
    for row in range(WIDE):
        cut = cut_of(row - NEAR)
        scale_row = spread(scale[row])
        place = row - NEAR
        if place in OUTER:
            base = base_ref[pl.ds(OUTER.index(place) * COLS, COLS), :]
        else:
            base = inner_ref[pl.ds((place - NEAR) * COLS, COLS), :]
        image = base + first[cut, :LINES] + scale_row * first[cut, LINES:]
        value = scale_row * image
        mass, bend = mass_taps[0] * value, bend_taps[0] * value
        for step in range(1, 4):
            pair = pair_of(value, step)
            mass = mass + mass_taps[step] * pair
            if bend_taps[step] != 0.0:
                bend = bend + bend_taps[step] * pair
        images.append(image)
        masses.append(mass + second[cut, :LINES])
        bends.append(bend + second[cut, LINES : 2 * LINES])
    seconds = []
    for row in range(ROWS):
        at_row = row + NEAR
        cut = cut_of(row)
        total = row_stencil(masses, at_row, bend_taps) + row_stencil(bends, at_row, mass_taps)
        product = (
            spread(scale[at_row]) * total
            + spread(d_ref[row : row + 1, :]) * images[at_row]
            + second[cut, 2 * LINES :]
        )
        w_ref[pl.ds(row * COLS, COLS), :] = images[at_row]
        z_ref[pl.ds(row * COLS, COLS), :] = product
        seconds.append(product)
    r = jnp.concatenate([field_ref[pl.ds(k * COLS, COLS), :] for k in range(ROWS)], axis=1)
    w = jnp.concatenate(images[NEAR : NEAR + ROWS], axis=1)
    z = jnp.concatenate(seconds, axis=1)
    fields = [part for field in (r, w, z) for part in parts_of(field, 2)]
    blank = jnp.zeros((2 * COLS, ROWS * LINES), f32)
    products = one_pass(
        jnp.concatenate(fields[:4], axis=0), jnp.concatenate(fields + [blank], axis=0), NT
    )
    by_r = products[:COLS] + products[COLS : 2 * COLS]
    by_w = products[2 * COLS : 3 * COLS] + products[3 * COLS :]
    by_r = by_r + pltpu.roll(by_r, LINES - COLS, 1)
    by_w = by_w + pltpu.roll(by_w, LINES - COLS, 1)
    lane16 = iota((COLS, LINES), 1)
    gram = jnp.where(lane16 // COLS % 2 == 0, by_r, pltpu.roll(by_w, LINES - COLS, 1))
    gram = jnp.where(lane < 4 * COLS, gram[:SLOTS], pltpu.roll(gram[SLOTS:], 4 * COLS, 1))
    for device in range(gram_ref.shape[0]):
        gram_ref[device] = gram


def total_kernel(parts_ref, out_ref):
    total = jnp.sum(parts_ref[...], axis=0)
    for device in range(out_ref.shape[0]):
        out_ref[device] = total


def spd_solve(matrix, right):
    size, width = matrix.shape[0], right.shape[1]
    blank = jnp.zeros((size, LINES - size - width), f32)
    work = jnp.concatenate([matrix, right, blank], axis=1)
    row = iota((size, LINES), 0)
    for start in range(0, size, PANEL):
        columns = [
            jnp.broadcast_to(work[:, start + k : start + k + 1], (size, LINES))
            for k in range(PANEL)
        ]
        for k in range(PANEL):
            at = start + k
            column = columns[k]
            scale = 1.0 / column[at : at + 1, :]

            def eliminate(block):
                pivot_row = block[at : at + 1, :] * scale
                return jnp.where(row == at, pivot_row, block - column * pivot_row)

            work = eliminate(work)
            columns = [eliminate(block) if j > k else block for j, block in enumerate(columns)]
    return work[:, size : size + width]


def finish_kernel(parts_ref, field_ref, w_ref, z_ref, x_ref, res_ref):
    packed = jnp.sum(parts_ref[...], axis=0)
    gram = jnp.concatenate([packed[:, : 4 * COLS], packed[:, 4 * COLS :]], axis=0)
    g00, g11 = gram[:, :COLS], gram[:, COLS : 2 * COLS]
    g01, g12 = gram[:, 2 * COLS : 3 * COLS], gram[:, 3 * COLS :]
    coeffs = spd_solve(
        jnp.concatenate(
            [
                jnp.concatenate([g01, g11], axis=1),
                jnp.concatenate([g11, g12], axis=1),
            ],
            axis=0,
        ),
        jnp.concatenate([g00, g01], axis=0),
    )
    r = jnp.concatenate([field_ref[pl.ds(k * COLS, COLS), :] for k in range(ROWS)], axis=1)
    w = jnp.concatenate([w_ref[pl.ds(k * COLS, COLS), :] for k in range(ROWS)], axis=1)
    z = jnp.concatenate([z_ref[pl.ds(k * COLS, COLS), :] for k in range(ROWS)], axis=1)
    none = jnp.zeros((COLS, COLS), f32)
    weights = jnp.concatenate(
        [
            jnp.concatenate([coeffs, none], axis=0),
            jnp.concatenate([none, -coeffs], axis=0),
        ],
        axis=1,
    )
    products = one_pass(
        jnp.concatenate([jnp.concatenate(parts_of(weights, 3), axis=1)] * 3, axis=0),
        jnp.concatenate(parts_of(jnp.concatenate([r, w, z], axis=0), 3), axis=0),
        TN,
    )
    products = products[: 2 * COLS] + products[2 * COLS : 4 * COLS] + products[4 * COLS :]
    x, res = products[:COLS], r + products[COLS:]
    for row in range(ROWS):
        cut = slice(row * LINES, (row + 1) * LINES)
        x_ref[pl.ds(row, COLS, stride=ROWS), :] = x[:, cut]
        res_ref[pl.ds(row, COLS, stride=ROWS), :] = res[:, cut]


def call(kernel, shapes, hbm=False, scratch=(), cost=None):
    def run(*args):
        if hbm and not INTERPRET:
            args = [pltpu.with_memory_space_constraint(arg, pltpu.HBM) for arg in args]
        return pl.pallas_call(
            kernel,
            out_shape=[
                jax.ShapeDtypeStruct(shape, kind) for shape, kind in map(typed, shapes)
            ],
            in_specs=[pl.BlockSpec(memory_space=pltpu.HBM if hbm else pltpu.VMEM)] * len(args),
            out_specs=[pl.BlockSpec(memory_space=pltpu.VMEM)] * len(shapes),
            scratch_shapes=scratch,
            interpret=INTERPRET,
            cost_estimate=cost,
            compiler_params=pltpu.CompilerParams(vmem_limit_bytes=KERNEL_BYTES),
        )(*args)

    return run


def typed(shape):
    return shape if isinstance(shape[0], tuple) else (shape, f32)


def body(right_side, stiff_scale, extra_diag, iface_line, partner):
    span = lax.axis_size(SPAN)
    plane = lax.axis_size(("core", "chord"))
    depth = lax.axis_size("z")
    cells = right_side.reshape(COLS * ROWS, LINES)
    halo = (DEEP * COLS + 16, LINES)
    flat = (ROWS * COLS, LINES)
    one = (ROWS, LINES)
    field, far, near, scale, extra, slots = call(
        pack_kernel,
        [flat, halo, halo, one, one, ((2, SLOTS, LINES), jnp.int32)],
        hbm=True,
        scratch=[
            pltpu.VMEM(flat, f32),
            pltpu.SMEM((SLOTS,), jnp.int32),
            pltpu.SMEM((SLOTS,), jnp.int32),
            pltpu.SemaphoreType.DMA((5,)),
        ],
    )(iface_line, partner, cells, stiff_scale, extra_diag)
    swaps = [(i, i + 1) for i in range(1, span - 1, 2)]
    far = lax.ppermute(far, SPAN, swaps + [(b, a) for a, b in swaps])
    swaps = [(i, i + 1) for i in range(0, span, 2)]
    near = lax.ppermute(near, SPAN, swaps + [(b, a) for a, b in swaps])
    kept = (len(KEPT) * COLS, LINES)
    inner = call(
        inner_kernel,
        [
            ((ROWS - 2 * NEAR) * COLS, LINES),
            kept,
            kept,
            (SLOTS, INNER),
            (2 * SLOTS, 2 * LINES),
            (SLOTS, 2 * LINES),
        ],
        cost=pl.CostEstimate(flops=40_000_000, bytes_accessed=2_000_000, transcendentals=0),
    )
    inner = inner(field, scale, extra, slots)
    base, scale, message = call(
        send_kernel,
        [(len(OUTER) * COLS, LINES), (ROWS + 2 * DEEP, LINES), (CHORD, SPARE, LINES)],
    )(field, scale, extra, far, near, slots, *inner)
    got = lax.all_to_all(message, "chord", 0, 0)
    w, z, gram = call(apply_kernel, [flat, flat, (plane, 8, LINES)])(
        got, field, inner[0], base, scale, extra
    )
    gram = lax.all_to_all(gram, ("core", "chord"), 0, 0)
    (gram,) = call(total_kernel, [(depth, 8, LINES)])(gram)
    gram = lax.all_to_all(gram, "z", 0, 0)
    x, res = call(finish_kernel, [flat, flat])(gram, field, w, z)
    return (x.reshape(COLS, ROWS, LINES), res.reshape(COLS, ROWS, LINES))


def solution(mesh):
    chord = mesh.devices.shape[1]
    fine = Mesh(mesh.devices.reshape(-1, 2, chord), ("z", "core", "chord"))
    return jax.shard_map(
        body,
        mesh=fine,
        in_specs=(
            P(None, SPAN, "chord"),
            P(SPAN, "chord"),
            P(SPAN, "chord"),
            P("chord"),
            P("chord"),
        ),
        out_specs=(P(None, SPAN, "chord"), P(None, SPAN, "chord")),
        check_vma=False,
    )
```

```python
import jax
import jax.numpy as jnp
from jax import lax
from jax.experimental import pallas as pl
from jax.experimental.pallas import tpu as pltpu
from jax.sharding import Mesh
from jax.sharding import PartitionSpec as P

SPAN = ("z", "core")
COLS = 16
ROWS = 32
LINES = 128
SLOTS = 8
CHORD = 16
DEEP = 6
NEAR = 3
WIDE = ROWS + 2 * NEAR
FLAT = WIDE * COLS
INNER = ROWS * COLS
SENT = 640
KEPT = [3, 4, 5, 6, 7, 24, 25, 26, 27, 28]
OUTER = [-3, -2, -1, 0, 1, 2, 29, 30, 31, 32, 33, 34]
PARTNER_LANE = 104
LINE_LANE = 105
PANEL = 16
SPARE = 128

mass_taps = (2416.0 / 5040.0, 1191.0 / 5040.0, 120.0 / 5040.0, 1.0 / 5040.0)
bend_taps = (8.0 / 3.0, -1.5, 0.0, 1.0 / 6.0)
penalty_weight = 4.0

f32 = jnp.float32
KERNEL_BYTES = 24 << 20
INTERPRET = False


def one_pass(left, right, contract):
    return lax.dot_general(
        left.astype(jnp.bfloat16),
        right.astype(jnp.bfloat16),
        (contract, ((), ())),
        preferred_element_type=f32,
    )


NN, NT, TN = ((1,), (0,)), ((1,), (1,)), ((0,), (0,))


def parts_of(value, count):
    parts = []
    for _ in range(count):
        parts.append(value.astype(jnp.bfloat16).astype(f32))
        value = value - parts[-1]
    return parts


def select(pick, data, contract):
    (left,), (right,) = contract
    return one_pass(
        jnp.concatenate([pick] * 2, axis=left),
        jnp.concatenate(parts_of(data, 2), axis=right),
        contract,
    )


def mix(left, right, contract, pairs):
    count = 1 + max(max(pair) for pair in pairs)
    lefts, rights = parts_of(left, count), parts_of(right, count)
    return one_pass(
        jnp.concatenate([lefts[a] for a, _ in pairs], axis=contract[0][0]),
        jnp.concatenate([rights[b] for _, b in pairs], axis=contract[1][0]),
        contract,
    )


THREE = ((0, 0), (0, 1), (1, 0))


def iota(shape, dim):
    return lax.broadcasted_iota(jnp.int32, shape, dim)


def taps_at(distance, taps):
    value = jnp.zeros(distance.shape, f32)
    for step in range(4):
        if taps[step] != 0.0:
            value = jnp.where(distance == step, taps[step], value)
    return value


def outer_line(row):
    return jnp.where(row < 3, row - 3, jnp.where(row < 6, row + LINES - 3, 4 * LINES))


def edge_line(row):
    return jnp.where(row < 3, row + LINES - 3, jnp.where(row < 6, row - 3, 4 * LINES))


def pair_of(field, step):
    lane = iota((COLS, LINES), 1)
    ahead = jnp.where(lane < LINES - step, pltpu.roll(field, LINES - step, 1), 0.0)
    behind = jnp.where(lane >= step, pltpu.roll(field, step, 1), 0.0)
    return ahead + behind


def row_stencil(rows, at, taps):
    total = taps[0] * rows[at]
    for step in range(1, 4):
        if taps[step] != 0.0:
            total = total + taps[step] * (rows[at - step] + rows[at + step])
    return total


def spread(row):
    return jnp.broadcast_to(row, (COLS, LINES))


def pack_kernel(
    line_hbm, partner_hbm, r_hbm, s_hbm, d_hbm,
    r_ref, far_ref, near_ref, s_ref, d_ref, slots_ref,
    line_ref, partner_ref, sems
):
    copies = [
        pltpu.make_async_copy(source, target, sems.at[k])
        for k, (source, target) in enumerate(
            [
                (r_hbm, r_ref),
                (s_hbm, s_ref),
                (d_hbm, d_ref),
                (line_hbm, line_ref),
                (partner_hbm, partner_ref),
            ]
        )
    ]
    for copy in copies:
        copy.start()
    for copy in copies:
        copy.wait()
    first_core = lax.axis_index("core") == 0
    pad = jnp.zeros((2, LINES), f32)
    low, high = slice(0, DEEP), slice(ROWS - DEEP, ROWS)
    ends = [
        jnp.concatenate(
            [r_ref[pl.ds(row, COLS, stride=ROWS), :] for row in range(cut.start, cut.stop)]
            + [s_ref[cut, :], pad, d_ref[cut, :], pad],
            axis=0,
        )
        for cut in (low, high)
    ]
    far_ref[...] = jnp.where(first_core, ends[0], ends[1])
    near_ref[...] = jnp.where(first_core, ends[1], ends[0])
    row = iota((SLOTS, LINES), 0)
    for k, scalars in enumerate((line_ref, partner_ref)):
        value = jnp.zeros((SLOTS, LINES), jnp.int32)
        for slot in range(SLOTS):
            value = jnp.where(row == slot, scalars[slot], value)
        slots_ref[k] = value


def first_product(weighted, at, scale, extra, cells):
    mass = row_stencil(weighted, at, mass_taps)
    bend = row_stencil(weighted, at, bend_taps)
    total = mass_taps[0] * bend + bend_taps[0] * mass
    for step in range(1, 4):
        mixed = mass_taps[step] * bend
        if bend_taps[step] != 0.0:
            mixed = mixed + bend_taps[step] * mass
        total = total + pair_of(mixed, step)
    return mass, bend, spread(scale) * total + spread(extra) * cells


def line_picks(slots_ref):
    lane = iota((SLOTS, LINES), 1)
    row8 = iota((SLOTS, LINES), 0)
    at_slot = (lane == slots_ref[0]).astype(f32)
    at_edge = (lane == edge_line(row8)).astype(f32)
    other_edge = (
        ((lane == row8 + 1) & (row8 < 2)) | ((lane == row8 + LINES - 9) & (row8 >= 6))
    ).astype(f32)
    distance = jnp.abs(outer_line(row8) - lane)
    reach = jnp.concatenate([taps_at(distance, mass_taps), taps_at(distance, bend_taps)], axis=1)
    return at_slot, at_edge, jnp.concatenate([at_slot, other_edge], axis=0), reach


def reach_of(reach, bends, masses):
    return mix(reach, jnp.concatenate([bends, masses], axis=1), NT, THREE)


def inner_kernel(
    r_ref, s_ref, d_ref, slots_ref,
    base_ref, mass_ref, bend_ref, cells_ref, sent_ref, reach_ref, field_ref, layers_ref
):
    cells = [r_ref[pl.ds(k, COLS, stride=ROWS), :] for k in range(ROWS)]
    for row in range(ROWS):
        field_ref[pl.ds(row * COLS, COLS), :] = cells[row]
        layers_ref[:, row * LINES : (row + 1) * LINES] = jnp.concatenate(
            parts_of(cells[row], 3), axis=0
        ).astype(jnp.bfloat16)
    weighted = [spread(s_ref[k : k + 1, :]) * cells[k] for k in range(ROWS)]
    masses, bends, bases = {}, {}, {}
    for row in range(NEAR, ROWS - NEAR):
        masses[row], bends[row], bases[row] = first_product(
            weighted, row, s_ref[row : row + 1, :], d_ref[row : row + 1, :], cells[row]
        )
        base_ref[pl.ds((row - NEAR) * COLS, COLS), :] = bases[row]
    for place, row in enumerate(KEPT):
        mass_ref[pl.ds(place * COLS, COLS), :] = masses[row]
        bend_ref[pl.ds(place * COLS, COLS), :] = bends[row]

    def middle(rows):
        return jnp.concatenate([rows[row] for row in range(8, ROWS - 8)], axis=0)

    at_slot, _, at_lines, reach = line_picks(slots_ref)
    cells_ref[...] = select(at_slot, jnp.concatenate(cells, axis=0), NT)
    sent_ref[...] = select(at_lines, middle(bases), NT)
    reach_ref[...] = reach_of(reach, middle(bends), middle(masses))


def send_kernel(
    field_ref, s_ref, d_ref, far_ref, near_ref, slots_ref,
    inner_ref, mass_ref, bend_ref, cells_ref, sent_ref, reach_ref,
    base_ref, scale_ref, message_ref
):
    first_core = lax.axis_index("core") == 0
    below = jnp.where(first_core, far_ref[...], near_ref[...])
    above = jnp.where(first_core, near_ref[...], far_ref[...])
    start = DEEP * COLS
    scale_ref[0:DEEP, :] = below[start : start + DEEP]
    scale_ref[DEEP : DEEP + ROWS, :] = s_ref[...]
    scale_ref[DEEP + ROWS : 2 * DEEP + ROWS, :] = above[start : start + DEEP]
    cells, scale, extra, weighted = {}, {}, {}, {}
    ends = list(range(-DEEP, DEEP)) + list(range(ROWS - DEEP, ROWS + DEEP))
    for row in ends:
        if row < 0:
            source, at = below, row + DEEP
        elif row >= ROWS:
            source, at = above, row - ROWS
        else:
            source, at = None, row
        if source is None:
            cells[row] = field_ref[pl.ds(at * COLS, COLS), :]
            scale[row], extra[row] = s_ref[at : at + 1, :], d_ref[at : at + 1, :]
        else:
            cells[row] = source[at * COLS : (at + 1) * COLS]
            scale[row] = source[start + at : start + at + 1]
            extra[row] = source[start + 8 + at : start + 9 + at]
        weighted[row] = spread(scale[row]) * cells[row]
    masses, bends, bases = {}, {}, {}
    for place, row in enumerate(OUTER):
        masses[row], bends[row], bases[row] = first_product(
            weighted, row, scale[row], extra[row], cells[row]
        )
        base_ref[pl.ds(place * COLS, COLS), :] = bases[row]
    for place, row in enumerate(KEPT):
        masses[row] = mass_ref[pl.ds(place * COLS, COLS), :]
        bends[row] = bend_ref[pl.ds(place * COLS, COLS), :]
        bases[row] = inner_ref[pl.ds((row - NEAR) * COLS, COLS), :]
    halo_rows = list(range(-NEAR, 0)) + list(range(ROWS, ROWS + NEAR))
    blank = jnp.zeros((SENT - FLAT, LINES), f32)
    tail = FLAT - INNER

    def outer(rows):
        listed = list(range(8)) + list(range(ROWS - 8, ROWS)) + halo_rows
        return jnp.concatenate([rows[row] for row in listed] + [blank], axis=0)

    scales = jnp.concatenate(
        [jnp.zeros((tail, LINES), f32), s_ref[...], jnp.zeros((tail, LINES), f32)]
        + [scale[row] for row in halo_rows]
        + [jnp.zeros((LINES - tail - 6, LINES), f32)],
        axis=0,
    )
    lane = iota((SLOTS, LINES), 1)
    row8 = iota((SLOTS, LINES), 0)
    at_slot, at_edge, at_lines, reach = line_picks(slots_ref)
    halo_cells = jnp.concatenate([cells[row] for row in halo_rows] + [blank], axis=0)
    sent_tail = select(at_slot, halo_cells, NT)
    sent_scale = select(at_edge, scales, NT)
    outer_base = select(at_lines, outer(bases), NT)
    outer_reach = reach_of(reach, outer(bends), outer(masses))

    def joined(outer_part, middle_part):
        return jnp.concatenate(
            [outer_part[:, :LINES], middle_part, outer_part[:, LINES:]], axis=1
        )

    sent_base = joined(outer_base, sent_ref[...])
    sent_reach = joined(outer_reach, reach_ref[...])
    slot_base, edge_base = sent_base[:SLOTS], sent_base[SLOTS:]
    wide_row = iota((SLOTS, SENT), 0)
    wide_lane = iota((SLOTS, SENT), 1)
    third = jnp.where((wide_row < 6) | (wide_lane >= FLAT), sent_reach, edge_base)
    last = third[:, INNER:] + sent_scale[:, LINES:]
    last = jnp.where(lane == PARTNER_LANE, slots_ref[1].astype(f32), last)
    last = jnp.where(lane == LINE_LANE, slots_ref[0].astype(f32), last)

    def piece(block, at):
        return block[:, at * LINES : (at + 1) * LINES]

    def moved(block, at, shift):
        return pltpu.roll(piece(block, at), shift, 0)

    parts = []
    for at in range(4):
        parts += [piece(cells_ref, at), piece(slot_base, at), piece(third, at)]
    parts += [sent_tail + sent_scale[:, :LINES], last]
    parts += [
        jnp.where(
            row8 < 4,
            jnp.where(row8 < 2, piece(slot_base, 4), moved(edge_base, 4, 2)),
            jnp.where(row8 < 6, moved(edge_base, 0, 4), moved(edge_base, 1, 6)),
        ),
        jnp.where(row8 < 2, piece(edge_base, 2), moved(edge_base, 3, 2)),
    ]
    message = jnp.concatenate(parts, axis=0)
    for device in range(CHORD):
        message_ref[device] = message


def cut_of(row):
    place = row if 0 <= row < ROWS else ROWS + NEAR + row if row < 0 else NEAR + row
    return slice(place * COLS, (place + 1) * COLS)


def expand(data, pattern):
    rows = data.shape[0]
    product = one_pass(jnp.concatenate(parts_of(data, 2), axis=0), pattern, NN)
    return product[:rows] + product[rows:]


def spread_lines(data, pattern):
    return one_pass(
        jnp.concatenate(parts_of(data, 2), axis=0), jnp.concatenate([pattern] * 2, axis=0), TN
    )


def rim_spread():
    spot = iota((LINES, LINES), 0) - (FLAT - INNER)
    return ((spot == iota((LINES, LINES), 1) // COLS) & (spot < 2 * NEAR)).astype(f32)


def apply_kernel(
    got_ref, layers_ref, inner_ref, base_ref, scale_ref, d_ref, w_ref, z_ref, gram_ref
):
    here = lax.axis_index("chord")
    devices = [here, lax.rem(here + CHORD - 1, CHORD), lax.rem(here + 1, CHORD)]
    mine, left, right = [got_ref[device] for device in devices]

    def group(block, first, tail):
        tiles = [block[first + 24 * k : first + 24 * k + 8] for k in range(4)]
        return jnp.concatenate(tiles + [block[tail : tail + 8]], axis=1)

    def everyone(at):
        return got_ref[:, at : at + 8, :].reshape(CHORD * SLOTS, LINES)

    all_cells = jnp.concatenate([everyone(at) for at in (0, 24, 48, 72, 96)], axis=1)
    all_base = jnp.concatenate([everyone(at) for at in (8, 32, 56, 80)], axis=1)
    all_reach = jnp.concatenate([everyone(at) for at in (16, 40, 64, 88)], axis=1)

    slots = jnp.concatenate([group(block, 0, 96) for block in (mine, left, right)], axis=0)
    numbers = jnp.concatenate([block[104:112] for block in (mine, left, right)], axis=0)
    partner = numbers[:, PARTNER_LANE : PARTNER_LANE + 1].astype(jnp.int32)
    line = numbers[:, LINE_LANE : LINE_LANE + 1].astype(jnp.int32)
    pick = (iota((3 * SLOTS, LINES), 1) == partner).astype(f32)
    other = select(pick, all_cells, NN)
    apart = penalty_weight * (slots - other)
    other_numbers = one_pass(pick[:SLOTS], everyone(104), NN)
    other_line = other_numbers[:, LINE_LANE : LINE_LANE + 1].astype(jnp.int32)
    other_device = partner[:SLOTS] // SLOTS
    other_base = select(pick[:SLOTS], all_base, NN)

    device = jnp.concatenate([jnp.full((SLOTS, 1), here, jnp.int32), other_device], axis=0)
    at = jnp.concatenate([line[:SLOTS], other_line], axis=0)
    before = lax.rem(device + CHORD - 1, CHORD) * SLOTS + NEAR + at
    after = lax.rem(device + 1, CHORD) * SLOTS + at - (LINES - NEAR)
    is_low, is_high = at < NEAR, at >= LINES - NEAR
    source = jnp.where(is_low, before, jnp.where(is_high, after, -1))
    added = select((iota((2 * SLOTS, LINES), 1) == source).astype(f32), all_reach, NN)
    edge = device * SLOTS + jnp.where(is_low, at + NEAR, at - (LINES - NEAR))
    edge = jnp.where(is_low | is_high, edge, -1)
    spare = select((iota((2 * SLOTS, LINES), 1) == edge).astype(f32), everyone(96), NN)

    low8 = iota((SLOTS, LINES), 0)
    row8 = iota((SLOTS, SENT), 0)
    halo_spare = jnp.where(low8 < 3, left[96:104], right[96:104])
    halo_rim = jnp.where(low8 < 3, left[104:112], right[104:112])
    inner = (
        iota((LINES, INNER), 0) == iota((LINES, INNER), 1) // COLS + (FLAT - INNER)
    ).astype(f32)
    scales = expand(jnp.concatenate([spare, halo_spare], axis=0), inner)
    slot_scale = scales[: 2 * SLOTS]
    halo_scale = jnp.concatenate(
        [scales[2 * SLOTS :], expand(halo_rim, rim_spread())], axis=1
    )
    reach = group(mine, 16, 104)
    arrived = jnp.where(row8 < 3, group(right, 16, 104), group(left, 16, 104))

    from_base = group(left, 8, 112)
    to_base = group(right, 8, 112)
    halo_base = jnp.where(
        row8 < 3,
        jnp.where(row8 < 2, pltpu.roll(group(left, 16, 104), 2, 0), pltpu.roll(from_base, 1, 0)),
        jnp.where(
            row8 < 4,
            pltpu.roll(to_base, 3, 0),
            jnp.concatenate(
                [
                    right[112:120],
                    pltpu.roll(right[112:120], 6, 0),
                    pltpu.roll(right[120:128], 4, 0),
                    pltpu.roll(right[120:128], 2, 0),
                    pltpu.roll(right[112:120], 2, 0),
                ],
                axis=1,
            ),
        ),
    )

    slot_base = group(mine, 8, 112)[:, :INNER]
    near = apart[:SLOTS, :INNER]
    own_w = slot_base + slot_scale[:SLOTS] * added[:SLOTS] + near
    other_w = other_base + slot_scale[SLOTS:] * added[SLOTS:] - near
    apart_w = penalty_weight * (own_w - other_w)
    apart_w = jnp.concatenate([apart_w, jnp.zeros((SLOTS, SENT - INNER), f32)], axis=1)

    target = iota((2 * SLOTS, SLOTS), 1)
    from_left = iota((2 * SLOTS, SLOTS), 0) < SLOTS
    chosen = (edge_line(target) == line[SLOTS:]) & ((target < 3) == from_left)
    halo_apart = select(chosen.astype(f32), apart[SLOTS:], TN)
    halo_w = halo_base + halo_scale * reach + halo_apart
    halo_v = jnp.where(row8 < 6, halo_scale * halo_w, 0.0)

    lane = iota((SLOTS, LINES), 1)
    at_slot = (lane == line[:SLOTS]).astype(f32)
    at_edge = (lane == edge_line(low8)).astype(f32)
    none = jnp.zeros((SLOTS, LINES), f32)
    first = spread_lines(
        jnp.concatenate([apart[:SLOTS], arrived], axis=0),
        jnp.concatenate(
            [
                jnp.concatenate([at_slot, none], axis=1),
                jnp.concatenate([none, at_edge], axis=1),
            ],
            axis=0,
        ),
    )
    distance = jnp.abs(outer_line(low8) - lane)
    second = mix(
        jnp.concatenate([halo_v, apart_w], axis=0),
        jnp.concatenate(
            [
                jnp.concatenate(
                    [taps_at(distance, mass_taps), taps_at(distance, bend_taps), none], axis=1
                ),
                jnp.concatenate([none, none, at_slot], axis=1),
            ],
            axis=0,
        ),
        TN,
        THREE,
    )
    scale = [scale_ref[NEAR + k : NEAR + k + 1, :] for k in range(WIDE)]
    images, masses, bends = [], [], []
    for row in range(WIDE):
        cut = cut_of(row - NEAR)
        scale_row = spread(scale[row])
        place = row - NEAR
        if place in OUTER:
            base = base_ref[pl.ds(OUTER.index(place) * COLS, COLS), :]
        else:
            base = inner_ref[pl.ds((place - NEAR) * COLS, COLS), :]
        image = base + first[cut, :LINES] + scale_row * first[cut, LINES:]
        value = scale_row * image
        mass, bend = mass_taps[0] * value, bend_taps[0] * value
        for step in range(1, 4):
            pair = pair_of(value, step)
            mass = mass + mass_taps[step] * pair
            if bend_taps[step] != 0.0:
                bend = bend + bend_taps[step] * pair
        images.append(image)
        masses.append(mass + second[cut, :LINES])
        bends.append(bend + second[cut, LINES : 2 * LINES])
    seconds = []
    for row in range(ROWS):
        at_row = row + NEAR
        cut = cut_of(row)
        total = row_stencil(masses, at_row, bend_taps) + row_stencil(bends, at_row, mass_taps)
        product = (
            spread(scale[at_row]) * total
            + spread(d_ref[row : row + 1, :]) * images[at_row]
            + second[cut, 2 * LINES :]
        )
        w_ref[pl.ds(row * COLS, COLS), :] = images[at_row]
        z_ref[pl.ds(row * COLS, COLS), :] = product
        seconds.append(product)
    w = jnp.concatenate(images[NEAR : NEAR + ROWS], axis=1)
    z = jnp.concatenate(seconds, axis=1)
    w_parts, z_parts = [
        jnp.concatenate(parts_of(field, 2), axis=0).astype(jnp.bfloat16) for field in (w, z)
    ]
    left = jnp.concatenate([layers_ref[: 2 * COLS, :], w_parts], axis=0)
    blank = jnp.zeros((2 * COLS, ROWS * LINES), jnp.bfloat16)
    products = one_pass(left, jnp.concatenate([left, z_parts, blank], axis=0), NT)
    by_r = products[:COLS] + products[COLS : 2 * COLS]
    by_w = products[2 * COLS : 3 * COLS] + products[3 * COLS :]
    by_r = by_r + pltpu.roll(by_r, LINES - COLS, 1)
    by_w = by_w + pltpu.roll(by_w, LINES - COLS, 1)
    lane16 = iota((COLS, LINES), 1)
    gram = jnp.where(lane16 // COLS % 2 == 0, by_r, pltpu.roll(by_w, LINES - COLS, 1))
    gram = jnp.where(lane < 4 * COLS, gram[:SLOTS], pltpu.roll(gram[SLOTS:], 4 * COLS, 1))
    for device in range(gram_ref.shape[0]):
        gram_ref[device] = gram


def total_kernel(parts_ref, out_ref):
    total = jnp.sum(parts_ref[...], axis=0)
    for device in range(out_ref.shape[0]):
        out_ref[device] = total


def spd_solve(matrix, right):
    size, width = matrix.shape[0], right.shape[1]
    blank = jnp.zeros((size, LINES - size - width), f32)
    work = jnp.concatenate([matrix, right, blank], axis=1)
    row = iota((size, LINES), 0)
    for start in range(0, size, PANEL):
        columns = [
            jnp.broadcast_to(work[:, start + k : start + k + 1], (size, LINES))
            for k in range(PANEL)
        ]
        for k in range(PANEL):
            at = start + k
            column = columns[k]
            scale = 1.0 / column[at : at + 1, :]

            def eliminate(block):
                pivot_row = block[at : at + 1, :] * scale
                return jnp.where(row == at, pivot_row, block - column * pivot_row)

            work = eliminate(work)
            columns = [eliminate(block) if j > k else block for j, block in enumerate(columns)]
    return work[:, size : size + width]


def finish_kernel(parts_ref, field_ref, layers_ref, w_ref, z_ref, x_ref, res_ref):
    packed = jnp.sum(parts_ref[...], axis=0)
    gram = jnp.concatenate([packed[:, : 4 * COLS], packed[:, 4 * COLS :]], axis=0)
    g00, g11 = gram[:, :COLS], gram[:, COLS : 2 * COLS]
    g01, g12 = gram[:, 2 * COLS : 3 * COLS], gram[:, 3 * COLS :]
    coeffs = spd_solve(
        jnp.concatenate(
            [
                jnp.concatenate([g01, g11], axis=1),
                jnp.concatenate([g11, g12], axis=1),
            ],
            axis=0,
        ),
        jnp.concatenate([g00, g01], axis=0),
    )
    r = jnp.concatenate([field_ref[pl.ds(k * COLS, COLS), :] for k in range(ROWS)], axis=1)
    w = jnp.concatenate([w_ref[pl.ds(k * COLS, COLS), :] for k in range(ROWS)], axis=1)
    z = jnp.concatenate([z_ref[pl.ds(k * COLS, COLS), :] for k in range(ROWS)], axis=1)
    none = jnp.zeros((COLS, COLS), f32)
    weights = jnp.concatenate(
        [
            jnp.concatenate([coeffs, none], axis=0),
            jnp.concatenate([none, -coeffs], axis=0),
        ],
        axis=1,
    )
    weights = jnp.concatenate(parts_of(weights, 3), axis=1)
    rest = jnp.concatenate(parts_of(jnp.concatenate([w, z], axis=0), 3), axis=0)
    products = one_pass(
        jnp.concatenate([weights[:COLS]] * 3 + [weights[COLS:]] * 3, axis=0),
        jnp.concatenate([layers_ref[...], rest.astype(jnp.bfloat16)], axis=0),
        TN,
    )
    products = products[: 2 * COLS] + products[2 * COLS : 4 * COLS] + products[4 * COLS :]
    x, res = products[:COLS], r + products[COLS:]
    for row in range(ROWS):
        cut = slice(row * LINES, (row + 1) * LINES)
        x_ref[pl.ds(row, COLS, stride=ROWS), :] = x[:, cut]
        res_ref[pl.ds(row, COLS, stride=ROWS), :] = res[:, cut]


def call(kernel, shapes, hbm=False, scratch=(), cost=None):
    def run(*args):
        if hbm and not INTERPRET:
            args = [pltpu.with_memory_space_constraint(arg, pltpu.HBM) for arg in args]
        return pl.pallas_call(
            kernel,
            out_shape=[
                jax.ShapeDtypeStruct(shape, kind) for shape, kind in map(typed, shapes)
            ],
            in_specs=[pl.BlockSpec(memory_space=pltpu.HBM if hbm else pltpu.VMEM)] * len(args),
            out_specs=[pl.BlockSpec(memory_space=pltpu.VMEM)] * len(shapes),
            scratch_shapes=scratch,
            interpret=INTERPRET,
            cost_estimate=cost,
            compiler_params=pltpu.CompilerParams(vmem_limit_bytes=KERNEL_BYTES),
        )(*args)

    return run


def typed(shape):
    return shape if isinstance(shape[0], tuple) else (shape, f32)


def body(right_side, stiff_scale, extra_diag, iface_line, partner):
    span = lax.axis_size(SPAN)
    plane = lax.axis_size(("core", "chord"))
    depth = lax.axis_size("z")
    cells = right_side.reshape(COLS * ROWS, LINES)
    halo = (DEEP * COLS + 16, LINES)
    flat = (ROWS * COLS, LINES)
    one = (ROWS, LINES)
    loaded, far, near, scale, extra, slots = call(
        pack_kernel,
        [flat, halo, halo, one, one, ((2, SLOTS, LINES), jnp.int32)],
        hbm=True,
        scratch=[
            pltpu.SMEM((SLOTS,), jnp.int32),
            pltpu.SMEM((SLOTS,), jnp.int32),
            pltpu.SemaphoreType.DMA((5,)),
        ],
    )(iface_line, partner, cells, stiff_scale, extra_diag)
    swaps = [(i, i + 1) for i in range(1, span - 1, 2)]
    far = lax.ppermute(far, SPAN, swaps + [(b, a) for a, b in swaps])
    swaps = [(i, i + 1) for i in range(0, span, 2)]
    near = lax.ppermute(near, SPAN, swaps + [(b, a) for a, b in swaps])
    kept = (len(KEPT) * COLS, LINES)
    inner = call(
        inner_kernel,
        [
            ((ROWS - 2 * NEAR) * COLS, LINES),
            kept,
            kept,
            (SLOTS, INNER),
            (2 * SLOTS, 2 * LINES),
            (SLOTS, 2 * LINES),
            flat,
            ((3 * COLS, ROWS * LINES), jnp.bfloat16),
        ],
        cost=pl.CostEstimate(flops=40_000_000, bytes_accessed=2_000_000, transcendentals=0),
    )
    *inner, field, layers = inner(loaded, scale, extra, slots)
    base, scale, message = call(
        send_kernel,
        [(len(OUTER) * COLS, LINES), (ROWS + 2 * DEEP, LINES), (CHORD, SPARE, LINES)],
    )(field, scale, extra, far, near, slots, *inner)
    got = lax.all_to_all(message, "chord", 0, 0)
    w, z, gram = call(apply_kernel, [flat, flat, (plane, 8, LINES)])(
        got, layers, inner[0], base, scale, extra
    )
    gram = lax.all_to_all(gram, ("core", "chord"), 0, 0)
    (gram,) = call(total_kernel, [(depth, 8, LINES)])(gram)
    gram = lax.all_to_all(gram, "z", 0, 0)
    x, res = call(finish_kernel, [flat, flat])(gram, field, layers, w, z)
    return (x.reshape(COLS, ROWS, LINES), res.reshape(COLS, ROWS, LINES))


def solution(mesh):
    chord = mesh.devices.shape[1]
    fine = Mesh(mesh.devices.reshape(-1, 2, chord), ("z", "core", "chord"))
    return jax.shard_map(
        body,
        mesh=fine,
        in_specs=(
            P(None, SPAN, "chord"),
            P(SPAN, "chord"),
            P(SPAN, "chord"),
            P("chord"),
            P("chord"),
        ),
        out_specs=(P(None, SPAN, "chord"), P(None, SPAN, "chord")),
        check_vma=False,
    )
```
